32 devices in a mesh: view: 4 (over z), gz: 2 (over x), gy: 4 (over y, core).
Axes of the slice: x: 2, y: 2, z: 4, core: 2. Of those that a mesh axis runs over, the one named last changes fastest.
Arguments:
- pieces: bfloat16 [4, 128, 8, 2048], P('view', ('gz', 'gy')), may hold values from 0.19921875 to 2
- piece_owner: int32 [4, 128, 1], P('view', ('gz', 'gy')), may hold values from 0 to 7; in each aligned block of 16 rows (0 to 15, 16 to 31, ..., all dimensions but the last counted through in order) at most 4 rows name the same one
- piece_row: int32 [4, 128], P('view', ('gz', 'gy')), may hold values from 0 to 3
- estimate: float32 [8, 32, 2048], P('gz', 'gy', 'view'), may hold values from 0.5 to 1.5
- psf_x: float32 [4, 257], P('view'), may hold values from 0.00097276265 to 0.0068093385
- stencil: float32 [4, 3, 3], P('view'), may hold values from 0.03 to 0.2
- background: float32 [4], P('view'), may hold values from 0.05 to 0.5
- bleach_table: float32 [4, 16], replicated, may hold values from 0.2 to 2
- bleach_index: int32 [4, 8], P(None, 'gz'), may hold values from 0 to 15
Outputs:
- joined: float32 [8, 32, 2048], P('gz', 'gy', 'view')
The draws below stay inside these ranges and needn't reach their ends.
Inputs may be any that keep to these rules, and one draw needn't show every extreme that they name: `piece_owner`: among the 16 blocks of a view that one device holds (aligned blocks of rows), no owner is named more than 4 times, a bound that some block reaches.
All inputs are finite; a program needn't handle non-finite values.
Results may differ from the reference program's by a relative error of at most 0.00098.
Values may be sent and summed in bfloat16 or wider, within the bound.
No kernel may reach another device: no remote copies, remote signals or barrier semaphores. Data moves between devices by JAX's collectives and lax.ppermute only.
A program may use at most 64 MiB of HBM per device.

```python
import math
import jax
import jax.numpy as jnp
import numpy as np
from jax import lax

X = 2048
KX = 257
HX = 128
LEVELS = 16
ITERS = 2
CZ = 4
CY = 8
VIEWS = 4
PIECES_DEV = 16
CAP = 4
NZ = 8
NY = 32
PIECES = 128
N_GZ = 2
N_GY = 4


def with_ends(drawn, own_key, smallest, high):
    longest = drawn.shape.index(max(drawn.shape))
    spots = []
    for shift in (0, 1):
        where = [jax.random.randint(jax.random.fold_in(own_key, axis), (), 0, length) for axis, length in enumerate(drawn.shape)]
        where[longest] = (where[longest] + shift) % drawn.shape[longest]
        spots.append(tuple(where))
    return drawn.at[spots[0]].set(smallest).at[spots[1]].set(high)


def block_levels(stream_key, extent, shards, smallest, largest):
    def one(axis_at, blocks):
        draws = jax.random.uniform(jax.random.fold_in(jax.random.fold_in(stream_key, 6), axis_at), (blocks,), jnp.float32, smallest / len(shards), largest / len(shards))
        return jnp.repeat(jnp.exp(draws), extent[axis_at] // blocks).reshape((-1,) + (1,) * (len(extent) - axis_at - 1))

    loudness = one(*shards[0])
    for cut in shards[1:]:
        loudness = loudness * one(*cut)
    return loudness


def assign_block(rng, own, number, rows, count, top, most, slope):
    ranking = jax.random.permutation(rng, count)
    packed, ordinary = portions_of(count, rows * top, most, slope, True), portions_of(count, rows * top, most, slope, False)
    places = jnp.arange(count)

    def named(tallies, rotation):
        used = int((tallies > 0).sum())
        fixed = max(1, used // 4)
        shifted = fixed + (places - fixed + rotation * (used - fixed)) % max(1, count - fixed)
        return jnp.zeros((count,), jnp.int32).at[ranking[jnp.where(places < fixed, places, shifted)]].set(jnp.asarray(tallies, jnp.int32))

    tallies = jnp.where(number % 4 == 0, named(packed, number // 4), named(ordinary, number - number // 4 - 1))
    mixed = jax.random.permutation(jax.random.fold_in(own, 3), count)
    giver, taker = mixed[0:count // 2 * 2:2], mixed[1:count // 2 * 2:2]
    room = jnp.minimum(tallies[giver] - 1, most - tallies[taker]) // 2
    room = jnp.where((giver == ranking[0]) | (taker == ranking[0]) | (tallies[taker] == 0), 0, jnp.maximum(room, 0))
    shifted = jax.random.randint(jax.random.fold_in(own, 4), (count // 2,), 0, 1 << 20) % (room + 1)
    tallies = tallies.at[giver].add(-shifted).at[taker].add(shifted)
    labels = jnp.searchsorted(jnp.cumsum(tallies), jnp.arange(rows * top), side="right").astype(jnp.int32)
    table = labels.reshape(top, rows).T
    table = table[jax.random.permutation(jax.random.fold_in(own, 1), rows)]
    rotation = jax.random.randint(jax.random.fold_in(own, 2), (rows, 1), 0, top)
    return jnp.take_along_axis(table, (jnp.arange(top)[None, :] + rotation) % top, axis=1)


def portions_of(amount, total, reach, lean, full):
    portions = [(1 << 20) // math.isqrt(standing ** lean) + 1 for standing in range(1, amount + 1)]
    largest = reach if full else min(reach, max(-(-total // amount), total * portions[0] // sum(portions)))
    least = 1 if total - largest >= amount - 1 else 0
    holding, surplus = [largest] + [least] * (amount - 1), total - largest - least * (amount - 1)
    while surplus > 0:
        candidates = [i for i in range(1, amount) if holding[i] < largest] or [i for i in range(1, amount) if holding[i] < reach]
        whole, left = sum([portions[i] for i in candidates]), surplus
        for i in candidates:
            more = min(reach - holding[i], max(1, left * portions[i] // whole), surplus)
            holding[i] = holding[i] + more
            surplus = surplus - more
    return np.array(holding)


def setup_inputs(seed: int = 0) -> dict:
    key_of = jax.random.split(jax.random.key(seed), 10)
    pieces = jnp.clip(0.19921875 + 1.8007812 * jax.random.uniform(key_of[0], (VIEWS, PIECES, CY, X), jnp.float32) ** block_levels(key_of[0], (VIEWS, PIECES, CY, X), ((0, 4), (1, 8)), -0.2, 0.2), 0.19921875, 2.0).astype(jnp.bfloat16)
    piece_owner_keys = jax.random.split(jax.random.fold_in(key_of[1], 1), VIEWS * PIECES // PIECES_DEV)
    piece_owner_turns = jax.random.permutation(jax.random.fold_in(key_of[1], 3), VIEWS * PIECES // PIECES_DEV)
    piece_owner = jax.vmap(lambda own, number: assign_block(jax.random.fold_in(key_of[1], 2), own, number, PIECES_DEV, N_GZ * N_GY, 1, CAP, 2))(piece_owner_keys, piece_owner_turns).reshape((VIEWS, PIECES, 1))
    piece_row = with_ends(jax.random.randint(key_of[2], (VIEWS, PIECES), 0, CZ), jax.random.fold_in(key_of[2], 1), 0, CZ - 1).astype(jnp.int32)
    estimate = jnp.clip(0.5 + 1.0 * jax.random.uniform(key_of[3], (NZ, NY, X), jnp.float32) ** block_levels(key_of[3], (NZ, NY, X), ((0, 2), (1, 4), (2, 4)), -0.2, 0.2), 0.5, 1.5)
    psf_x = jnp.clip(0.00097276265 + 0.0058365758 * jax.random.uniform(key_of[4], (VIEWS, KX), jnp.float32) ** block_levels(key_of[4], (VIEWS, KX), ((0, 4),), -0.2, 0.2), 0.00097276265, 0.0068093385)
    stencil = jnp.clip(0.03 + 0.17 * jax.random.uniform(key_of[5], (VIEWS, 3, 3), jnp.float32) ** block_levels(key_of[5], (VIEWS, 3, 3), ((0, 4),), -0.2, 0.2), 0.03, 0.2)
    background = jnp.clip(jnp.exp(math.log(0.5) - 2.3025851 * jax.random.uniform(key_of[6], (VIEWS,), jnp.float32) ** block_levels(key_of[6], (VIEWS,), ((0, 4),), -0.2, 0.2)), 0.05, 0.5)
    bleach_table = jnp.clip(jnp.exp(jax.random.uniform(key_of[7], (VIEWS, LEVELS), jnp.float32, math.log(0.2), math.log(2.0))), 0.2, 2.0)
    bleach_index = with_ends(jax.random.randint(key_of[8], (VIEWS, NZ), 0, LEVELS), jax.random.fold_in(key_of[8], 1), 0, LEVELS - 1).astype(jnp.int32)
    return dict(pieces=pieces, piece_owner=piece_owner, piece_row=piece_row, estimate=estimate, psf_x=psf_x, stencil=stencil, background=background, bleach_table=bleach_table, bleach_index=bleach_index)


def toeplitz(profile):
    row_ids = jnp.arange(X)[:, None]
    col_ids = jnp.arange(X)[None, :]
    offsets = row_ids - col_ids + HX
    inside = (offsets >= 0) & (offsets < KX)
    entries = jnp.take(profile, jnp.clip(offsets, 0, KX - 1))
    return jnp.where(inside, entries, jnp.float32(0.0)).astype(jnp.bfloat16)


def smear(padded, taps, depth_n, height_n):
    result = jnp.zeros((depth_n, height_n, padded.shape[2]), jnp.float32)
    for tap_z in range(3):
        for tap_y in range(3):
            result = result + taps[tap_z, tap_y] * padded[tap_z:tap_z + depth_n, tap_y:tap_y + height_n].astype(jnp.float32)
    return result


def apply_taps(volume, taps):
    padded = jnp.pad(volume, ((1, 1), (1, 1), (0, 0)))
    return smear(padded, taps, volume.shape[0], volume.shape[1])


def reference(pieces, piece_owner, piece_row, estimate, psf_x, stencil, background, bleach_table, bleach_index):
    owners = piece_owner[..., 0]
    z_rows = (owners // N_GY) * CZ + piece_row
    y_start = (owners % N_GY) * CY
    measured = []
    for view_no in range(VIEWS):
        y_cols = y_start[view_no][:, None] + jnp.arange(CY)[None, :]
        accumulated = jnp.zeros((NZ, NY, X), jnp.float32)
        accumulated = accumulated.at[z_rows[view_no][:, None], y_cols].add(pieces[view_no].astype(jnp.float32))
        measured.append(accumulated)
    levels = jnp.arange(LEVELS)
    matches = bleach_index[:, :, None] == levels[None, None, :]
    weight = jnp.sum(jnp.where(matches, bleach_table[:, None, :], jnp.float32(0.0)), axis=-1)
    total = jnp.sum(weight, axis=0)
    kernels = [toeplitz(psf_x[view_no]) for view_no in range(VIEWS)]
    latent = estimate
    for iteration in range(ITERS):
        latent_b = latent.astype(jnp.bfloat16).reshape(NZ * NY, X)
        ratios = []
        for view_no in range(VIEWS):
            blur_x = jnp.dot(latent_b, kernels[view_no], preferred_element_type=jnp.float32).astype(jnp.bfloat16).reshape(NZ, NY, X)
            blurred = apply_taps(blur_x, stencil[view_no])
            ratios.append((measured[view_no] / (blurred + background[view_no])).astype(jnp.bfloat16))
        numerator = jnp.zeros((NZ, NY, X), jnp.float32)
        for view_no in range(VIEWS):
            partner = ratios[view_no ^ 2]
            mixed = (0.5 * (ratios[view_no].astype(jnp.float32) + partner[:, :, ::-1].astype(jnp.float32))).astype(jnp.bfloat16)
            back_x = lax.dot_general(mixed.reshape(NZ * NY, X), kernels[view_no], (((1,), (1,)), ((), ())), preferred_element_type=jnp.float32)
            back_x = back_x.astype(jnp.bfloat16).reshape(NZ, NY, X)
            corrected = apply_taps(back_x, stencil[view_no][::-1, ::-1])
            numerator = numerator + weight[view_no][:, None, None] * corrected
        latent = latent * numerator / total[:, None, None]
    return latent
```

```python
import functools

import jax
import jax.numpy as jnp
from jax import lax
from jax.experimental import pallas as pl
from jax.experimental.pallas import tpu as pltpu
from jax.sharding import PartitionSpec as P

BF = jnp.bfloat16
F32 = jnp.float32
TILE = 256
LIMIT = 56 << 20


def whole(*spaces):
    return [pl.BlockSpec(memory_space=space) for space in spaces]


def swap(array, axis, size, mask):
    return lax.ppermute(array, axis, [(i, i ^ mask) for i in range(size)])


def upward(array, axis, size):
    return lax.ppermute(array, axis, [(i, i + 1) for i in range(size - 1)])


def downward(array, axis, size):
    return lax.ppermute(array, axis, [(i + 1, i) for i in range(size - 1)])


class Frame:
    def __init__(self, slabs, depth):
        self.mirrored = slabs == 2
        self.depth = depth
        self.own = 0 if self.mirrored else depth
        self.size = 2 * depth if self.mirrored else 3 * depth

    def need(self, radius):
        return range(
            max(0, self.own - radius), min(self.size, self.own + self.depth + radius)
        )

    def source(self, f):
        k = f - self.own
        if 0 <= k < self.depth:
            return "own", k
        if self.mirrored:
            return "up", 2 * self.depth - 1 - k
        return ("dn", f) if k < 0 else ("up", k - self.depth)

    def sent(self, radius):
        if self.mirrored:
            return {"up": range(self.depth - radius, self.depth)}
        return {
            "dn": range(self.depth - radius, self.depth),
            "up": range(0, radius),
        }


def exchange_z(frame, make, slabs, radius):
    got = {}
    for side, slices in frame.sent(radius).items():
        payload = make(slices)
        if frame.mirrored:
            got[side] = swap(payload, "gz", slabs, 1)
        elif side == "dn":
            got[side] = upward(payload, "gz", slabs)
        else:
            got[side] = downward(payload, "gz", slabs)
    return got


def cells_kernel(pairs, cell_ref, pieces_ref, even_ref, odd_ref, acc):
    count = pieces_ref.shape[0]

    def clear(i, carry):
        acc[i] = jnp.zeros(acc.shape[1:], F32)
        return carry

    lax.fori_loop(0, acc.shape[0], clear, 0)

    def add(i, carry):
        c = cell_ref[i]
        acc[c] = acc[c] + pieces_ref[i].astype(F32)
        return carry

    lax.fori_loop(0, count, add, 0)
    depth = even_ref.shape[1]

    def put(i, carry):
        pair = i // depth
        f = i % depth
        even_ref[pair, f] = acc[pair * 2 * depth + f].astype(BF)
        odd_ref[pair, f] = acc[(pair * 2 + 1) * depth + f].astype(BF)
        return carry

    lax.fori_loop(0, pairs * depth, put, 0)


def reversal():
    rows = lax.broadcasted_iota(jnp.int32, (TILE, TILE), 0)
    cols = lax.broadcasted_iota(jnp.int32, (TILE, TILE), 1)
    return jnp.where(rows + cols == TILE - 1, F32(1.0), F32(0.0)).astype(BF)


def total_kernel(parts, *refs):
    ins, (out_ref, rev_ref) = refs[:parts], refs[parts:]
    tiles = out_ref.shape[0]
    flip = reversal()
    for t in range(tiles):
        cut = slice(t * TILE, (t + 1) * TILE)
        acc = ins[0][:, :, cut].astype(F32)
        for ref in ins[1:]:
            acc = acc + ref[:, :, cut].astype(F32)
        block = acc.reshape(out_ref.shape[1:]).astype(BF)
        out_ref[t] = block
        rev_ref[tiles - 1 - t] = jnp.dot(
            block, flip, preferred_element_type=F32
        ).astype(BF)


def band(base_row):
    wide = jnp.broadcast_to(base_row, (TILE, 3 * TILE))
    return pltpu.roll(wide, 0, 1, stride=1, stride_axis=0).astype(BF)


def conv(src, first, tiles, rows, blocks, dst, step):
    s = 0
    while s < tiles:
        n = min(step, tiles - s)
        lhs = jnp.concatenate(
            [
                src[pl.ds(first + s + k, n)].reshape(n * rows, TILE)
                for k in range(3)
            ],
            axis=1,
        )
        dst[s : s + n] = jnp.dot(lhs, blocks, preferred_element_type=F32).reshape(
            n, rows, TILE
        )
        s += n


def taps_sum(slices, zs, taps):
    result = {}
    for z in zs:
        sums = [None, None, None]
        for j in range(3):
            for i in range(3):
                at = z + i - 1
                if at in slices:
                    term = taps(z, i, j) * slices[at]
                    sums[j] = term if sums[j] is None else sums[j] + term
        result[z] = sums
    return result


def along_y(sums):
    n = sums[0].shape[0]
    return pltpu.roll(sums[0], 1, 0) + sums[1] + pltpu.roll(sums[2], n - 1, 0)


def forward_kernel(
    frame, tiles, sides, num_ref, base_ref, own_ref, *refs
):
    halo_ref = refs[len(sides)]
    side_refs = dict(zip(sides, refs[: len(sides)]))
    blocks_ref, recip_ref, frame_ref, u, c = refs[len(sides) + 1 :]
    size = frame.size
    rows = size * 16
    flip = reversal()
    for v in range(4):
        fwd = band(base_ref[v : v + 1, :])
        bwd = band(base_ref[4 + v : 5 + v, :])
        f3 = [fwd[:, 2 * TILE :], fwd[:, TILE : 2 * TILE], fwd[:, :TILE]]
        b3 = [bwd[:, 2 * TILE :], bwd[:, TILE : 2 * TILE], bwd[:, :TILE]]
        if v >= 2:
            f3 = [
                jnp.dot(x, flip, preferred_element_type=F32).astype(BF) for x in f3
            ]
            b3 = [
                jnp.dot(flip, x, preferred_element_type=F32).astype(BF)
                for x in b3[::-1]
            ]
        for k in range(3):
            blocks_ref[v, 0, k * TILE : (k + 1) * TILE, :] = f3[k]
            blocks_ref[v, 1, k * TILE : (k + 1) * TILE, :] = b3[k]
    u[0] = jnp.zeros((rows, TILE), BF)
    u[tiles + 1] = jnp.zeros((rows, TILE), BF)

    def fill(t, carry):
        for f in range(size):
            where, k = frame.source(f)
            src = own_ref if where == "own" else side_refs[where]
            both = jnp.concatenate(
                [
                    src[t, k * 8 : (k + 1) * 8, :].astype(F32),
                    halo_ref[t, f * 8 : (f + 1) * 8, :].astype(F32),
                ],
                axis=0,
            ).astype(BF)
            u[t + 1, f * 16 : (f + 1) * 16, :] = both
            frame_ref[t, f * 16 : (f + 1) * 16, :] = both
        return carry

    lax.fori_loop(0, tiles, fill, 0)
    zs = frame.need(3)
    for v in range(4):
        conv(u, 0, tiles, rows, blocks_ref[v, 0], c, 2)

        def divide(t, carry, v=v):
            from_t = t if v < 2 else tiles - 1 - t
            for h in range(TILE // 128):
                cut = slice(h * 128, (h + 1) * 128)
                slices = {
                    f: c[from_t, f * 16 : (f + 1) * 16, cut] for f in range(size)
                }
                sums = taps_sum(slices, zs, lambda z, i, j: num_ref[v * 9 + i * 3 + j])
                for n, z in enumerate(zs):
                    recip_ref[v, t, n * 16 : (n + 1) * 16, cut] = (
                        1.0 / (along_y(sums[z]) + num_ref[36 + v])
                    ).astype(BF)
            return carry

        lax.fori_loop(0, tiles, divide, 0)


def main_kernel(frame, tiles, sides, int_ref, num_ref, wt_ref, est_ref, *refs):
    own_refs = refs[:4]
    side_refs = dict(zip(sides, refs[4 : 4 + len(sides)]))
    halo_ref, blocks_ref, recip_ref, frame_ref, out_ref = refs[
        4 + len(sides) : 9 + len(sides)
    ]
    m1, u2, m2, c0, c1, c2, c3, kept = refs[9 + len(sides) :]
    c = [c0, c1, c2, c3]
    view, upside = int_ref[0], int_ref[1]
    depth = frame.depth
    z3, z2, z1, z0 = (frame.need(r) for r in (3, 2, 1, 0))
    skip = {
        side: min(slices) for side, slices in frame.sent(3).items()
    }
    meas_at = {z: n for n, z in enumerate(z3)}

    def measured(v, t, z, cut):
        where, k = frame.source(z)
        n = meas_at[z]
        if where == "own":
            own = own_refs[v][t, k * 8 : (k + 1) * 8, cut]
        else:
            k = k - skip[where]
            own = side_refs[where][v, t, k * 8 : (k + 1) * 8, cut]
        return jnp.concatenate(
            [
                own.astype(F32),
                halo_ref[v, t, n * 8 : (n + 1) * 8, cut].astype(F32),
            ],
            axis=0,
        )

    def mix(v, t, z, cut, recip_a, recip_b):
        a = (measured(v, t, z, cut) * recip_a).astype(BF).astype(F32)
        b = (measured(v + 2, t, z, cut) * recip_b).astype(BF).astype(F32)
        return (0.5 * (a + b)).astype(BF)

    def zero_ends(ref):
        for e in (0, ref.shape[0] - 1):
            ref[e] = jnp.zeros(ref.shape[1:], BF)

    for ref in (m1, u2, m2):
        zero_ends(ref)

    for v in range(2):

        def ratios(t, carry, v=v):
            for h in range(TILE // 128):
                cut = slice(h * 128, (h + 1) * 128)
                for n, z in enumerate(z3):
                    at = slice(n * 16, (n + 1) * 16)
                    m1[t + 1, at, cut] = mix(
                        v,
                        t,
                        z,
                        cut,
                        recip_ref[v, t, at, cut].astype(F32),
                        recip_ref[v + 2, t, at, cut].astype(F32),
                    )
            return carry

        lax.fori_loop(0, tiles, ratios, 0)
        for w in (v, v + 2):
            conv(m1, 0, tiles, m1.shape[1], blocks_ref[w, 1], c[w], 2)

    def numerator(slices_of, zs):
        totals = {z: [None, None, None] for z in zs}
        for v in range(4):
            slices = slices_of(v)
            sums = taps_sum(
                slices,
                zs,
                lambda z, i, j, v=v: wt_ref[(v * frame.size + z) * 9 + i * 3 + j],
            )
            for z in zs:
                for j in range(3):
                    old = totals[z][j]
                    totals[z][j] = sums[z][j] if old is None else old + sums[z][j]
        return totals

    def update(t, carry):
        for h in range(TILE // 128):
            cut = slice(h * 128, (h + 1) * 128)

            def slices_of(v):
                from_t = t if v < 2 else tiles - 1 - t
                return {
                    z: c[v][from_t, n * 16 : (n + 1) * 16, cut]
                    for n, z in enumerate(z3)
                }

            totals = numerator(slices_of, z2)
            for n, z in enumerate(z2):
                change = along_y(totals[z])
                before = frame_ref[t, z * 16 : (z + 1) * 16, cut].astype(F32)
                u2[t + 1, n * 16 : (n + 1) * 16, cut] = (before * change).astype(BF)
                if z in z0:
                    k = z - frame.own
                    kept[t, k * 8 : (k + 1) * 8, cut] = change[:8]
        return carry

    lax.fori_loop(0, tiles, update, 0)

    rows1 = m2.shape[1]
    n2 = u2.shape[1]
    for v in range(2):
        for w in (v, v + 2):
            conv(u2, 0, tiles, n2, blocks_ref[w, 0], c[w].at[:, :n2, :], 2)

        def ratios2(t, carry, v=v):
            for h in range(TILE // 128):
                cut = slice(h * 128, (h + 1) * 128)
                recips = []
                for w in (v, v + 2):
                    from_t = t if w < 2 else tiles - 1 - t
                    slices = {
                        z: c[w][from_t, n * 16 : (n + 1) * 16, cut]
                        for n, z in enumerate(z2)
                    }
                    sums = taps_sum(
                        slices, z1, lambda z, i, j, w=w: num_ref[w * 9 + i * 3 + j]
                    )
                    recips.append(
                        {z: 1.0 / (along_y(sums[z]) + num_ref[36 + w]) for z in z1}
                    )
                for n, z in enumerate(z1):
                    m2[t + 1, n * 16 : (n + 1) * 16, cut] = mix(
                        v, t, z, cut, recips[0][z], recips[1][z]
                    )
            return carry

        lax.fori_loop(0, tiles, ratios2, 0)
        mine = tiles // 4
        for w in (v, v + 2):
            first = view * mine if w < 2 else tiles - (view + 1) * mine
            conv(m2, first, mine, rows1, blocks_ref[w, 1], c[w].at[:, :rows1, :], 2)

    mine = tiles // 4
    for s in range(mine):
        for h in range(TILE // 128):
            cut = slice(h * 128, (h + 1) * 128)

            def slices_of(v):
                from_s = s if v < 2 else mine - 1 - s
                return {
                    z: c[v][from_s, n * 16 : (n + 1) * 16, cut]
                    for n, z in enumerate(z1)
                }

            totals = numerator(slices_of, z0)
            for z in z0:
                k = z - frame.own
                to = k + upside * (depth - 1 - 2 * k)
                lanes = slice(s * TILE + h * 128, s * TILE + (h + 1) * 128)
                first_change = kept[view * mine + s, k * 8 : (k + 1) * 8, cut]
                out_ref[to, :, lanes] = (
                    est_ref[to, :, lanes] * first_change * along_y(totals[z])[:8]
                )


def shards(
    pieces, piece_owner, piece_row, estimate, psf_x, stencil, background, bleach_table, bleach_index
):
    depth, height = estimate.shape[:2]
    chunk = estimate.shape[2]
    width = pieces.shape[3]
    tiles = width // TILE
    slabs = lax.axis_size("gz")
    bands = lax.axis_size("gy")
    blocks = slabs * bands
    frame = Frame(slabs, depth)
    view = lax.axis_index("view")
    slab = lax.axis_index("gz")
    me = slab * bands + lax.axis_index("gy")
    upside = (slab if frame.mirrored else 0 * slab).astype(jnp.int32)
    vmem, smem = pltpu.VMEM, pltpu.SMEM
    params = pltpu.CompilerParams(vmem_limit_bytes=LIMIT)

    turned = jnp.where(upside == 1, estimate[::-1], estimate).astype(BF)
    half = (psf_x.shape[1] - 1) // 2
    profile = psf_x[0].astype(BF)
    exact = jnp.concatenate(
        [
            jnp.where(upside == 1, stencil[0][::-1], stencil[0]).reshape(-1),
            background,
        ]
    )
    part0 = lax.reduce_precision(exact, 8, 7)
    part1 = lax.reduce_precision(exact - part0, 8, 7)
    part2 = lax.reduce_precision(exact - part0 - part1, 8, 7)

    def row(x):
        return jnp.pad(x, (0, chunk - x.shape[0]))[None]

    extra = jnp.concatenate(
        [row(profile), row(profile[::-1])]
        + [row(x.astype(BF)) for x in (part0, part1, part2)]
        + [jnp.zeros((3, chunk), BF)],
        axis=0,
    )
    payload = jnp.concatenate([turned.reshape(depth * height, chunk), extra], axis=0)
    heard = [payload] + [swap(payload, "view", 4, mask) for mask in (1, 2, 3)]
    heard = jnp.stack(heard)
    numbers = heard[:, depth * height :]
    parts = numbers[:, 2:5, :10].astype(F32)
    exacts = parts[:, 0] + parts[:, 1] + parts[:, 2]
    taps_all = exacts[:, :9]
    nums = jnp.concatenate([taps_all.reshape(-1), exacts[:, 9]])
    edge = TILE - half
    base = jnp.pad(
        jnp.concatenate([numbers[:, 1, : 2 * half + 1], numbers[:, 0, : 2 * half + 1]]),
        ((0, 0), (edge, 3 * TILE - edge - 2 * half - 1)),
    ).astype(F32)

    def ordered(x):
        a = jnp.where(view % 2 == 1, jnp.stack([x[1], x[0], x[3], x[2]]), x)
        return jnp.where(view // 2 == 1, jnp.concatenate([a[2:], a[:2]]), a)

    own_est = ordered(
        heard[:, : depth * height]
        .reshape(4, depth * height, chunk // TILE, TILE)
        .transpose(0, 2, 1, 3)
    ).reshape(tiles, depth * height, TILE)

    index_own = jnp.where(upside == 1, bleach_index[:, ::-1], bleach_index)
    index_far = exchange_z(
        frame, lambda s: index_own[:, s.start : s.stop], slabs, depth
    )

    def frame_index(f):
        where, k = frame.source(f)
        return (index_own if where == "own" else index_far[where])[:, k]

    indices = jnp.stack([frame_index(f) for f in range(frame.size)], axis=1)
    levels = jnp.arange(bleach_table.shape[1])
    matches = indices[:, :, None] == levels[None, None, :]
    weight = jnp.sum(jnp.where(matches, bleach_table[:, None, :], F32(0.0)), axis=-1)
    share = ordered(weight / jnp.sum(weight, axis=0))
    weighted = (share[:, :, None] * taps_all[:, ::-1][:, None, :]).reshape(-1)

    sides = tuple(frame.sent(1))
    far_est = exchange_z(
        frame,
        lambda s: own_est[:, s.start * height : s.stop * height],
        slabs,
        depth,
    )

    def z_list(own, far, radius):
        first = {side: min(s) for side, s in frame.sent(radius).items()}
        picked = []
        for f in frame.need(radius):
            where, k = frame.source(f)
            if where == "own":
                picked.append(own[..., k * height : (k + 1) * height, :])
            else:
                k = k - first[where]
                picked.append(far[where][..., k * height : (k + 1) * height, :])
        return jnp.stack(picked, axis=-3)

    def y_halo(stacked):
        hi = downward(stacked[..., : height // 2, :], "gy", bands)
        lo = upward(stacked[..., height // 2 :, :], "gy", bands)
        tile = jnp.concatenate([hi, lo], axis=-2)
        return tile.reshape(tile.shape[:-3] + (-1, TILE))

    halo_est = y_halo(z_list(own_est, far_est, depth))
    size = frame.size
    blocks_all, recip, est_frame = pl.pallas_call(
        functools.partial(forward_kernel, frame, tiles, sides),
        out_shape=(
            jax.ShapeDtypeStruct((4, 2, 3 * TILE, TILE), BF),
            jax.ShapeDtypeStruct((4, tiles, len(frame.need(3)) * 16, TILE), BF),
            jax.ShapeDtypeStruct((tiles, size * 16, TILE), BF),
        ),
        in_specs=whole(smem, *([vmem] * (3 + len(sides)))),
        out_specs=whole(vmem, vmem, vmem),
        scratch_shapes=[
            vmem((tiles + 2, size * 16, TILE), BF),
            vmem((tiles, size * 16, TILE), F32),
        ],
        compiler_params=params,
    )(nums, base, own_est, *[far_est[s] for s in sides], halo_est)

    owners = piece_owner[0, :, 0]
    rows = piece_row[0]
    if frame.mirrored:
        rows = jnp.where(owners // bands == 1, depth - 1 - rows, rows)
    cell = (owners ^ me) * depth + rows
    pairs = blocks // 2
    half_cells = jax.ShapeDtypeStruct((pairs, depth, height, width), BF)
    even, odd = pl.pallas_call(
        functools.partial(cells_kernel, pairs),
        out_shape=(half_cells, half_cells),
        in_specs=whole(smem, vmem),
        out_specs=whole(vmem, vmem),
        scratch_shapes=[vmem((blocks * depth, height, width), F32)],
        compiler_params=params,
    )(cell, pieces[0])
    other = swap(odd, "gy", bands, 1)
    kept = [even[k] + other[k] for k in range(pairs)]
    kept = kept[:1] + [
        swap(kept[k], ("gz", "gy"), blocks, 2 * k) for k in range(1, pairs)
    ]
    block = jax.ShapeDtypeStruct((tiles, depth * height, TILE), BF)
    plain, turned_x = pl.pallas_call(
        functools.partial(total_kernel, pairs),
        out_shape=(block, block),
        in_specs=whole(*([vmem] * pairs)),
        out_specs=whole(vmem, vmem),
        compiler_params=params,
    )(*kept)
    views = [
        plain,
        swap(plain, "view", 4, 1),
        swap(turned_x, "view", 4, 2),
        swap(turned_x, "view", 4, 3),
    ]
    far = exchange_z(
        frame,
        lambda s: jnp.stack([x[:, s.start * height : s.stop * height] for x in views]),
        slabs,
        3,
    )
    halo = y_halo(
        jnp.stack(
            [
                z_list(x, {s: far[s][v] for s in sides}, 3)
                for v, x in enumerate(views)
            ]
        )
    )
    ints = jnp.stack([view.astype(jnp.int32), upside])
    n3, n2, n1 = (len(frame.need(r)) * 16 for r in (3, 2, 1))
    return pl.pallas_call(
        functools.partial(main_kernel, frame, tiles, sides),
        out_shape=jax.ShapeDtypeStruct(estimate.shape, F32),
        in_specs=whole(smem, smem, smem, *([vmem] * (9 + len(sides)))),
        out_specs=pl.BlockSpec(memory_space=vmem),
        scratch_shapes=[
            vmem((tiles + 2, n3, TILE), BF),
            vmem((tiles + 2, n2, TILE), BF),
            vmem((tiles + 2, n1, TILE), BF),
        ]
        + [vmem((tiles, n3, TILE), F32)] * 4
        + [vmem((tiles, depth * height, TILE), F32)],
        compiler_params=params,
    )(
        ints,
        nums,
        weighted,
        estimate,
        *views,
        *[far[s] for s in sides],
        halo,
        blocks_all,
        recip,
        est_frame,
    )


def solution(mesh):
    placed = (
        P("view", ("gz", "gy"), None, None),
        P("view", ("gz", "gy"), None),
        P("view", ("gz", "gy")),
        P("gz", "gy", "view"),
        P("view", None),
        P("view", None, None),
        P("view"),
        P(),
        P(None, "gz"),
    )
    return jax.shard_map(
        shards, mesh=mesh, in_specs=placed, out_specs=P("gz", "gy", "view"), check_vma=False
    )
```

```python
import functools

import jax
import jax.numpy as jnp
from jax import lax
from jax.experimental import pallas as pl
from jax.experimental.pallas import tpu as pltpu
from jax.sharding import PartitionSpec as P

BF = jnp.bfloat16
F32 = jnp.float32
TILE = 256
LIMIT = 56 << 20


def whole(*spaces):
    return [pl.BlockSpec(memory_space=space) for space in spaces]


def swap(array, axis, size, mask):
    return lax.ppermute(array, axis, [(i, i ^ mask) for i in range(size)])


def upward(array, axis, size):
    return lax.ppermute(array, axis, [(i, i + 1) for i in range(size - 1)])


def downward(array, axis, size):
    return lax.ppermute(array, axis, [(i + 1, i) for i in range(size - 1)])


class Frame:
    def __init__(self, slabs, depth):
        self.mirrored = slabs == 2
        self.depth = depth
        self.own = 0 if self.mirrored else depth
        self.size = 2 * depth if self.mirrored else 3 * depth

    def need(self, radius):
        return range(
            max(0, self.own - radius), min(self.size, self.own + self.depth + radius)
        )

    def source(self, f):
        k = f - self.own
        if 0 <= k < self.depth:
            return "own", k
        if self.mirrored:
            return "up", 2 * self.depth - 1 - k
        return ("dn", f) if k < 0 else ("up", k - self.depth)

    def place(self, f, radius):
        where, k = self.source(f)
        at = 0
        for name, slices in [("own", range(self.depth))] + list(self.sent(radius).items()):
            if name == where:
                return at + k - slices.start
            at += len(slices)

    def sent(self, radius):
        if self.mirrored:
            return {"up": range(self.depth - radius, self.depth)}
        return {
            "dn": range(self.depth - radius, self.depth),
            "up": range(0, radius),
        }


def exchange_z(frame, make, slabs, radius):
    got = {}
    for side, slices in frame.sent(radius).items():
        payload = make(slices)
        if frame.mirrored:
            got[side] = swap(payload, "gz", slabs, 1)
        elif side == "dn":
            got[side] = upward(payload, "gz", slabs)
        else:
            got[side] = downward(payload, "gz", slabs)
    return got


def place():
    return lax.axis_index("view"), lax.axis_index("gz")


def cells_kernel(pairs, bands, mirrored, owner_ref, row_ref, pieces_ref, even_ref, odd_ref, acc):
    count = pieces_ref.shape[0]
    depth = even_ref.shape[1]
    me = lax.axis_index("gz") * bands + lax.axis_index("gy")

    def clear(i, carry):
        acc[i] = jnp.zeros(acc.shape[1:], F32)
        return carry

    lax.fori_loop(0, acc.shape[0], clear, 0)

    def add(i, carry):
        owner = owner_ref[0, i, 0]
        row = row_ref[0, i]
        if mirrored:
            row = jnp.where(owner >= bands, depth - 1 - row, row)
        c = (owner ^ me) * depth + row
        acc[c] = acc[c] + pieces_ref[i].astype(F32)
        return carry

    lax.fori_loop(0, count, add, 0)

    def put(pair, carry):
        for f in range(depth):
            even_ref[pair, f] = acc[pair * 2 * depth + f].astype(BF)
            odd_ref[pair, f] = acc[(pair * 2 + 1) * depth + f].astype(BF)
        return carry

    lax.fori_loop(0, pairs, put, 0)


def payload_kernel(mirrored, taps_ref, bg_ref, est_ref, psf_ref, out_ref, tail):
    depth, height = est_ref.shape[:2]
    upside = lax.axis_index("gz") if mirrored else 0
    for k in range(depth):
        out_ref[k * height : (k + 1) * height, :] = est_ref[
            k + upside * (depth - 1 - 2 * k)
        ].astype(BF)
    tail[...] = jnp.zeros(tail.shape, F32)
    tail[0:1, : psf_ref.shape[1]] = psf_ref[...]
    lanes = lax.broadcasted_iota(jnp.int32, (1, 128), 1)
    exact = jnp.where(lanes == 9, bg_ref[0], F32(0.0))
    for i in range(3):
        for j in range(3):
            tap = taps_ref[0, i + upside * (2 - 2 * i), j]
            exact = jnp.where(lanes == i * 3 + j, tap, exact)
    for n in range(3):
        part = exact.astype(BF).astype(F32)
        tail[n + 1 : n + 2, :128] = part
        exact = exact - part
    out_ref[depth * height :, :] = tail[...].astype(BF)


def reversal():
    rows = lax.broadcasted_iota(jnp.int32, (TILE, TILE), 0)
    cols = lax.broadcasted_iota(jnp.int32, (TILE, TILE), 1)
    return jnp.where(rows + cols == TILE - 1, F32(1.0), F32(0.0)).astype(BF)


def total_kernel(parts, *refs):
    ins, (out_ref, rev_ref) = refs[:parts], refs[parts:]
    tiles, rows, _ = out_ref.shape
    for t in range(tiles):
        cut = slice(t * TILE, (t + 1) * TILE)
        acc = ins[0][:, :, cut].astype(F32)
        for ref in ins[1:]:
            acc = acc + ref[:, :, cut].astype(F32)
        out_ref[t] = acc.reshape(rows, TILE).astype(BF)
    back = jnp.dot(
        out_ref[...].reshape(tiles * rows, TILE), reversal(), preferred_element_type=F32
    ).astype(BF)
    for t in range(tiles):
        rev_ref[tiles - 1 - t] = back[t * rows : (t + 1) * rows]


def band_kernel(at, *refs):
    heard, out_ref = refs[:4], refs[4]
    flip = reversal()
    for v in range(4):
        row = heard[v][at : at + 8, : 3 * 128].astype(F32)[0:1]
        edge = TILE // 2
        base = jnp.concatenate(
            [jnp.zeros((1, edge), F32), row, jnp.zeros((1, 2 * edge), F32)], axis=1
        )
        wide = pltpu.roll(
            jnp.broadcast_to(base, (TILE, 3 * TILE)), 0, 1, stride=1, stride_axis=0
        ).astype(BF)
        turned = jnp.dot(flip, wide, preferred_element_type=F32).astype(BF)
        for k in range(3):
            cut = slice(k * TILE, (k + 1) * TILE)
            to = slice((2 - k) * TILE, (3 - k) * TILE)
            if v >= 2:
                out_ref[2 + v, cut, :] = turned[:, cut]
            else:
                out_ref[2 + v, to, :] = wide[:, cut]
                out_ref[v, cut, :] = jnp.dot(
                    turned[:, cut], flip, preferred_element_type=F32
                ).astype(BF)


def forward_block(v):
    return v if v < 2 else v + 2


def backward_block(v):
    return v + 2


def conv(src, first, tiles, rows, blocks, dst, step):
    s = 0
    while s < tiles:
        n = min(step, tiles - s)
        lhs = jnp.concatenate(
            [
                src[pl.ds(first + s + k, n)].reshape(n * rows, TILE)
                for k in range(3)
            ],
            axis=1,
        )
        out = jnp.dot(lhs, blocks, preferred_element_type=F32).astype(BF)
        dst[s : s + n] = out.reshape(n, rows, TILE)
        s += n


def taps_sum(slices, zs, taps):
    result = {}
    for z in zs:
        sums = [None, None, None]
        for j in range(3):
            for i in range(3):
                at = z + i - 1
                if at in slices:
                    term = taps(z, i, j) * slices[at]
                    sums[j] = term if sums[j] is None else sums[j] + term
        result[z] = sums
    return result


def along_y(sums):
    n = sums[0].shape[0]
    return pltpu.roll(sums[0], 1, 0) + sums[1] + pltpu.roll(sums[2], n - 1, 0)


def frame_kernel(frame, tiles, sides, *refs):
    own_refs, refs = refs[:4], refs[4:]
    side_refs = dict(zip(sides, refs[: len(sides)]))
    hi_ref, lo_ref, out_ref = refs[len(sides) :]
    view = lax.axis_index("view")
    for e in (0, tiles + 1):
        out_ref[e] = jnp.zeros(out_ref.shape[1:], BF)
    for v in range(4):
        for s in range(tiles // 4):
            t = (view ^ v) * (tiles // 4) + s + 1
            cut = slice(s * TILE, (s + 1) * TILE)
            for f in range(frame.size):
                where, k = frame.source(f)
                rows = slice(k * 8, (k + 1) * 8)
                if where == "own":
                    own = own_refs[v][rows, cut]
                else:
                    own = side_refs[where][v, rows, cut]
                n = frame.place(f, frame.depth)
                out_ref[t, f * 16 : (f + 1) * 16, :] = jnp.concatenate(
                    [
                        own.astype(F32),
                        hi_ref[v, n, :, cut].astype(F32),
                        lo_ref[v, n, :, cut].astype(F32),
                    ],
                    axis=0,
                ).astype(BF)


def forward_kernel(frame, tiles, views, num_ref, blocks_ref, frame_ref, recip_ref, c):
    size = frame.size
    zs = frame.need(3)
    for at, v in enumerate(views):
        conv(frame_ref, 0, tiles, size * 16, blocks_ref[forward_block(v)], c, 2)

        def divide(t, carry, v=v, at=at):
            from_t = t if v < 2 else tiles - 1 - t
            for h in range(TILE // 128):
                cut = slice(h * 128, (h + 1) * 128)
                slices = {
                    f: c[from_t, f * 16 : (f + 1) * 16, cut].astype(F32)
                    for f in range(size)
                }
                sums = taps_sum(slices, zs, lambda z, i, j: num_ref[v * 9 + i * 3 + j])
                for n, z in enumerate(zs):
                    recip_ref[at, t, n * 16 : (n + 1) * 16, cut] = (
                        1.0 / (along_y(sums[z]) + num_ref[36 + v])
                    ).astype(BF)
            return carry

        lax.fori_loop(0, tiles, divide, 0)


def main_kernel(frame, tiles, sides, num_ref, wt_ref, est_ref, *refs):
    own_refs, refs = refs[:4], refs[4:]
    count = len(sides)
    far_refs, refs = refs[: 2 * count], refs[2 * count :]
    hi_refs, lo_refs = refs[0:2], refs[2:4]
    recip_refs = refs[4:6]
    blocks_ref, frame_ref, out_ref = refs[6:9]
    m1, u2, m2, c0, c1, c2, c3, kept = refs[9:]
    c = [c0, c1, c2, c3]
    view = lax.axis_index("view")
    upside = lax.axis_index("gz") if frame.mirrored else 0
    depth = frame.depth
    z3, z2, z1, z0 = (frame.need(r) for r in (3, 2, 1, 0))
    sent = frame.sent(3)

    def measured(v, t, z, cut):
        where, k = frame.source(z)
        pair, w = v // 2, v % 2
        if where == "own":
            own = own_refs[v][t, k * 8 : (k + 1) * 8, cut]
        else:
            k = k - sent[where].start
            far = far_refs[pair * count + sides.index(where)]
            own = far[w, t, k * 8 : (k + 1) * 8, cut]
        n = frame.place(z, 3)
        return jnp.concatenate(
            [
                own.astype(F32),
                hi_refs[pair][w, t, n, :, cut].astype(F32),
                lo_refs[pair][w, t, n, :, cut].astype(F32),
            ],
            axis=0,
        )

    def mix(v, t, z, cut, recip_a, recip_b):
        a = (measured(v, t, z, cut) * recip_a).astype(BF).astype(F32)
        b = (measured(v + 2, t, z, cut) * recip_b).astype(BF).astype(F32)
        return (0.5 * (a + b)).astype(BF)

    def zero_ends(ref):
        for e in (0, ref.shape[0] - 1):
            ref[e] = jnp.zeros(ref.shape[1:], BF)

    for ref in (m1, u2, m2):
        zero_ends(ref)

    for v in range(2):

        def ratios(t, carry, v=v):
            for h in range(TILE // 128):
                cut = slice(h * 128, (h + 1) * 128)
                for n, z in enumerate(z3):
                    at = slice(n * 16, (n + 1) * 16)
                    m1[t + 1, at, cut] = mix(
                        v,
                        t,
                        z,
                        cut,
                        recip_refs[0][v, t, at, cut].astype(F32),
                        recip_refs[1][v, t, at, cut].astype(F32),
                    )
            return carry

        lax.fori_loop(0, tiles, ratios, 0)
        for w in (v, v + 2):
            conv(m1, 0, tiles, m1.shape[1], blocks_ref[backward_block(w)], c[w], 2)

    def numerator(slices_of, zs):
        totals = {z: [None, None, None] for z in zs}
        for v in range(4):
            slices = slices_of(v)
            sums = taps_sum(
                slices,
                zs,
                lambda z, i, j, v=v: wt_ref[(v * frame.size + z) * 9 + i * 3 + j],
            )
            for z in zs:
                for j in range(3):
                    old = totals[z][j]
                    totals[z][j] = sums[z][j] if old is None else old + sums[z][j]
        return totals

    def update(t, carry):
        for h in range(TILE // 128):
            cut = slice(h * 128, (h + 1) * 128)

            def slices_of(v):
                from_t = t if v < 2 else tiles - 1 - t
                return {
                    z: c[v][from_t, n * 16 : (n + 1) * 16, cut].astype(F32)
                    for n, z in enumerate(z3)
                }

            totals = numerator(slices_of, z2)
            for n, z in enumerate(z2):
                change = along_y(totals[z])
                before = frame_ref[t + 1, z * 16 : (z + 1) * 16, cut].astype(F32)
                u2[t + 1, n * 16 : (n + 1) * 16, cut] = (before * change).astype(BF)
                if z in z0:
                    k = z - frame.own
                    kept[t, k * 8 : (k + 1) * 8, cut] = change[:8]
        return carry

    lax.fori_loop(0, tiles, update, 0)

    rows1 = m2.shape[1]
    n2 = u2.shape[1]
    for v in range(2):
        for w in (v, v + 2):
            conv(u2, 0, tiles, n2, blocks_ref[forward_block(w)], c[w].at[:, :n2, :], 2)

        def ratios2(t, carry, v=v):
            for h in range(TILE // 128):
                cut = slice(h * 128, (h + 1) * 128)
                recips = []
                for w in (v, v + 2):
                    from_t = t if w < 2 else tiles - 1 - t
                    slices = {
                        z: c[w][from_t, n * 16 : (n + 1) * 16, cut].astype(F32)
                        for n, z in enumerate(z2)
                    }
                    sums = taps_sum(
                        slices, z1, lambda z, i, j, w=w: num_ref[w * 9 + i * 3 + j]
                    )
                    recips.append(
                        {z: 1.0 / (along_y(sums[z]) + num_ref[36 + w]) for z in z1}
                    )
                for n, z in enumerate(z1):
                    m2[t + 1, n * 16 : (n + 1) * 16, cut] = mix(
                        v, t, z, cut, recips[0][z], recips[1][z]
                    )
            return carry

        lax.fori_loop(0, tiles, ratios2, 0)
        mine = tiles // 4
        for w in (v, v + 2):
            first = view * mine if w < 2 else tiles - (view + 1) * mine
            conv(m2, first, mine, rows1, blocks_ref[backward_block(w)], c[w].at[:, :rows1, :], 2)

    mine = tiles // 4
    for s in range(mine):
        for h in range(TILE // 128):
            cut = slice(h * 128, (h + 1) * 128)

            def slices_of(v):
                from_s = s if v < 2 else mine - 1 - s
                return {
                    z: c[v][from_s, n * 16 : (n + 1) * 16, cut].astype(F32)
                    for n, z in enumerate(z1)
                }

            totals = numerator(slices_of, z0)
            for z in z0:
                k = z - frame.own
                to = k + upside * (depth - 1 - 2 * k)
                lanes = slice(s * TILE + h * 128, s * TILE + (h + 1) * 128)
                first_change = kept[view * mine + s, k * 8 : (k + 1) * 8, cut]
                out_ref[to, :, lanes] = (
                    est_ref[to, :, lanes] * first_change * along_y(totals[z])[:8]
                )


def after(token, *arrays):
    return lax.optimization_barrier((token,) + arrays)[1:]


def shards(
    pieces, piece_owner, piece_row, estimate, psf_x, stencil, background, bleach_table, bleach_index
):
    depth, height, chunk = estimate.shape
    width = pieces.shape[3]
    tiles = width // TILE
    slabs = lax.axis_size("gz")
    bands = lax.axis_size("gy")
    blocks = slabs * bands
    frame = Frame(slabs, depth)
    size = frame.size
    sides = tuple(frame.sent(1))
    view = lax.axis_index("view")
    vmem, smem = pltpu.VMEM, pltpu.SMEM
    params = pltpu.CompilerParams(vmem_limit_bytes=LIMIT)

    def call(kernel, shapes, ins, outs, *args, scratch=()):
        return pl.pallas_call(
            kernel,
            out_shape=shapes,
            in_specs=whole(*ins),
            out_specs=whole(*outs) if isinstance(shapes, tuple) else whole(*outs)[0],
            scratch_shapes=list(scratch),
            compiler_params=params,
        )(*args)

    def shape(*dims, dtype=BF):
        return jax.ShapeDtypeStruct(dims, dtype)

    pairs = blocks // 2
    half_cells = shape(pairs, depth, height, width)
    even, odd = call(
        functools.partial(cells_kernel, pairs, bands, frame.mirrored),
        (half_cells, half_cells),
        (smem, smem, vmem),
        (vmem, vmem),
        piece_owner,
        piece_row,
        pieces[0],
        scratch=[vmem((blocks * depth, height, width), F32)],
    )
    other = swap(odd, "gy", bands, 1)

    area = depth * height
    late = after(even[0, 0, 0, 0], stencil, background, estimate, psf_x, bleach_index)
    payload = call(
        functools.partial(payload_kernel, frame.mirrored),
        shape(area + 8, chunk),
        (smem, smem, vmem, vmem),
        (vmem,),
        *late[:4],
        scratch=[vmem((8, chunk), F32)],
    )
    heard = [payload] + [swap(payload, "view", 4, mask) for mask in (1, 2, 3)]

    kept = [even[k] + other[k] for k in range(pairs)]
    moved = [swap(kept[k], ("gz", "gy"), blocks, 2 * k) for k in range(1, pairs)]
    plain, turned = call(
        functools.partial(total_kernel, pairs),
        (shape(tiles, area, TILE), shape(tiles, area, TILE)),
        [vmem] * pairs,
        (vmem, vmem),
        kept[0],
        *moved,
    )

    heard = after(kept[1][0, 0, 0], *heard)
    own_est = jnp.stack([x[:area] for x in heard])
    far_est = exchange_z(
        frame, lambda s: own_est[:, s.start * height : s.stop * height], slabs, depth
    )

    def y_halo(own, far):
        def rows(cut):
            parts = [
                x.reshape(x.shape[:-2] + (-1, height, x.shape[-1]))[..., cut, :]
                for x in [own] + [far[s] for s in sides]
            ]
            return jnp.concatenate(parts, axis=-3)

        hi = downward(rows(slice(0, height // 2)), "gy", bands)
        lo = upward(rows(slice(height // 2, height)), "gy", bands)
        return hi, lo

    hi_est, lo_est = y_halo(own_est, far_est)
    table = call(
        functools.partial(band_kernel, area),
        shape(6, 3 * TILE, TILE),
        [vmem] * 4,
        (vmem,),
        *heard,
    )
    numbers = jnp.stack([x[area + 1 : area + 4, :10] for x in heard]).astype(F32)
    exacts = numbers[:, 0] + numbers[:, 1] + numbers[:, 2]
    taps_all = exacts[:, :9]
    nums = jnp.concatenate([taps_all.reshape(-1), exacts[:, 9]])

    def relative(x):
        a = jnp.where(view % 2 == 1, jnp.stack([x[1], x[0], x[3], x[2]]), x)
        return jnp.where(view // 2 == 1, jnp.concatenate([a[2:], a[:2]]), a)

    index_own = late[4]
    if frame.mirrored:
        index_own = jnp.where(lax.axis_index("gz") == 1, index_own[:, ::-1], index_own)
    index_far = exchange_z(frame, lambda s: index_own[:, s.start : s.stop], slabs, depth)

    def frame_index(f):
        where, k = frame.source(f)
        return (index_own if where == "own" else index_far[where])[:, k]

    indices = jnp.stack([frame_index(f) for f in range(size)], axis=1)
    levels = jnp.arange(bleach_table.shape[1])
    matches = indices[:, :, None] == levels[None, None, :]
    weight = jnp.sum(jnp.where(matches, bleach_table[:, None, :], F32(0.0)), axis=-1)
    share = relative(weight / jnp.sum(weight, axis=0))
    weighted = (share[:, :, None] * taps_all[:, ::-1][:, None, :]).reshape(-1)

    near = swap(plain, "view", 4, 1)
    opposite = swap(turned, "view", 4, 2)
    last = swap(opposite, "view", 4, 1)

    def halos(pair):
        own = jnp.stack(pair)
        far = exchange_z(
            frame, lambda s: own[:, :, s.start * height : s.stop * height], slabs, 3
        )
        hi, lo = y_halo(own, far)
        return [far[s] for s in sides], hi, lo

    far_a, hi_a, lo_a = halos((plain, near))
    far_b, hi_b, lo_b = halos((opposite, last))

    est_frame = call(
        functools.partial(frame_kernel, frame, tiles, sides),
        shape(tiles + 2, size * 16, TILE),
        [vmem] * (6 + len(sides)),
        (vmem,),
        *heard,
        *[far_est[s] for s in sides],
        hi_est,
        lo_est,
    )
    n3, n2, n1 = (len(frame.need(r)) * 16 for r in (3, 2, 1))

    def forward(views, nums):
        return call(
            functools.partial(forward_kernel, frame, tiles, views),
            shape(2, tiles, n3, TILE),
            (smem, vmem, vmem),
            (vmem,),
            nums,
            table,
            est_frame,
            scratch=[vmem((tiles, size * 16, TILE), BF)],
        )

    recip_a = forward((0, 1), *after(plain[0, 0, 0], nums))
    recip_b = forward((2, 3), *after(recip_a[0, 0, 0, 0], nums))
    return call(
        functools.partial(main_kernel, frame, tiles, sides),
        shape(*estimate.shape, dtype=F32),
        [smem, smem] + [vmem] * (13 + 2 * len(sides)),
        (vmem,),
        nums,
        weighted,
        estimate,
        plain,
        near,
        opposite,
        last,
        *far_a,
        *far_b,
        hi_a,
        hi_b,
        lo_a,
        lo_b,
        recip_a,
        recip_b,
        table,
        est_frame,
        scratch=[
            vmem((tiles + 2, n3, TILE), BF),
            vmem((tiles + 2, n2, TILE), BF),
            vmem((tiles + 2, n1, TILE), BF),
        ]
        + [vmem((tiles, n3, TILE), BF)] * 4
        + [vmem((tiles, area, TILE), F32)],
    )


def solution(mesh):
    placed = (
        P("view", ("gz", "gy"), None, None),
        P("view", ("gz", "gy"), None),
        P("view", ("gz", "gy")),
        P("gz", "gy", "view"),
        P("view", None),
        P("view", None, None),
        P("view"),
        P(),
        P(None, "gz"),
    )
    return jax.shard_map(
        shards, mesh=mesh, in_specs=placed, out_specs=P("gz", "gy", "view"), check_vma=False
    )
```

```python
import functools

import jax
import jax.numpy as jnp
from jax import lax
from jax.experimental import pallas as pl
from jax.experimental.pallas import tpu as pltpu
from jax.sharding import PartitionSpec as P

BF = jnp.bfloat16
F32 = jnp.float32
TILE = 256
LIMIT = 56 << 20


def whole(*spaces):
    return [pl.BlockSpec(memory_space=space) for space in spaces]


def swap(array, axis, size, mask):
    return lax.ppermute(array, axis, [(i, i ^ mask) for i in range(size)])


def core_side(own, bands):
    first = swap(own[0], "gy", bands, 1)
    return first, swap(own[1], "gy", bands, 3)


def upward(array, axis, size):
    return lax.ppermute(array, axis, [(i, i + 1) for i in range(size - 1)])


def downward(array, axis, size):
    return lax.ppermute(array, axis, [(i + 1, i) for i in range(size - 1)])


class Frame:
    def __init__(self, slabs, depth):
        self.mirrored = slabs == 2
        self.depth = depth
        self.own = 0 if self.mirrored else depth
        self.size = 2 * depth if self.mirrored else 3 * depth

    def need(self, radius):
        return range(
            max(0, self.own - radius), min(self.size, self.own + self.depth + radius)
        )

    def source(self, f):
        k = f - self.own
        if 0 <= k < self.depth:
            return "own", k
        if self.mirrored:
            return "up", 2 * self.depth - 1 - k
        return ("dn", f) if k < 0 else ("up", k - self.depth)

    def place(self, f, radius):
        where, k = self.source(f)
        at = 0
        for name, slices in [("own", range(self.depth))] + list(self.sent(radius).items()):
            if name == where:
                return at + k - slices.start
            at += len(slices)

    def sent(self, radius):
        if self.mirrored:
            return {"up": range(self.depth - radius, self.depth)}
        return {
            "dn": range(self.depth - radius, self.depth),
            "up": range(0, radius),
        }


def exchange_z(frame, make, slabs, radius):
    got = {}
    for side, slices in frame.sent(radius).items():
        payload = make(slices)
        if frame.mirrored:
            got[side] = swap(payload, "gz", slabs, 1)
        elif side == "dn":
            got[side] = upward(payload, "gz", slabs)
        else:
            got[side] = downward(payload, "gz", slabs)
    return got


def place():
    return lax.axis_index("view"), lax.axis_index("gz")


def cells_kernel(pairs, bands, mirrored, owner_ref, row_ref, pieces_ref, even_ref, odd_ref, acc):
    count = pieces_ref.shape[0]
    depth = even_ref.shape[1]
    me = lax.axis_index("gz") * bands + lax.axis_index("gy")

    def clear(i, carry):
        acc[i] = jnp.zeros(acc.shape[1:], F32)
        return carry

    lax.fori_loop(0, acc.shape[0], clear, 0)

    def add(i, carry):
        owner = owner_ref[0, i, 0]
        row = row_ref[0, i]
        if mirrored:
            row = jnp.where(owner >= bands, depth - 1 - row, row)
        c = (owner ^ me) * depth + row
        acc[c] = acc[c] + pieces_ref[i].astype(F32)
        return carry

    lax.fori_loop(0, count, add, 0)

    def put(pair, carry):
        for f in range(depth):
            even_ref[pair, f] = acc[pair * 2 * depth + f].astype(BF)
            odd_ref[pair, f] = acc[(pair * 2 + 1) * depth + f].astype(BF)
        return carry

    lax.fori_loop(0, pairs, put, 0)


def payload_kernel(mirrored, bg_ref, taps_ref, est_ref, psf_ref, _, out_ref, tail):
    depth, height = est_ref.shape[:2]
    upside = lax.axis_index("gz") if mirrored else 0
    for k in range(depth):
        out_ref[k * height : (k + 1) * height, :] = est_ref[
            k + upside * (depth - 1 - 2 * k)
        ].astype(BF)
    tail[...] = jnp.zeros(tail.shape, F32)
    for i in range(3):
        tail[0:1, 3 * i : 3 * i + 3] = taps_ref[0, pl.ds(i + upside * (2 - 2 * i), 1), :]
    lanes = lax.broadcasted_iota(jnp.int32, (1, 128), 1)
    exact = jnp.where(lanes == 9, bg_ref[0], tail[0:1, :128])
    for n in range(3):
        part = exact.astype(BF).astype(F32)
        tail[n + 1 : n + 2, :128] = part
        exact = exact - part
    tail[0:1, : psf_ref.shape[1]] = psf_ref[...]
    out_ref[depth * height :, :] = tail[...].astype(BF)


def stack_kernel(rows, *refs):
    ins, out_ref = refs[:-2], refs[-1]
    for v, ref in enumerate(ins):
        out_ref[v] = ref[..., rows, :]


def edges_kernel(height, depth, groups, *refs):
    out1, out2 = refs[-2:]
    views, fars = refs[: groups[0]], refs[groups[0] : groups[0] + groups[1]]
    half = height // 2
    gy = lax.axis_index("gy")
    even = gy % 2 == 0
    inner = (gy == 1) | (gy == 2)
    lead = out1.shape[1:-3]

    def put(at, block):
        turned = pltpu.roll(block, half, block.ndim - 2)
        one = jnp.where(even, turned, block)
        two = jnp.where(inner, jnp.where(even, block, turned), 0.0)
        out1[at] = one[..., :half, :].astype(BF)
        out2[at] = two[..., :half, :].astype(BF)

    for v, own in enumerate(views):
        n = 0
        for number, source in [(depth, own)] + [
            (far.shape[-2] // height, far.at[v]) for far in fars
        ]:
            for k in range(number):
                rows = slice(k * height, (k + 1) * height)
                if lead:
                    for t in range(lead[0]):
                        put((v, t, n), source[t, rows, :].astype(F32))
                else:
                    put((v, n), source[rows, :].astype(F32))
                n += 1


def beside(even, one, two):
    one, two = one.astype(F32), two.astype(F32)
    return jnp.where(
        even, jnp.concatenate([one, two], axis=0), jnp.concatenate([two, one], axis=0)
    )


def reversal():
    rows = lax.broadcasted_iota(jnp.int32, (TILE, TILE), 0)
    cols = lax.broadcasted_iota(jnp.int32, (TILE, TILE), 1)
    return jnp.where(rows + cols == TILE - 1, F32(1.0), F32(0.0)).astype(BF)


def total_kernel(parts, *refs):
    ins, (out_ref, rev_ref) = refs[:parts], refs[parts + 1 :]
    tiles, rows, _ = out_ref.shape
    for t in range(tiles):
        cut = slice(t * TILE, (t + 1) * TILE)
        acc = ins[0][:, :, cut].astype(F32)
        for ref in ins[1:]:
            acc = acc + ref[:, :, cut].astype(F32)
        out_ref[t] = acc.reshape(rows, TILE).astype(BF)
    back = jnp.dot(
        out_ref[...].reshape(tiles * rows, TILE), reversal(), preferred_element_type=F32
    ).astype(BF)
    for t in range(tiles):
        rev_ref[tiles - 1 - t] = back[t * rows : (t + 1) * rows]


def band_kernel(at, *refs):
    heard, out_ref = refs[:4], refs[5]
    flip = reversal()
    for v in range(4):
        row = heard[v][at : at + 8, : 3 * 128].astype(F32)[0:1]
        edge = TILE // 2
        base = jnp.concatenate(
            [jnp.zeros((1, edge), F32), row, jnp.zeros((1, 2 * edge), F32)], axis=1
        )
        wide = pltpu.roll(
            jnp.broadcast_to(base, (TILE, 3 * TILE)), 0, 1, stride=1, stride_axis=0
        ).astype(BF)
        turned = jnp.dot(flip, wide, preferred_element_type=F32).astype(BF)
        for k in range(3):
            cut = slice(k * TILE, (k + 1) * TILE)
            to = slice((2 - k) * TILE, (3 - k) * TILE)
            if v >= 2:
                out_ref[2 + v, cut, :] = turned[:, cut]
            else:
                out_ref[2 + v, to, :] = wide[:, cut]
                out_ref[v, cut, :] = jnp.dot(
                    turned[:, cut], flip, preferred_element_type=F32
                ).astype(BF)


def forward_block(v):
    return v if v < 2 else v + 2


def backward_block(v):
    return v + 2


def conv(src, first, tiles, rows, blocks, dst, step):
    s = 0
    while s < tiles:
        n = min(step, tiles - s)
        lhs = jnp.concatenate(
            [
                src[pl.ds(first + s + k, n)].reshape(n * rows, TILE)
                for k in range(3)
            ],
            axis=1,
        )
        out = jnp.dot(lhs, blocks, preferred_element_type=F32).astype(BF)
        dst[s : s + n] = out.reshape(n, rows, TILE)
        s += n


def taps_sum(slices, zs, taps):
    result = {}
    for z in zs:
        sums = [None, None, None]
        for j in range(3):
            for i in range(3):
                at = z + i - 1
                if at in slices:
                    term = taps(z, i, j) * slices[at]
                    sums[j] = term if sums[j] is None else sums[j] + term
        result[z] = sums
    return result


def along_y(sums):
    n = sums[0].shape[0]
    return pltpu.roll(sums[0], 1, 0) + sums[1] + pltpu.roll(sums[2], n - 1, 0)


def frame_kernel(frame, tiles, sides, *refs):
    own_refs, refs = refs[:4], refs[4:]
    side_refs = dict(zip(sides, refs[: len(sides)]))
    one_ref, two_ref, _, out_ref = refs[len(sides) :]
    view = lax.axis_index("view")
    even = lax.axis_index("gy") % 2 == 0
    for e in (0, tiles + 1):
        out_ref[e] = jnp.zeros(out_ref.shape[1:], BF)
    for v in range(4):
        for s in range(tiles // 4):
            t = (view ^ v) * (tiles // 4) + s + 1
            cut = slice(s * TILE, (s + 1) * TILE)
            for f in range(frame.size):
                where, k = frame.source(f)
                rows = slice(k * 8, (k + 1) * 8)
                if where == "own":
                    own = own_refs[v][rows, cut]
                else:
                    own = side_refs[where][v, rows, cut]
                n = frame.place(f, frame.depth)
                out_ref[t, f * 16 : (f + 1) * 16, :] = jnp.concatenate(
                    [
                        own.astype(F32),
                        beside(even, one_ref[v, n, :, cut], two_ref[v, n, :, cut]),
                    ],
                    axis=0,
                ).astype(BF)


def forward_kernel(frame, tiles, views, num_ref, blocks_ref, frame_ref, _, recip_ref, c):
    size = frame.size
    zs = frame.need(3)
    for at, v in enumerate(views):
        conv(frame_ref, 0, tiles, size * 16, blocks_ref[forward_block(v)], c, 2)

        def divide(t, carry, v=v, at=at):
            from_t = t if v < 2 else tiles - 1 - t
            for h in range(TILE // 128):
                cut = slice(h * 128, (h + 1) * 128)
                slices = {
                    f: c[from_t, f * 16 : (f + 1) * 16, cut].astype(F32)
                    for f in range(size)
                }
                sums = taps_sum(slices, zs, lambda z, i, j: num_ref[v * 9 + i * 3 + j])
                for n, z in enumerate(zs):
                    recip_ref[at, t, n * 16 : (n + 1) * 16, cut] = (
                        1.0 / (along_y(sums[z]) + num_ref[36 + v])
                    ).astype(BF)
            return carry

        lax.fori_loop(0, tiles, divide, 0)


def main_kernel(frame, tiles, sides, num_ref, wt_ref, est_ref, *refs):
    own_refs, refs = refs[:4], refs[4:]
    count = len(sides)
    far_refs, refs = refs[: 2 * count], refs[2 * count :]
    one_refs, two_refs = refs[0:2], refs[2:4]
    even = lax.axis_index("gy") % 2 == 0
    recip_refs = refs[4:6]
    blocks_ref, frame_ref, out_ref = refs[6:9]
    m1, u2, m2, c0, c1, c2, c3, kept = refs[9:]
    c = [c0, c1, c2, c3]
    view = lax.axis_index("view")
    upside = lax.axis_index("gz") if frame.mirrored else 0
    depth = frame.depth
    z3, z2, z1, z0 = (frame.need(r) for r in (3, 2, 1, 0))
    sent = frame.sent(3)

    def measured(v, t, z, cut):
        where, k = frame.source(z)
        pair, w = v // 2, v % 2
        if where == "own":
            own = own_refs[v][t, k * 8 : (k + 1) * 8, cut]
        else:
            k = k - sent[where].start
            far = far_refs[pair * count + sides.index(where)]
            own = far[w, t, k * 8 : (k + 1) * 8, cut]
        n = frame.place(z, 3)
        return jnp.concatenate(
            [
                own.astype(F32),
                beside(
                    even,
                    one_refs[pair][w, t, n, :, cut],
                    two_refs[pair][w, t, n, :, cut],
                ),
            ],
            axis=0,
        )

    def mix(v, t, z, cut, recip_a, recip_b):
        a = (measured(v, t, z, cut) * recip_a).astype(BF).astype(F32)
        b = (measured(v + 2, t, z, cut) * recip_b).astype(BF).astype(F32)
        return (0.5 * (a + b)).astype(BF)

    def zero_ends(ref):
        for e in (0, ref.shape[0] - 1):
            ref[e] = jnp.zeros(ref.shape[1:], BF)

    for ref in (m1, u2, m2):
        zero_ends(ref)

    for v in range(2):

        def ratios(t, carry, v=v):
            for h in range(TILE // 128):
                cut = slice(h * 128, (h + 1) * 128)
                for n, z in enumerate(z3):
                    at = slice(n * 16, (n + 1) * 16)
                    m1[t + 1, at, cut] = mix(
                        v,
                        t,
                        z,
                        cut,
                        recip_refs[0][v, t, at, cut].astype(F32),
                        recip_refs[1][v, t, at, cut].astype(F32),
                    )
            return carry

        lax.fori_loop(0, tiles, ratios, 0)
        for w in (v, v + 2):
            conv(m1, 0, tiles, m1.shape[1], blocks_ref[backward_block(w)], c[w], 2)

    def numerator(slices_of, zs):
        totals = {z: [None, None, None] for z in zs}
        for v in range(4):
            slices = slices_of(v)
            sums = taps_sum(
                slices,
                zs,
                lambda z, i, j, v=v: wt_ref[(v * frame.size + z) * 9 + i * 3 + j],
            )
            for z in zs:
                for j in range(3):
                    old = totals[z][j]
                    totals[z][j] = sums[z][j] if old is None else old + sums[z][j]
        return totals

    def update(t, carry):
        for h in range(TILE // 128):
            cut = slice(h * 128, (h + 1) * 128)

            def slices_of(v):
                from_t = t if v < 2 else tiles - 1 - t
                return {
                    z: c[v][from_t, n * 16 : (n + 1) * 16, cut].astype(F32)
                    for n, z in enumerate(z3)
                }

            totals = numerator(slices_of, z2)
            for n, z in enumerate(z2):
                change = along_y(totals[z])
                before = frame_ref[t + 1, z * 16 : (z + 1) * 16, cut].astype(F32)
                u2[t + 1, n * 16 : (n + 1) * 16, cut] = (before * change).astype(BF)
                if z in z0:
                    k = z - frame.own
                    kept[t, k * 8 : (k + 1) * 8, cut] = change[:8]
        return carry

    lax.fori_loop(0, tiles, update, 0)

    rows1 = m2.shape[1]
    n2 = u2.shape[1]
    for v in range(2):
        for w in (v, v + 2):
            conv(u2, 0, tiles, n2, blocks_ref[forward_block(w)], c[w].at[:, :n2, :], 2)

        def ratios2(t, carry, v=v):
            for h in range(TILE // 128):
                cut = slice(h * 128, (h + 1) * 128)
                recips = []
                for w in (v, v + 2):
                    from_t = t if w < 2 else tiles - 1 - t
                    slices = {
                        z: c[w][from_t, n * 16 : (n + 1) * 16, cut].astype(F32)
                        for n, z in enumerate(z2)
                    }
                    sums = taps_sum(
                        slices, z1, lambda z, i, j, w=w: num_ref[w * 9 + i * 3 + j]
                    )
                    recips.append(
                        {z: 1.0 / (along_y(sums[z]) + num_ref[36 + w]) for z in z1}
                    )
                for n, z in enumerate(z1):
                    m2[t + 1, n * 16 : (n + 1) * 16, cut] = mix(
                        v, t, z, cut, recips[0][z], recips[1][z]
                    )
            return carry

        lax.fori_loop(0, tiles, ratios2, 0)
        mine = tiles // 4
        for w in (v, v + 2):
            first = view * mine if w < 2 else tiles - (view + 1) * mine
            conv(m2, first, mine, rows1, blocks_ref[backward_block(w)], c[w].at[:, :rows1, :], 2)

    mine = tiles // 4
    for s in range(mine):
        for h in range(TILE // 128):
            cut = slice(h * 128, (h + 1) * 128)

            def slices_of(v):
                from_s = s if v < 2 else mine - 1 - s
                return {
                    z: c[v][from_s, n * 16 : (n + 1) * 16, cut].astype(F32)
                    for n, z in enumerate(z1)
                }

            totals = numerator(slices_of, z0)
            for z in z0:
                k = z - frame.own
                to = k + upside * (depth - 1 - 2 * k)
                lanes = slice(s * TILE + h * 128, s * TILE + (h + 1) * 128)
                first_change = kept[view * mine + s, k * 8 : (k + 1) * 8, cut]
                out_ref[to, :, lanes] = (
                    est_ref[to, :, lanes] * first_change * along_y(totals[z])[:8]
                )


def shards(
    pieces, piece_owner, piece_row, estimate, psf_x, stencil, background, bleach_table, bleach_index
):
    depth, height, chunk = estimate.shape
    width = pieces.shape[3]
    tiles = width // TILE
    slabs = lax.axis_size("gz")
    bands = lax.axis_size("gy")
    blocks = slabs * bands
    frame = Frame(slabs, depth)
    size = frame.size
    sides = tuple(frame.sent(1))
    view = lax.axis_index("view")
    vmem, smem = pltpu.VMEM, pltpu.SMEM
    params = pltpu.CompilerParams(vmem_limit_bytes=LIMIT)

    def call(kernel, shapes, ins, outs, *args, scratch=()):
        return pl.pallas_call(
            kernel,
            out_shape=shapes,
            in_specs=whole(*ins),
            out_specs=whole(*outs) if isinstance(shapes, tuple) else whole(*outs)[0],
            scratch_shapes=list(scratch),
            compiler_params=params,
        )(*args)

    def shape(*dims, dtype=BF):
        return jax.ShapeDtypeStruct(dims, dtype)

    pairs = blocks // 2
    half_cells = shape(pairs, depth, height, width)
    even, odd = call(
        functools.partial(cells_kernel, pairs, bands, frame.mirrored),
        (half_cells, half_cells),
        (smem, smem, vmem),
        (vmem, vmem),
        piece_owner,
        piece_row,
        pieces[0],
        scratch=[vmem((blocks * depth, height, width), F32)],
    )
    other = swap(odd, "gy", bands, 1)

    free = pl.ANY

    area = depth * height
    payload = call(
        functools.partial(payload_kernel, frame.mirrored),
        shape(area + 8, chunk),
        (smem, vmem, vmem, vmem, free),
        (vmem,),
        background,
        stencil,
        estimate,
        psf_x,
        even,
        scratch=[vmem((8, chunk), F32)],
    )
    heard = [payload] + [swap(payload, "view", 4, mask) for mask in (1, 2, 3)]

    kept = [even[k] + other[k] for k in range(pairs)]
    moved = [swap(kept[k], ("gz", "gy"), blocks, 2 * k) for k in range(1, pairs)]

    def stack(arrays, slices, token):
        rows = slice(slices.start * height, slices.stop * height)
        dims = (len(arrays),) + arrays[0].shape[:-2] + (len(slices) * height, arrays[0].shape[-1])
        return call(
            functools.partial(stack_kernel, rows),
            shape(*dims),
            [vmem] * len(arrays) + [free],
            (vmem,),
            *arrays,
            token,
        )

    def edges(arrays, far, token, count):
        dims = (len(arrays),) + arrays[0].shape[:-2] + (count, height // 2, arrays[0].shape[-1])
        fars = [far[s] for s in sides]
        return call(
            functools.partial(edges_kernel, height, depth, (len(arrays), len(fars))),
            (shape(*dims), shape(*dims)),
            [vmem] * (len(arrays) + len(fars)) + [free],
            (vmem, vmem),
            *arrays,
            *fars,
            token,
        )

    far_est = exchange_z(frame, lambda s: stack(heard, s, kept[1]), slabs, depth)
    table = call(
        functools.partial(band_kernel, area),
        shape(6, 3 * TILE, TILE),
        [vmem] * 4 + [free],
        (vmem,),
        *heard,
        kept[1],
    )
    est_edges = edges(heard, far_est, table, size)
    one_est, two_est = core_side(est_edges, bands)

    plain, turned = call(
        functools.partial(total_kernel, pairs),
        (shape(tiles, area, TILE), shape(tiles, area, TILE)),
        [vmem] * pairs + [free],
        (vmem, vmem),
        kept[0],
        *moved,
        est_edges[0],
    )

    numbers = jnp.stack([x[area + 1 : area + 4, :10] for x in heard]).astype(F32)
    exacts = numbers[:, 0] + numbers[:, 1] + numbers[:, 2]
    taps_all = exacts[:, :9]
    nums = jnp.concatenate([taps_all.reshape(-1), exacts[:, 9]])

    def relative(x):
        a = jnp.where(view % 2 == 1, jnp.stack([x[1], x[0], x[3], x[2]]), x)
        return jnp.where(view // 2 == 1, jnp.concatenate([a[2:], a[:2]]), a)

    index_own = bleach_index
    if frame.mirrored:
        index_own = jnp.where(lax.axis_index("gz") == 1, index_own[:, ::-1], index_own)
    index_far = exchange_z(frame, lambda s: index_own[:, s.start : s.stop], slabs, depth)

    def frame_index(f):
        where, k = frame.source(f)
        return (index_own if where == "own" else index_far[where])[:, k]

    indices = jnp.stack([frame_index(f) for f in range(size)], axis=1)
    levels = jnp.arange(bleach_table.shape[1])
    matches = indices[:, :, None] == levels[None, None, :]
    weight = jnp.sum(jnp.where(matches, bleach_table[:, None, :], F32(0.0)), axis=-1)
    share = relative(weight / jnp.sum(weight, axis=0))
    weighted = (share[:, :, None] * taps_all[:, ::-1][:, None, :]).reshape(-1)

    near = swap(plain, "view", 4, 1)
    opposite = swap(turned, "view", 4, 2)
    last = swap(opposite, "view", 4, 1)

    n3, n2, n1 = (len(frame.need(r)) * 16 for r in (3, 2, 1))

    est_frame = call(
        functools.partial(frame_kernel, frame, tiles, sides),
        shape(tiles + 2, size * 16, TILE),
        [vmem] * (6 + len(sides)) + [free],
        (vmem,),
        *heard,
        *[far_est[s] for s in sides],
        one_est,
        two_est,
        plain,
    )

    def far_rows(pair, token):
        tokens = []

        def make(slices):
            tokens.append(stack(pair, slices, token))
            return tokens[-1]

        return exchange_z(frame, make, slabs, 3), tokens[-1]

    def forward(views, token):
        return call(
            functools.partial(forward_kernel, frame, tiles, views),
            shape(2, tiles, n3, TILE),
            (smem, vmem, vmem, free),
            (vmem,),
            nums,
            table,
            est_frame,
            token,
            scratch=[vmem((tiles, size * 16, TILE), BF)],
        )

    count3 = len(frame.need(3))
    far_a, token = far_rows((plain, near), est_frame)
    recip_a = forward((0, 1), token)
    far_b, token = far_rows((opposite, last), recip_a)
    edges_a = edges((plain, near), far_a, token, count3)
    one_a, two_a = core_side(edges_a, bands)
    edges_b = edges((opposite, last), far_b, edges_a[0], count3)
    one_b, two_b = core_side(edges_b, bands)
    recip_b = forward((2, 3), edges_b[0])
    return call(
        functools.partial(main_kernel, frame, tiles, sides),
        shape(*estimate.shape, dtype=F32),
        [smem, smem] + [vmem] * (13 + 2 * len(sides)),
        (vmem,),
        nums,
        weighted,
        estimate,
        plain,
        near,
        opposite,
        last,
        *[far_a[s] for s in sides],
        *[far_b[s] for s in sides],
        one_a,
        one_b,
        two_a,
        two_b,
        recip_a,
        recip_b,
        table,
        est_frame,
        scratch=[
            vmem((tiles + 2, n3, TILE), BF),
            vmem((tiles + 2, n2, TILE), BF),
            vmem((tiles + 2, n1, TILE), BF),
        ]
        + [vmem((tiles, n3, TILE), BF)] * 4
        + [vmem((tiles, area, TILE), F32)],
    )


def solution(mesh):
    placed = (
        P("view", ("gz", "gy"), None, None),
        P("view", ("gz", "gy"), None),
        P("view", ("gz", "gy")),
        P("gz", "gy", "view"),
        P("view", None),
        P("view", None, None),
        P("view"),
        P(),
        P(None, "gz"),
    )
    return jax.shard_map(
        shards, mesh=mesh, in_specs=placed, out_specs=P("gz", "gy", "view"), check_vma=False
    )
```

```python
import functools

import jax
import jax.numpy as jnp
from jax import lax
from jax.experimental import pallas as pl
from jax.experimental.pallas import tpu as pltpu
from jax.sharding import PartitionSpec as P

BF = jnp.bfloat16
F32 = jnp.float32
TILE = 256
LIMIT = 56 << 20


def whole(*spaces):
    return [pl.BlockSpec(memory_space=space) for space in spaces]


def swap(array, axis, size, mask):
    return lax.ppermute(array, axis, [(i, i ^ mask) for i in range(size)])


def core_side(own, bands, all_take_part):
    first = swap(own[0], "gy", bands, 1)
    if all_take_part:
        return first, swap(own[1], "gy", bands, 3)
    return first, lax.ppermute(own[1], "gy", [(1, 2), (2, 1)])


def upward(array, axis, size):
    return lax.ppermute(array, axis, [(i, i + 1) for i in range(size - 1)])


def downward(array, axis, size):
    return lax.ppermute(array, axis, [(i + 1, i) for i in range(size - 1)])


class Frame:
    def __init__(self, slabs, depth):
        self.mirrored = slabs == 2
        self.depth = depth
        self.own = 0 if self.mirrored else depth
        self.size = 2 * depth if self.mirrored else 3 * depth

    def need(self, radius):
        return range(
            max(0, self.own - radius), min(self.size, self.own + self.depth + radius)
        )

    def source(self, f):
        k = f - self.own
        if 0 <= k < self.depth:
            return "own", k
        if self.mirrored:
            return "up", 2 * self.depth - 1 - k
        return ("dn", f) if k < 0 else ("up", k - self.depth)

    def place(self, f, radius):
        where, k = self.source(f)
        at = 0
        for name, slices in [("own", range(self.depth))] + list(self.sent(radius).items()):
            if name == where:
                return at + k - slices.start
            at += len(slices)

    def sent(self, radius):
        if self.mirrored:
            return {"up": range(self.depth - radius, self.depth)}
        return {
            "dn": range(self.depth - radius, self.depth),
            "up": range(0, radius),
        }


def exchange_z(frame, make, slabs, radius):
    got = {}
    for side, slices in frame.sent(radius).items():
        payload = make(slices)
        if frame.mirrored:
            got[side] = swap(payload, "gz", slabs, 1)
        elif side == "dn":
            got[side] = upward(payload, "gz", slabs)
        else:
            got[side] = downward(payload, "gz", slabs)
    return got


def place():
    return lax.axis_index("view"), lax.axis_index("gz")


def cells_kernel(pairs, bands, mirrored, owner_ref, row_ref, pieces_ref, even_ref, odd_ref, acc):
    count = pieces_ref.shape[0]
    depth = even_ref.shape[1]
    me = lax.axis_index("gz") * bands + lax.axis_index("gy")

    def clear(i, carry):
        acc[i] = jnp.zeros(acc.shape[1:], F32)
        return carry

    lax.fori_loop(0, acc.shape[0], clear, 0)

    def add(i, carry):
        owner = owner_ref[0, i, 0]
        row = row_ref[0, i]
        if mirrored:
            row = jnp.where(owner >= bands, depth - 1 - row, row)
        c = (owner ^ me) * depth + row
        acc[c] = acc[c] + pieces_ref[i].astype(F32)
        return carry

    lax.fori_loop(0, count, add, 0)

    def put(pair, carry):
        for f in range(depth):
            even_ref[pair, f] = acc[pair * 2 * depth + f].astype(BF)
            odd_ref[pair, f] = acc[(pair * 2 + 1) * depth + f].astype(BF)
        return carry

    lax.fori_loop(0, pairs, put, 0)


def payload_kernel(mirrored, bg_ref, taps_ref, est_ref, psf_ref, _, out_ref, tail):
    depth, height = est_ref.shape[:2]
    upside = lax.axis_index("gz") if mirrored else 0
    for k in range(depth):
        out_ref[k * height : (k + 1) * height, :] = est_ref[
            k + upside * (depth - 1 - 2 * k)
        ].astype(BF)
    tail[...] = jnp.zeros(tail.shape, F32)
    for i in range(3):
        tail[0:1, 3 * i : 3 * i + 3] = taps_ref[0, pl.ds(i + upside * (2 - 2 * i), 1), :]
    lanes = lax.broadcasted_iota(jnp.int32, (1, 128), 1)
    exact = jnp.where(lanes == 9, bg_ref[0], tail[0:1, :128])
    for n in range(3):
        part = exact.astype(BF).astype(F32)
        tail[n + 1 : n + 2, :128] = part
        exact = exact - part
    tail[0:1, : psf_ref.shape[1]] = psf_ref[...]
    out_ref[depth * height :, :] = tail[...].astype(BF)


def numbers_of(heard, at):
    rows = heard[at : at + 8, :128].astype(F32)
    exact = rows[1:2] + rows[2:3] + rows[3:4]
    wide = jnp.broadcast_to(exact, (16, 128))
    spot = lax.broadcasted_iota(jnp.int32, (16, 128), 0) == lax.broadcasted_iota(
        jnp.int32, (16, 128), 1
    )
    column = jnp.sum(jnp.where(spot, wide, 0.0), axis=1, keepdims=True)
    return jnp.broadcast_to(column, (16, 128))


def stack_kernel(rows, *refs):
    ins, out_ref = refs[:-2], refs[-1]
    for v, ref in enumerate(ins):
        out_ref[v] = ref[..., rows, :]


def edges_kernel(height, depth, sides, *refs):
    out1, out2 = refs[-2:]
    count = out1.shape[0]
    views, fars = refs[:count], refs[count:-3]
    half = height // 2
    gy = lax.axis_index("gy")
    even = gy % 2 == 0
    inner = (gy == 1) | (gy == 2)
    lead = out1.shape[1:-3]

    def put(at, block):
        turned = pltpu.roll(block, half, block.ndim - 2)
        one = jnp.where(even, turned, block)
        two = jnp.where(inner, jnp.where(even, block, turned), 0.0)
        out1[at] = one[..., :half, :].astype(BF)
        out2[at] = two[..., :half, :].astype(BF)

    def far_of(v, side):
        for ref in fars[side::sides]:
            if v < ref.shape[0]:
                return ref.at[v]
            v -= ref.shape[0]

    for v, own in enumerate(views):
        n = 0
        for number, source in [(depth, own)] + [
            (fars[side].shape[-2] // height, far_of(v, side)) for side in range(sides)
        ]:
            for k in range(number):
                rows = slice(k * height, (k + 1) * height)
                if lead:

                    def one_tile(t, carry, v=v, n=n, source=source, rows=rows):
                        put((v, t, n), source[t, rows, :].astype(F32))
                        return carry

                    lax.fori_loop(0, lead[0], one_tile, 0, unroll=True)
                else:
                    put((v, n), source[rows, :].astype(F32))
                n += 1


def beside(even, one, two):
    one, two = one.astype(F32), two.astype(F32)
    return jnp.where(
        even, jnp.concatenate([one, two], axis=0), jnp.concatenate([two, one], axis=0)
    )


def reversal():
    rows = lax.broadcasted_iota(jnp.int32, (TILE, TILE), 0)
    cols = lax.broadcasted_iota(jnp.int32, (TILE, TILE), 1)
    return jnp.where(rows + cols == TILE - 1, F32(1.0), F32(0.0)).astype(BF)


def total_kernel(parts, far_rows, *refs):
    ins, (out_ref, rev_ref, *far_refs) = refs[:parts], refs[parts + 1 :]
    tiles, rows, _ = out_ref.shape
    for t in range(tiles):
        cut = slice(t * TILE, (t + 1) * TILE)
        acc = ins[0][:, :, cut].astype(F32)
        for ref in ins[1:]:
            acc = acc + ref[:, :, cut].astype(F32)
        block = acc.reshape(rows, TILE).astype(BF)
        out_ref[t] = block
        for ref, part in zip(far_refs, far_rows):
            ref[0, t] = block[part]
    back = jnp.dot(
        out_ref[...].reshape(tiles * rows, TILE), reversal(), preferred_element_type=F32
    ).astype(BF)
    for t in range(tiles):
        rev_ref[tiles - 1 - t] = back[t * rows : (t + 1) * rows]


def band_kernel(at, *refs):
    heard, (out_ref, num_ref) = refs[:4], refs[5:]
    for v in range(4):
        num_ref[v * 16 : (v + 1) * 16, :] = numbers_of(heard[v], at)
    flip = reversal()
    for v in range(4):
        row = heard[v][at : at + 8, : 3 * 128].astype(F32)[0:1]
        edge = TILE // 2
        base = jnp.concatenate(
            [jnp.zeros((1, edge), F32), row, jnp.zeros((1, 2 * edge), F32)], axis=1
        )
        wide = pltpu.roll(
            jnp.broadcast_to(base, (TILE, 3 * TILE)), 0, 1, stride=1, stride_axis=0
        ).astype(BF)
        turned = jnp.dot(flip, wide, preferred_element_type=F32).astype(BF)
        for k in range(3):
            cut = slice(k * TILE, (k + 1) * TILE)
            to = slice((2 - k) * TILE, (3 - k) * TILE)
            if v >= 2:
                out_ref[2 + v, cut, :] = turned[:, cut]
            else:
                out_ref[2 + v, to, :] = wide[:, cut]
                out_ref[v, cut, :] = jnp.dot(
                    turned[:, cut], flip, preferred_element_type=F32
                ).astype(BF)


def forward_block(v):
    return v if v < 2 else v + 2


def backward_block(v):
    return v + 2


def conv(src, first, tiles, rows, blocks, dst, step):
    s = 0
    while s < tiles:
        n = min(step, tiles - s)
        lhs = jnp.concatenate(
            [
                src[pl.ds(first + s + k, n)].reshape(n * rows, TILE)
                for k in range(3)
            ],
            axis=1,
        )
        out = jnp.dot(lhs, blocks, preferred_element_type=F32).astype(BF)
        dst[s : s + n] = out.reshape(n, rows, TILE)
        s += n


def taps_sum(slices, zs, taps):
    result = {}
    for z in zs:
        sums = [None, None, None]
        for j in range(3):
            for i in range(3):
                at = z + i - 1
                if at in slices:
                    term = taps(z, i, j) * slices[at]
                    sums[j] = term if sums[j] is None else sums[j] + term
        result[z] = sums
    return result


def along_y(sums):
    n = sums[0].shape[0]
    return pltpu.roll(sums[0], 1, 0) + sums[1] + pltpu.roll(sums[2], n - 1, 0)


def frame_kernel(frame, tiles, sides, *refs):
    own_refs, refs = refs[:4], refs[4:]
    side_refs = dict(zip(sides, refs[: len(sides)]))
    one_ref, two_ref, _, out_ref = refs[len(sides) :]
    view = lax.axis_index("view")
    even = lax.axis_index("gy") % 2 == 0
    for e in (0, tiles + 1):
        out_ref[e] = jnp.zeros(out_ref.shape[1:], BF)
    for v in range(4):
        for s in range(tiles // 4):
            t = (view ^ v) * (tiles // 4) + s + 1
            cut = slice(s * TILE, (s + 1) * TILE)
            for f in range(frame.size):
                where, k = frame.source(f)
                rows = slice(k * 8, (k + 1) * 8)
                if where == "own":
                    own = own_refs[v][rows, cut]
                else:
                    own = side_refs[where][v, rows, cut]
                n = frame.place(f, frame.depth)
                out_ref[t, f * 16 : (f + 1) * 16, :] = jnp.concatenate(
                    [
                        own.astype(F32),
                        beside(even, one_ref[v, n, :, cut], two_ref[v, n, :, cut]),
                    ],
                    axis=0,
                ).astype(BF)


def forward_kernel(frame, tiles, views, num_ref, blocks_ref, frame_ref, _, recip_ref, c):
    size = frame.size
    zs = frame.need(3)
    for at, v in enumerate(views):
        conv(frame_ref, 0, tiles, size * 16, blocks_ref[forward_block(v)], c, 2)

        def divide(t, carry, v=v, at=at):
            from_t = t if v < 2 else tiles - 1 - t
            for h in range(TILE // 128):
                cut = slice(h * 128, (h + 1) * 128)
                slices = {
                    f: c[from_t, f * 16 : (f + 1) * 16, cut].astype(F32)
                    for f in range(size)
                }
                sums = taps_sum(slices, zs, lambda z, i, j: num_ref[v * 16 + i * 3 + j : v * 16 + i * 3 + j + 1, :])
                for n, z in enumerate(zs):
                    recip_ref[at, t, n * 16 : (n + 1) * 16, cut] = (
                        1.0 / (along_y(sums[z]) + num_ref[v * 16 + 9 : v * 16 + 10, :])
                    ).astype(BF)
            return carry

        lax.fori_loop(0, tiles, divide, 0)


def main_kernel(frame, tiles, sides, table_ref, *refs):
    count = len(sides)
    index_refs, refs = refs[: count + 1], refs[count + 1 :]
    num_ref, est_ref, refs = refs[0], refs[1], refs[2:]
    own_refs, refs = refs[:4], refs[4:]
    far_refs, refs = refs[: 2 * count], refs[2 * count :]
    one_ref, two_ref = refs[:2]
    recip_refs = refs[2:4]
    blocks_ref, frame_ref, out_ref = refs[4:7]
    m1, u2, m2, c0, c1, c2, c3, kept, wt = refs[7:]
    even = lax.axis_index("gy") % 2 == 0
    c = [c0, c1, c2, c3]
    view = lax.axis_index("view")
    upside = lax.axis_index("gz") if frame.mirrored else 0
    depth = frame.depth
    z3, z2, z1, z0 = (frame.need(r) for r in (3, 2, 1, 0))
    sent = frame.sent(3)

    for f in z2:
        where, k = frame.source(f)
        index_ref = index_refs[0 if where == "own" else 1 + sides.index(where)]
        over = upside if where == "own" else 1 - upside
        raw = k + over * (depth - 1 - 2 * k) if frame.mirrored else k
        weights = [
            jnp.full((16, 128), table_ref[v, index_ref[v, raw]], F32) for v in range(4)
        ]
        total = (weights[0] + weights[1]) + (weights[2] + weights[3])
        for v in range(4):
            mine = jnp.full(
                (16, 128), table_ref[view ^ v, index_ref[view ^ v, raw]], F32
            )
            at = (v * frame.size + f) * 16
            wt[at : at + 16, :] = num_ref[v * 16 : (v + 1) * 16, :] * (mine / total)

    def weighted(v, z, n):
        at = (v * frame.size + z) * 16 + 8 - n
        return wt[at : at + 1, :]

    def measured(v, t, z, cut):
        where, k = frame.source(z)
        if where == "own":
            own = own_refs[v][t, k * 8 : (k + 1) * 8, cut]
        else:
            k = k - sent[where].start
            far = far_refs[(count if v else 0) + sides.index(where)]
            own = far[v - 1 if v else 0, t, k * 8 : (k + 1) * 8, cut]
        n = frame.place(z, 3)
        return jnp.concatenate(
            [
                own.astype(F32),
                beside(
                    even,
                    one_ref[v, t, n, :, cut],
                    two_ref[v, t, n, :, cut],
                ),
            ],
            axis=0,
        )

    def mix(v, t, z, cut, recip_a, recip_b):
        a = (measured(v, t, z, cut) * recip_a).astype(BF).astype(F32)
        b = (measured(v + 2, t, z, cut) * recip_b).astype(BF).astype(F32)
        return (0.5 * (a + b)).astype(BF)

    def zero_ends(ref):
        for e in (0, ref.shape[0] - 1):
            ref[e] = jnp.zeros(ref.shape[1:], BF)

    for ref in (m1, u2, m2):
        zero_ends(ref)

    for v in range(2):

        def ratios(t, carry, v=v):
            for h in range(TILE // 128):
                cut = slice(h * 128, (h + 1) * 128)
                for n, z in enumerate(z3):
                    at = slice(n * 16, (n + 1) * 16)
                    m1[t + 1, at, cut] = mix(
                        v,
                        t,
                        z,
                        cut,
                        recip_refs[0][v, t, at, cut].astype(F32),
                        recip_refs[1][v, t, at, cut].astype(F32),
                    )
            return carry

        lax.fori_loop(0, tiles, ratios, 0)
        for w in (v, v + 2):
            conv(m1, 0, tiles, m1.shape[1], blocks_ref[backward_block(w)], c[w], 2)

    def numerator(slices_of, zs):
        totals = {z: [None, None, None] for z in zs}
        for v in range(4):
            slices = slices_of(v)
            sums = taps_sum(
                slices,
                zs,
                lambda z, i, j, v=v: weighted(v, z, i * 3 + j),
            )
            for z in zs:
                for j in range(3):
                    old = totals[z][j]
                    totals[z][j] = sums[z][j] if old is None else old + sums[z][j]
        return totals

    def update(t, carry):
        for h in range(TILE // 128):
            cut = slice(h * 128, (h + 1) * 128)

            def slices_of(v):
                from_t = t if v < 2 else tiles - 1 - t
                return {
                    z: c[v][from_t, n * 16 : (n + 1) * 16, cut].astype(F32)
                    for n, z in enumerate(z3)
                }

            totals = numerator(slices_of, z2)
            for n, z in enumerate(z2):
                change = along_y(totals[z])
                before = frame_ref[t + 1, z * 16 : (z + 1) * 16, cut].astype(F32)
                u2[t + 1, n * 16 : (n + 1) * 16, cut] = (before * change).astype(BF)
                if z in z0:
                    k = z - frame.own
                    kept[t, k * 8 : (k + 1) * 8, cut] = change[:8]
        return carry

    lax.fori_loop(0, tiles, update, 0)

    rows1 = m2.shape[1]
    n2 = u2.shape[1]
    for v in range(2):
        for w in (v, v + 2):
            conv(u2, 0, tiles, n2, blocks_ref[forward_block(w)], c[w].at[:, :n2, :], 2)

        def ratios2(t, carry, v=v):
            for h in range(TILE // 128):
                cut = slice(h * 128, (h + 1) * 128)
                recips = []
                for w in (v, v + 2):
                    from_t = t if w < 2 else tiles - 1 - t
                    slices = {
                        z: c[w][from_t, n * 16 : (n + 1) * 16, cut].astype(F32)
                        for n, z in enumerate(z2)
                    }
                    sums = taps_sum(
                        slices, z1, lambda z, i, j, w=w: num_ref[w * 16 + i * 3 + j : w * 16 + i * 3 + j + 1, :]
                    )
                    recips.append(
                        {z: 1.0 / (along_y(sums[z]) + num_ref[w * 16 + 9 : w * 16 + 10, :]) for z in z1}
                    )
                for n, z in enumerate(z1):
                    m2[t + 1, n * 16 : (n + 1) * 16, cut] = mix(
                        v, t, z, cut, recips[0][z], recips[1][z]
                    )
            return carry

        lax.fori_loop(0, tiles, ratios2, 0)
        mine = tiles // 4
        for w in (v, v + 2):
            first = view * mine if w < 2 else tiles - (view + 1) * mine
            conv(m2, first, mine, rows1, blocks_ref[backward_block(w)], c[w].at[:, :rows1, :], 2)

    mine = tiles // 4
    for s in range(mine):
        for h in range(TILE // 128):
            cut = slice(h * 128, (h + 1) * 128)

            def slices_of(v):
                from_s = s if v < 2 else mine - 1 - s
                return {
                    z: c[v][from_s, n * 16 : (n + 1) * 16, cut].astype(F32)
                    for n, z in enumerate(z1)
                }

            totals = numerator(slices_of, z0)
            for z in z0:
                k = z - frame.own
                to = k + upside * (depth - 1 - 2 * k)
                lanes = slice(s * TILE + h * 128, s * TILE + (h + 1) * 128)
                first_change = kept[view * mine + s, k * 8 : (k + 1) * 8, cut]
                out_ref[to, :, lanes] = (
                    est_ref[to, :, lanes] * first_change * along_y(totals[z])[:8]
                )


def shards(
    pieces, piece_owner, piece_row, estimate, psf_x, stencil, background, bleach_table, bleach_index
):
    depth, height, chunk = estimate.shape
    width = pieces.shape[3]
    tiles = width // TILE
    slabs = lax.axis_size("gz")
    bands = lax.axis_size("gy")
    blocks = slabs * bands
    frame = Frame(slabs, depth)
    size = frame.size
    sides = tuple(frame.sent(1))
    vmem, smem = pltpu.VMEM, pltpu.SMEM
    params = pltpu.CompilerParams(vmem_limit_bytes=LIMIT)

    def call(kernel, shapes, ins, outs, *args, scratch=()):
        return pl.pallas_call(
            kernel,
            out_shape=shapes,
            in_specs=whole(*ins),
            out_specs=whole(*outs) if isinstance(shapes, tuple) else whole(*outs)[0],
            scratch_shapes=list(scratch),
            compiler_params=params,
        )(*args)

    def shape(*dims, dtype=BF):
        return jax.ShapeDtypeStruct(dims, dtype)

    pairs = blocks // 2
    half_cells = shape(pairs, depth, height, width)
    even, odd = call(
        functools.partial(cells_kernel, pairs, bands, frame.mirrored),
        (half_cells, half_cells),
        (smem, smem, vmem),
        (vmem, vmem),
        piece_owner,
        piece_row,
        pieces[0],
        scratch=[vmem((blocks * depth, height, width), F32)],
    )
    other = swap(odd, "gy", bands, 1)

    free = pl.ANY
    kept = [even[k] + other[k] for k in range(pairs)]
    moved = [swap(kept[k], ("gz", "gy"), blocks, 2 * k) for k in range(1, pairs)]

    area = depth * height
    payload = call(
        functools.partial(payload_kernel, frame.mirrored),
        shape(area + 8, chunk),
        (smem, vmem, vmem, vmem, free),
        (vmem,),
        background,
        stencil,
        estimate,
        psf_x,
        kept[pairs - 1],
        scratch=[vmem((8, chunk), F32)],
    )
    heard = [payload] + [swap(payload, "view", 4, mask) for mask in (1, 2, 3)]

    def stack(arrays, slices, token):
        rows = slice(slices.start * height, slices.stop * height)
        dims = (len(arrays),) + arrays[0].shape[:-2] + (len(slices) * height, arrays[0].shape[-1])
        return call(
            functools.partial(stack_kernel, rows),
            shape(*dims),
            [vmem] * len(arrays) + [free],
            (vmem,),
            *arrays,
            token,
        )

    def edges(arrays, fars, token, count):
        dims = (len(arrays),) + arrays[0].shape[:-2] + (count, height // 2, arrays[0].shape[-1])
        return call(
            functools.partial(edges_kernel, height, depth, len(sides)),
            (shape(*dims), shape(*dims)),
            [vmem] * (len(arrays) + len(fars)) + [free],
            (vmem, vmem),
            *arrays,
            *fars,
            token,
        )

    far_est = exchange_z(frame, lambda s: stack(heard, s, payload), slabs, depth)
    far_est = [far_est[s] for s in sides]
    table, nums = call(
        functools.partial(band_kernel, area),
        (shape(6, 3 * TILE, TILE), shape(64, 128, dtype=F32)),
        [vmem] * 4 + [free],
        (vmem, vmem),
        *heard,
        payload,
    )
    est_edges = edges(heard, far_est, table, size)
    one_est, two_est = core_side(est_edges, bands, True)
    index_far = exchange_z(frame, lambda s: bleach_index[:, s.start : s.stop], slabs, depth)

    far_slices = frame.sent(3)
    plain, turned, *own_far = call(
        functools.partial(
            total_kernel,
            pairs,
            [slice(s.start * height, s.stop * height) for s in far_slices.values()],
        ),
        (shape(tiles, area, TILE), shape(tiles, area, TILE))
        + tuple(shape(1, tiles, len(s) * height, TILE) for s in far_slices.values()),
        [vmem] * pairs + [free],
        [vmem] * (2 + len(sides)),
        kept[0],
        *moved,
        est_edges[0],
    )
    near = swap(plain, "view", 4, 1)
    opposite = swap(turned, "view", 4, 2)
    last = swap(opposite, "view", 4, 1)
    ready = dict(zip([(s.start, s.stop) for s in far_slices.values()], own_far))
    far_own = exchange_z(frame, lambda s: ready[s.start, s.stop], slabs, 3)
    far_own = [far_own[s] for s in sides]
    n3, n2, n1 = (len(frame.need(r)) * 16 for r in (3, 2, 1))

    est_frame = call(
        functools.partial(frame_kernel, frame, tiles, sides),
        shape(tiles + 2, size * 16, TILE),
        [vmem] * (6 + len(sides)) + [free],
        (vmem,),
        *heard,
        *far_est,
        one_est,
        two_est,
        plain,
    )

    def forward(views, token):
        return call(
            functools.partial(forward_kernel, frame, tiles, views),
            shape(2, tiles, n3, TILE),
            (vmem, vmem, vmem, free),
            (vmem,),
            nums,
            table,
            est_frame,
            token,
            scratch=[vmem((tiles, size * 16, TILE), BF)],
        )

    recip_a = forward((0, 1), plain)
    tokens = []

    def others(slices):
        tokens.append(stack((near, opposite, last), slices, recip_a))
        return tokens[-1]

    far_others = exchange_z(frame, others, slabs, 3)
    far_others = [far_others[s] for s in sides]
    recip_b = forward((2, 3), tokens[-1])
    all_edges = edges(
        (plain, near, opposite, last), far_own + far_others, recip_b, len(frame.need(3))
    )
    one, two = core_side(all_edges, bands, False)
    return call(
        functools.partial(main_kernel, frame, tiles, sides),
        shape(*estimate.shape, dtype=F32),
        [smem] * (2 + len(sides)) + [vmem] * (12 + 2 * len(sides)),
        (vmem,),
        bleach_table,
        bleach_index,
        *[index_far[s] for s in sides],
        nums,
        estimate,
        plain,
        near,
        opposite,
        last,
        *far_own,
        *far_others,
        one,
        two,
        recip_a,
        recip_b,
        table,
        est_frame,
        scratch=[
            vmem((tiles + 2, n3, TILE), BF),
            vmem((tiles + 2, n2, TILE), BF),
            vmem((tiles + 2, n1, TILE), BF),
        ]
        + [vmem((tiles, n3, TILE), BF)] * 4
        + [vmem((tiles, area, TILE), F32), vmem((4 * size * 16, 128), F32)],
    )


def solution(mesh):
    placed = (
        P("view", ("gz", "gy"), None, None),
        P("view", ("gz", "gy"), None),
        P("view", ("gz", "gy")),
        P("gz", "gy", "view"),
        P("view", None),
        P("view", None, None),
        P("view"),
        P(),
        P(None, "gz"),
    )
    return jax.shard_map(
        shards, mesh=mesh, in_specs=placed, out_specs=P("gz", "gy", "view"), check_vma=False
    )
```

```python
import functools

import jax
import jax.numpy as jnp
from jax import lax
from jax.experimental import pallas as pl
from jax.experimental.pallas import tpu as pltpu
from jax.sharding import PartitionSpec as P

BF = jnp.bfloat16
F32 = jnp.float32
TILE = 256
LIMIT = 56 << 20


def whole(*spaces):
    return [pl.BlockSpec(memory_space=space) for space in spaces]


def swap(array, axis, size, mask):
    return lax.ppermute(array, axis, [(i, i ^ mask) for i in range(size)])


def core_side(own, bands, all_take_part):
    first = swap(own[0], "gy", bands, 1)
    if all_take_part:
        return first, swap(own[1], "gy", bands, 3)
    return first, lax.ppermute(own[1], "gy", [(1, 2), (2, 1)])


def upward(array, axis, size):
    return lax.ppermute(array, axis, [(i, i + 1) for i in range(size - 1)])


def downward(array, axis, size):
    return lax.ppermute(array, axis, [(i + 1, i) for i in range(size - 1)])


class Frame:
    def __init__(self, slabs, depth):
        self.mirrored = slabs == 2
        self.depth = depth
        self.own = 0 if self.mirrored else depth
        self.size = 2 * depth if self.mirrored else 3 * depth

    def need(self, radius):
        return range(
            max(0, self.own - radius), min(self.size, self.own + self.depth + radius)
        )

    def source(self, f):
        k = f - self.own
        if 0 <= k < self.depth:
            return "own", k
        if self.mirrored:
            return "up", 2 * self.depth - 1 - k
        return ("dn", f) if k < 0 else ("up", k - self.depth)

    def place(self, f, radius):
        where, k = self.source(f)
        at = 0
        for name, slices in [("own", range(self.depth))] + list(self.sent(radius).items()):
            if name == where:
                return at + k - slices.start
            at += len(slices)

    def sent(self, radius):
        if self.mirrored:
            return {"up": range(self.depth - radius, self.depth)}
        return {
            "dn": range(self.depth - radius, self.depth),
            "up": range(0, radius),
        }


def exchange_z(frame, make, slabs, radius):
    got = {}
    for side, slices in frame.sent(radius).items():
        payload = make(slices)
        if frame.mirrored:
            got[side] = swap(payload, "gz", slabs, 1)
        elif side == "dn":
            got[side] = upward(payload, "gz", slabs)
        else:
            got[side] = downward(payload, "gz", slabs)
    return got


def place():
    return lax.axis_index("view"), lax.axis_index("gz")


def first_kernel(
    pairs,
    bands,
    mirrored,
    owner_ref,
    row_ref,
    bg_ref,
    pieces_ref,
    taps_ref,
    est_ref,
    psf_ref,
    even_ref,
    odd_ref,
    payload_ref,
    acc,
    tail,
):
    write_payload(mirrored, bg_ref, taps_ref, est_ref, psf_ref, payload_ref, tail)
    count = pieces_ref.shape[0]
    depth = even_ref.shape[1]
    me = lax.axis_index("gz") * bands + lax.axis_index("gy")

    def clear(i, carry):
        acc[i] = jnp.zeros(acc.shape[1:], F32)
        return carry

    lax.fori_loop(0, acc.shape[0], clear, 0)

    def add(i, carry):
        owner = owner_ref[0, 0, i]
        row = row_ref[0, i]
        if mirrored:
            row = jnp.where(owner >= bands, depth - 1 - row, row)
        c = (owner ^ me) * depth + row
        acc[c] = acc[c] + pieces_ref[i].astype(F32)
        return carry

    lax.fori_loop(0, count, add, 0)

    def put(pair, carry):
        for f in range(depth):
            even_ref[pair, f] = acc[pair * 2 * depth + f].astype(BF)
            odd_ref[pair, f] = acc[(pair * 2 + 1) * depth + f].astype(BF)
        return carry

    lax.fori_loop(0, pairs, put, 0)


def write_payload(mirrored, bg_ref, taps_ref, est_ref, psf_ref, out_ref, tail):
    depth, height = est_ref.shape[:2]
    upside = lax.axis_index("gz") if mirrored else 0
    for k in range(depth):
        out_ref[k * height : (k + 1) * height, :] = est_ref[
            k + upside * (depth - 1 - 2 * k)
        ].astype(BF)
    tail[...] = jnp.zeros(tail.shape, F32)
    for i in range(3):
        tail[0:1, 3 * i : 3 * i + 3] = taps_ref[i + upside * (2 - 2 * i)]
    lanes = lax.broadcasted_iota(jnp.int32, (1, 128), 1)
    exact = jnp.where(lanes == 9, bg_ref[0], tail[0:1, :128])
    for n in range(3):
        part = exact.astype(BF).astype(F32)
        tail[n + 1 : n + 2, :128] = part
        exact = exact - part
    tail[0:1, : psf_ref.shape[1]] = psf_ref[...]
    out_ref[depth * height :, :] = tail[...].astype(BF)


def numbers_of(heard, at):
    rows = heard[at : at + 8, :128].astype(F32)
    exact = rows[1:2] + rows[2:3] + rows[3:4]
    wide = jnp.broadcast_to(exact, (16, 128))
    spot = lax.broadcasted_iota(jnp.int32, (16, 128), 0) == lax.broadcasted_iota(
        jnp.int32, (16, 128), 1
    )
    column = jnp.sum(jnp.where(spot, wide, 0.0), axis=1, keepdims=True)
    return jnp.broadcast_to(column, (16, 128))


def sum_kernel(pairs, parts, *refs):
    even_ref, other_ref = refs[:2]
    heard = refs[2:6]
    sums, stacks = refs[7 : 7 + pairs], refs[7 + pairs :]
    for k in range(pairs):
        sums[k][...] = (even_ref[k].astype(F32) + other_ref[k].astype(F32)).astype(BF)
    for rows, ref in zip(parts, stacks):
        for v in range(4):
            ref[v] = heard[v][rows, :]


def stack_kernel(rows, *refs):
    ins, out_ref = refs[:-2], refs[-1]
    for v, ref in enumerate(ins):
        out_ref[v] = ref[..., rows, :]


def edges_kernel(height, depth, sides, *refs):
    out1, out2 = refs[-2:]
    count = out1.shape[0]
    views, fars = refs[:count], refs[count:-3]
    half = height // 2
    gy = lax.axis_index("gy")
    even = gy % 2 == 0
    inner = (gy == 1) | (gy == 2)
    lead = out1.shape[1:-3]

    def put(at, block):
        turned = pltpu.roll(block, half, block.ndim - 2)
        one = jnp.where(even, turned, block)
        two = jnp.where(inner, jnp.where(even, block, turned), 0.0)
        out1[at] = one[..., :half, :].astype(BF)
        out2[at] = two[..., :half, :].astype(BF)

    def far_of(v, side):
        for ref in fars[side::sides]:
            if v < ref.shape[0]:
                return ref.at[v]
            v -= ref.shape[0]

    for v, own in enumerate(views):
        n = 0
        for number, source in [(depth, own)] + [
            (fars[side].shape[-2] // height, far_of(v, side)) for side in range(sides)
        ]:
            for k in range(number):
                rows = slice(k * height, (k + 1) * height)
                if lead:

                    def one_tile(t, carry, v=v, n=n, source=source, rows=rows):
                        put((v, t, n), source[t, rows, :].astype(F32))
                        return carry

                    lax.fori_loop(0, lead[0], one_tile, 0, unroll=True)
                else:
                    put((v, n), source[rows, :].astype(F32))
                n += 1


def beside(even, one, two):
    one, two = one.astype(F32), two.astype(F32)
    return jnp.where(
        even, jnp.concatenate([one, two], axis=0), jnp.concatenate([two, one], axis=0)
    )


def reversal():
    rows = lax.broadcasted_iota(jnp.int32, (TILE, TILE), 0)
    cols = lax.broadcasted_iota(jnp.int32, (TILE, TILE), 1)
    return jnp.where(rows + cols == TILE - 1, F32(1.0), F32(0.0)).astype(BF)


def total_kernel(parts, far_rows, *refs):
    ins, (out_ref, rev_ref, *far_refs) = refs[:parts], refs[parts + 1 :]
    tiles, rows, _ = out_ref.shape
    for t in range(tiles):
        cut = slice(t * TILE, (t + 1) * TILE)
        acc = ins[0][:, :, cut].astype(F32)
        for ref in ins[1:]:
            acc = acc + ref[:, :, cut].astype(F32)
        block = acc.reshape(rows, TILE).astype(BF)
        out_ref[t] = block
        for ref, part in zip(far_refs, far_rows):
            ref[0, t] = block[part]
    back = jnp.dot(
        out_ref[...].reshape(tiles * rows, TILE), reversal(), preferred_element_type=F32
    ).astype(BF)
    for t in range(tiles):
        rev_ref[tiles - 1 - t] = back[t * rows : (t + 1) * rows]


def band_kernel(at, *refs):
    heard, (out_ref, num_ref, done_ref) = refs[:4], refs[5:]
    done_ref[...] = jnp.zeros(done_ref.shape, F32)
    for v in range(4):
        num_ref[v * 16 : (v + 1) * 16, :] = numbers_of(heard[v], at)
    flip = reversal()
    for v in range(4):
        row = heard[v][at : at + 8, : 3 * 128].astype(F32)[0:1]
        edge = TILE // 2
        base = jnp.concatenate(
            [jnp.zeros((1, edge), F32), row, jnp.zeros((1, 2 * edge), F32)], axis=1
        )
        wide = pltpu.roll(
            jnp.broadcast_to(base, (TILE, 3 * TILE)), 0, 1, stride=1, stride_axis=0
        ).astype(BF)
        turned = jnp.dot(flip, wide, preferred_element_type=F32).astype(BF)
        for k in range(3):
            cut = slice(k * TILE, (k + 1) * TILE)
            to = slice((2 - k) * TILE, (3 - k) * TILE)
            if v >= 2:
                out_ref[2 + v, cut, :] = turned[:, cut]
            else:
                out_ref[2 + v, to, :] = wide[:, cut]
                out_ref[v, cut, :] = jnp.dot(
                    turned[:, cut], flip, preferred_element_type=F32
                ).astype(BF)


def forward_block(v):
    return v if v < 2 else v + 2


def backward_block(v):
    return v + 2


def conv(src, first, tiles, rows, blocks, dst, step):
    s = 0
    while s < tiles:
        n = min(step, tiles - s)
        lhs = jnp.concatenate(
            [
                src[pl.ds(first + s + k, n)].reshape(n * rows, TILE)
                for k in range(3)
            ],
            axis=1,
        )
        out = jnp.dot(lhs, blocks, preferred_element_type=F32).astype(BF)
        dst[s : s + n] = out.reshape(n, rows, TILE)
        s += n


def taps_sum(slices, zs, taps):
    result = {}
    for z in zs:
        sums = [None, None, None]
        for j in range(3):
            for i in range(3):
                at = z + i - 1
                if at in slices:
                    term = taps(z, i, j) * slices[at]
                    sums[j] = term if sums[j] is None else sums[j] + term
        result[z] = sums
    return result


def along_y(sums):
    n = sums[0].shape[0]
    return pltpu.roll(sums[0], 1, 0) + sums[1] + pltpu.roll(sums[2], n - 1, 0)


def write_frame(frame, tiles, sides, *refs):
    own_refs, refs = refs[:4], refs[4:]
    side_refs = dict(zip(sides, refs[: len(sides)]))
    one_ref, two_ref, out_ref = refs[len(sides) :]
    view = lax.axis_index("view")
    even = lax.axis_index("gy") % 2 == 0
    for e in (0, tiles + 1):
        out_ref[e] = jnp.zeros(out_ref.shape[1:], BF)
    for v in range(4):
        for s in range(tiles // 4):
            t = (view ^ v) * (tiles // 4) + s + 1
            cut = slice(s * TILE, (s + 1) * TILE)
            for f in range(frame.size):
                where, k = frame.source(f)
                rows = slice(k * 8, (k + 1) * 8)
                if where == "own":
                    own = own_refs[v][rows, cut]
                else:
                    own = side_refs[where][v, rows, cut]
                n = frame.place(f, frame.depth)
                out_ref[t, f * 16 : (f + 1) * 16, :] = jnp.concatenate(
                    [
                        own.astype(F32),
                        beside(even, one_ref[v, n, :, cut], two_ref[v, n, :, cut]),
                    ],
                    axis=0,
                ).astype(BF)


def start_kernel(frame, tiles, sides, views, num_ref, blocks_ref, *refs):
    count = len(sides)
    out_ref, recip_ref, done_ref, c = refs[7 + count :]
    write_frame(frame, tiles, sides, *refs[: 6 + count], out_ref)
    forward_views(frame, tiles, views, num_ref, blocks_ref, out_ref, recip_ref, c)
    done_ref[...] = jnp.zeros(done_ref.shape, F32)


def forward_kernel(frame, tiles, views, num_ref, blocks_ref, frame_ref, _, recip_ref, done_ref, c):
    forward_views(frame, tiles, views, num_ref, blocks_ref, frame_ref, recip_ref, c)
    done_ref[...] = jnp.zeros(done_ref.shape, F32)


def forward_views(frame, tiles, views, num_ref, blocks_ref, frame_ref, recip_ref, c):
    size = frame.size
    zs = frame.need(3)
    for at, v in enumerate(views):
        conv(frame_ref, 0, tiles, size * 16, blocks_ref[forward_block(v)], c, 2)

        def divide(t, carry, v=v, at=at):
            from_t = t if v < 2 else tiles - 1 - t
            for h in range(TILE // 128):
                cut = slice(h * 128, (h + 1) * 128)
                slices = {
                    f: c[from_t, f * 16 : (f + 1) * 16, cut].astype(F32)
                    for f in range(size)
                }
                sums = taps_sum(slices, zs, lambda z, i, j: num_ref[v * 16 + i * 3 + j : v * 16 + i * 3 + j + 1, :])
                for n, z in enumerate(zs):
                    recip_ref[at, t, n * 16 : (n + 1) * 16, cut] = (
                        1.0 / (along_y(sums[z]) + num_ref[v * 16 + 9 : v * 16 + 10, :])
                    ).astype(BF)
            return carry

        lax.fori_loop(0, tiles, divide, 0)


def main_kernel(frame, tiles, sides, table_ref, *refs):
    count = len(sides)
    index_refs, refs = refs[: count + 1], refs[count + 1 :]
    num_ref, est_ref, refs = refs[0], refs[1], refs[2:]
    own_refs, refs = refs[:4], refs[4:]
    far_refs, refs = refs[: 2 * count], refs[2 * count :]
    one_ref, two_ref = refs[:2]
    recip_refs = refs[2:4]
    blocks_ref, frame_ref, out_ref = refs[4:7]
    m1, u2, m2, c0, c1, c2, c3, kept, wt = refs[7:]
    even = lax.axis_index("gy") % 2 == 0
    c = [c0, c1, c2, c3]
    view = lax.axis_index("view")
    upside = lax.axis_index("gz") if frame.mirrored else 0
    depth = frame.depth
    z3, z2, z1, z0 = (frame.need(r) for r in (3, 2, 1, 0))
    sent = frame.sent(3)

    for f in z2:
        where, k = frame.source(f)
        index_ref = index_refs[0 if where == "own" else 1 + sides.index(where)]
        over = upside if where == "own" else 1 - upside
        raw = k + over * (depth - 1 - 2 * k) if frame.mirrored else k
        weights = [
            jnp.full((16, 128), table_ref[v, index_ref[v, raw]], F32) for v in range(4)
        ]
        total = (weights[0] + weights[1]) + (weights[2] + weights[3])
        for v in range(4):
            mine = jnp.full(
                (16, 128), table_ref[view ^ v, index_ref[view ^ v, raw]], F32
            )
            at = (v * frame.size + f) * 16
            wt[at : at + 16, :] = num_ref[v * 16 : (v + 1) * 16, :] * (mine / total)

    def weighted(v, z, n):
        at = (v * frame.size + z) * 16 + 8 - n
        return wt[at : at + 1, :]

    def measured(v, t, z, cut):
        where, k = frame.source(z)
        if where == "own":
            own = own_refs[v][t, k * 8 : (k + 1) * 8, cut]
        else:
            k = k - sent[where].start
            far = far_refs[(count if v else 0) + sides.index(where)]
            own = far[v - 1 if v else 0, t, k * 8 : (k + 1) * 8, cut]
        n = frame.place(z, 3)
        return jnp.concatenate(
            [
                own.astype(F32),
                beside(
                    even,
                    one_ref[v, t, n, :, cut],
                    two_ref[v, t, n, :, cut],
                ),
            ],
            axis=0,
        )

    def mix(v, t, z, cut, recip_a, recip_b):
        a = (measured(v, t, z, cut) * recip_a).astype(BF).astype(F32)
        b = (measured(v + 2, t, z, cut) * recip_b).astype(BF).astype(F32)
        return (0.5 * (a + b)).astype(BF)

    def zero_ends(ref):
        for e in (0, ref.shape[0] - 1):
            ref[e] = jnp.zeros(ref.shape[1:], BF)

    for ref in (m1, u2, m2):
        zero_ends(ref)

    for v in range(2):

        def ratios(t, carry, v=v):
            for h in range(TILE // 128):
                cut = slice(h * 128, (h + 1) * 128)
                for n, z in enumerate(z3):
                    at = slice(n * 16, (n + 1) * 16)
                    m1[t + 1, at, cut] = mix(
                        v,
                        t,
                        z,
                        cut,
                        recip_refs[0][v, t, at, cut].astype(F32),
                        recip_refs[1][v, t, at, cut].astype(F32),
                    )
            return carry

        lax.fori_loop(0, tiles, ratios, 0)
        for w in (v, v + 2):
            conv(m1, 0, tiles, m1.shape[1], blocks_ref[backward_block(w)], c[w], 2)

    def numerator(slices_of, zs):
        totals = {z: [None, None, None] for z in zs}
        for v in range(4):
            slices = slices_of(v)
            sums = taps_sum(
                slices,
                zs,
                lambda z, i, j, v=v: weighted(v, z, i * 3 + j),
            )
            for z in zs:
                for j in range(3):
                    old = totals[z][j]
                    totals[z][j] = sums[z][j] if old is None else old + sums[z][j]
        return totals

    def update(t, carry):
        for h in range(TILE // 128):
            cut = slice(h * 128, (h + 1) * 128)

            def slices_of(v):
                from_t = t if v < 2 else tiles - 1 - t
                return {
                    z: c[v][from_t, n * 16 : (n + 1) * 16, cut].astype(F32)
                    for n, z in enumerate(z3)
                }

            totals = numerator(slices_of, z2)
            for n, z in enumerate(z2):
                change = along_y(totals[z])
                before = frame_ref[t + 1, z * 16 : (z + 1) * 16, cut].astype(F32)
                u2[t + 1, n * 16 : (n + 1) * 16, cut] = (before * change).astype(BF)
                if z in z0:
                    k = z - frame.own
                    kept[t, k * 8 : (k + 1) * 8, cut] = change[:8]
        return carry

    lax.fori_loop(0, tiles, update, 0)

    rows1 = m2.shape[1]
    n2 = u2.shape[1]
    for v in range(2):
        for w in (v, v + 2):
            conv(u2, 0, tiles, n2, blocks_ref[forward_block(w)], c[w].at[:, :n2, :], 2)

        def ratios2(t, carry, v=v):
            for h in range(TILE // 128):
                cut = slice(h * 128, (h + 1) * 128)
                recips = []
                for w in (v, v + 2):
                    from_t = t if w < 2 else tiles - 1 - t
                    slices = {
                        z: c[w][from_t, n * 16 : (n + 1) * 16, cut].astype(F32)
                        for n, z in enumerate(z2)
                    }
                    sums = taps_sum(
                        slices, z1, lambda z, i, j, w=w: num_ref[w * 16 + i * 3 + j : w * 16 + i * 3 + j + 1, :]
                    )
                    recips.append(
                        {z: 1.0 / (along_y(sums[z]) + num_ref[w * 16 + 9 : w * 16 + 10, :]) for z in z1}
                    )
                for n, z in enumerate(z1):
                    m2[t + 1, n * 16 : (n + 1) * 16, cut] = mix(
                        v, t, z, cut, recips[0][z], recips[1][z]
                    )
            return carry

        lax.fori_loop(0, tiles, ratios2, 0)
        mine = tiles // 4
        for w in (v, v + 2):
            first = view * mine if w < 2 else tiles - (view + 1) * mine
            conv(m2, first, mine, rows1, blocks_ref[backward_block(w)], c[w].at[:, :rows1, :], 2)

    mine = tiles // 4
    for s in range(mine):
        for h in range(TILE // 128):
            cut = slice(h * 128, (h + 1) * 128)

            def slices_of(v):
                from_s = s if v < 2 else mine - 1 - s
                return {
                    z: c[v][from_s, n * 16 : (n + 1) * 16, cut].astype(F32)
                    for n, z in enumerate(z1)
                }

            totals = numerator(slices_of, z0)
            for z in z0:
                k = z - frame.own
                to = k + upside * (depth - 1 - 2 * k)
                lanes = slice(s * TILE + h * 128, s * TILE + (h + 1) * 128)
                first_change = kept[view * mine + s, k * 8 : (k + 1) * 8, cut]
                out_ref[to, :, lanes] = (
                    est_ref[to, :, lanes] * first_change * along_y(totals[z])[:8]
                )


def shards(
    pieces, piece_owner, piece_row, estimate, psf_x, stencil, background, bleach_table, bleach_index
):
    depth, height, chunk = estimate.shape
    width = pieces.shape[3]
    tiles = width // TILE
    slabs = lax.axis_size("gz")
    bands = lax.axis_size("gy")
    blocks = slabs * bands
    frame = Frame(slabs, depth)
    size = frame.size
    sides = tuple(frame.sent(1))
    vmem, smem = pltpu.VMEM, pltpu.SMEM
    params = pltpu.CompilerParams(vmem_limit_bytes=LIMIT)

    def call(kernel, shapes, ins, outs, *args, scratch=()):
        return pl.pallas_call(
            kernel,
            out_shape=shapes,
            in_specs=whole(*ins),
            out_specs=whole(*outs) if isinstance(shapes, tuple) else whole(*outs)[0],
            scratch_shapes=list(scratch),
            compiler_params=params,
        )(*args)

    def resident(*dims, dtype=BF):
        return pltpu.VMEM(dims, dtype)

    def stay(array):
        return pltpu.with_memory_space_constraint(array, pltpu.VMEM)

    def shape(*dims, dtype=BF):
        return jax.ShapeDtypeStruct(dims, dtype)

    free = pl.ANY
    area = depth * height

    pairs = blocks // 2
    half_cells = shape(pairs, depth, height, width)
    even, odd, payload = call(
        functools.partial(first_kernel, pairs, bands, frame.mirrored),
        (half_cells, half_cells, shape(area + 8, chunk)),
        (smem, smem, smem, vmem, vmem, vmem, vmem),
        (vmem, vmem, vmem),
        piece_owner.transpose(0, 2, 1),
        piece_row,
        background,
        pieces[0],
        stencil.transpose(1, 0, 2),
        estimate,
        psf_x,
        scratch=[vmem((blocks * depth, height, width), F32), vmem((8, chunk), F32)],
    )
    other = swap(odd, "gy", bands, 1)
    heard = [payload] + [swap(payload, "view", 4, mask) for mask in (1, 2, 3)]
    index_far = exchange_z(frame, lambda s: bleach_index[:, s.start : s.stop], slabs, depth)
    est_slices = frame.sent(depth)
    out = call(
        functools.partial(
            sum_kernel,
            pairs,
            [slice(s.start * height, s.stop * height) for s in est_slices.values()],
        ),
        (shape(depth, height, width),) * pairs
        + tuple(shape(4, len(s) * height, chunk) for s in est_slices.values()),
        [vmem] * 6 + [free],
        [vmem] * (pairs + len(sides)),
        even,
        other,
        *heard,
        index_far[sides[0]],
    )
    kept, est_stacks = out[:pairs], out[pairs:]
    moved = [swap(kept[k], ("gz", "gy"), blocks, 2 * k) for k in range(1, pairs)]

    def stack(arrays, slices, token):
        rows = slice(slices.start * height, slices.stop * height)
        dims = (len(arrays),) + arrays[0].shape[:-2] + (len(slices) * height, arrays[0].shape[-1])
        return call(
            functools.partial(stack_kernel, rows),
            shape(*dims),
            [vmem] * len(arrays) + [free],
            (vmem,),
            *arrays,
            token,
        )

    def edges(arrays, fars, token, count):
        dims = (len(arrays),) + arrays[0].shape[:-2] + (count, height // 2, arrays[0].shape[-1])
        return call(
            functools.partial(edges_kernel, height, depth, len(sides)),
            (shape(*dims), shape(*dims)),
            [vmem] * (len(arrays) + len(fars)) + [free],
            (vmem, vmem),
            *arrays,
            *fars,
            token,
        )

    stacks = dict(zip([(s.start, s.stop) for s in est_slices.values()], est_stacks))
    far_est = exchange_z(frame, lambda s: stacks[s.start, s.stop], slabs, depth)
    far_est = [far_est[s] for s in sides]
    table, nums, token = call(
        functools.partial(band_kernel, area),
        (resident(6, 3 * TILE, TILE), resident(64, 128, dtype=F32), shape(8, 128, dtype=F32)),
        [vmem] * 4 + [free],
        (vmem, vmem, vmem),
        *heard,
        kept[0],
    )
    kept_table, kept_nums = stay(table), stay(nums)
    est_edges = edges(heard, far_est, token, size)
    one_est, two_est = core_side(est_edges, bands, True)

    far_slices = frame.sent(3)
    plain, turned, *own_far = call(
        functools.partial(
            total_kernel,
            pairs,
            [slice(s.start * height, s.stop * height) for s in far_slices.values()],
        ),
        (shape(tiles, area, TILE), shape(tiles, area, TILE))
        + tuple(shape(1, tiles, len(s) * height, TILE) for s in far_slices.values()),
        [vmem] * pairs + [free],
        [vmem] * (2 + len(sides)),
        kept[0],
        *moved,
        est_edges[0],
    )
    near = swap(plain, "view", 4, 1)
    opposite = swap(turned, "view", 4, 2)
    last = swap(opposite, "view", 4, 1)
    ready = dict(zip([(s.start, s.stop) for s in far_slices.values()], own_far))
    far_own = exchange_z(frame, lambda s: ready[s.start, s.stop], slabs, 3)
    far_own = [far_own[s] for s in sides]
    n3, n2, n1 = (len(frame.need(r)) * 16 for r in (3, 2, 1))

    scratch = [vmem((tiles, size * 16, TILE), BF)]
    est_frame, recip_a, token = call(
        functools.partial(start_kernel, frame, tiles, sides, (0, 1)),
        (
            resident(tiles + 2, size * 16, TILE),
            resident(2, tiles, n3, TILE),
            shape(8, 128, dtype=F32),
        ),
        [vmem] * (8 + len(sides)) + [free],
        (vmem, vmem, vmem),
        kept_nums,
        kept_table,
        *heard,
        *far_est,
        one_est,
        two_est,
        plain,
        scratch=scratch,
    )
    tokens = []

    def others(slices):
        tokens.append(stack((near, opposite, last), slices, token))
        return tokens[-1]

    far_others = exchange_z(frame, others, slabs, 3)
    far_others = [far_others[s] for s in sides]
    recip_b, token_b = call(
        functools.partial(forward_kernel, frame, tiles, (2, 3)),
        (resident(2, tiles, n3, TILE), shape(8, 128, dtype=F32)),
        (vmem, vmem, vmem, free),
        (vmem, vmem),
        kept_nums,
        kept_table,
        stay(est_frame),
        tokens[-1],
        scratch=scratch,
    )
    all_edges = edges(
        (plain, near, opposite, last), far_own + far_others, token_b, len(frame.need(3))
    )
    one, two = core_side(all_edges, bands, False)
    return call(
        functools.partial(main_kernel, frame, tiles, sides),
        shape(*estimate.shape, dtype=F32),
        [smem] * (2 + len(sides)) + [vmem] * (12 + 2 * len(sides)),
        (vmem,),
        bleach_table,
        bleach_index,
        *[index_far[s] for s in sides],
        kept_nums,
        estimate,
        plain,
        near,
        opposite,
        last,
        *far_own,
        *far_others,
        one,
        two,
        stay(recip_a),
        stay(recip_b),
        kept_table,
        stay(est_frame),
        scratch=[
            vmem((tiles + 2, n3, TILE), BF),
            vmem((tiles + 2, n2, TILE), BF),
            vmem((tiles + 2, n1, TILE), BF),
        ]
        + [vmem((tiles, n3, TILE), BF)] * 4
        + [vmem((tiles, area, TILE), F32), vmem((4 * size * 16, 128), F32)],
    )


def solution(mesh):
    placed = (
        P("view", ("gz", "gy"), None, None),
        P("view", ("gz", "gy"), None),
        P("view", ("gz", "gy")),
        P("gz", "gy", "view"),
        P("view", None),
        P("view", None, None),
        P("view"),
        P(),
        P(None, "gz"),
    )
    return jax.shard_map(
        shards, mesh=mesh, in_specs=placed, out_specs=P("gz", "gy", "view"), check_vma=False
    )
```

```python
import functools

import jax
import jax.numpy as jnp
from jax import lax
from jax.experimental import pallas as pl
from jax.experimental.pallas import tpu as pltpu
from jax.sharding import PartitionSpec as P

BF = jnp.bfloat16
F32 = jnp.float32
TILE = 256
LIMIT = 24 << 20


def whole(*spaces):
    return [pl.BlockSpec(memory_space=space) for space in spaces]


def swap(array, axis, size, mask):
    return lax.ppermute(array, axis, [(i, i ^ mask) for i in range(size)])


def core_side(own, bands, all_take_part):
    first = swap(own[0], "gy", bands, 1)
    if all_take_part:
        return first, swap(own[1], "gy", bands, 3)
    return first, lax.ppermute(own[1], "gy", [(1, 2), (2, 1)])


def upward(array, axis, size):
    return lax.ppermute(array, axis, [(i, i + 1) for i in range(size - 1)])


def downward(array, axis, size):
    return lax.ppermute(array, axis, [(i + 1, i) for i in range(size - 1)])


class Frame:
    def __init__(self, slabs, depth):
        self.mirrored = slabs == 2
        self.depth = depth
        self.own = 0 if self.mirrored else depth
        self.size = 2 * depth if self.mirrored else 3 * depth

    def need(self, radius):
        return range(
            max(0, self.own - radius), min(self.size, self.own + self.depth + radius)
        )

    def source(self, f):
        k = f - self.own
        if 0 <= k < self.depth:
            return "own", k
        if self.mirrored:
            return "up", 2 * self.depth - 1 - k
        return ("dn", f) if k < 0 else ("up", k - self.depth)

    def place(self, f, radius):
        where, k = self.source(f)
        at = 0
        for name, slices in [("own", range(self.depth))] + list(self.sent(radius).items()):
            if name == where:
                return at + k - slices.start
            at += len(slices)

    def sent(self, radius):
        if self.mirrored:
            return {"up": range(self.depth - radius, self.depth)}
        return {
            "dn": range(self.depth - radius, self.depth),
            "up": range(0, radius),
        }


def exchange_z(frame, make, slabs, radius):
    got = {}
    for side, slices in frame.sent(radius).items():
        payload = make(slices)
        if frame.mirrored:
            got[side] = swap(payload, "gz", slabs, 1)
        elif side == "dn":
            got[side] = upward(payload, "gz", slabs)
        else:
            got[side] = downward(payload, "gz", slabs)
    return got


def place():
    return lax.axis_index("view"), lax.axis_index("gz")


def first_kernel(
    pairs,
    bands,
    mirrored,
    owner_ref,
    row_ref,
    bg_ref,
    pieces_ref,
    taps_ref,
    est_ref,
    psf_ref,
    even_ref,
    odd_ref,
    payload_ref,
    acc,
    tail,
):
    write_payload(mirrored, bg_ref, taps_ref, est_ref, psf_ref, payload_ref, tail)
    count = pieces_ref.shape[0]
    depth = even_ref.shape[1]
    me = lax.axis_index("gz") * bands + lax.axis_index("gy")

    def clear(i, carry):
        acc[i] = jnp.zeros(acc.shape[1:], F32)
        return carry

    lax.fori_loop(0, acc.shape[0], clear, 0)

    def add(i, carry):
        owner = owner_ref[0, 0, i]
        row = row_ref[0, i]
        if mirrored:
            row = jnp.where(owner >= bands, depth - 1 - row, row)
        c = (owner ^ me) * depth + row
        acc[c] = acc[c] + pieces_ref[i].astype(F32)
        return carry

    lax.fori_loop(0, count, add, 0)

    def put(pair, carry):
        for f in range(depth):
            even_ref[pair, f] = acc[pair * 2 * depth + f].astype(BF)
            odd_ref[pair, f] = acc[(pair * 2 + 1) * depth + f].astype(BF)
        return carry

    lax.fori_loop(0, pairs, put, 0)


def write_payload(mirrored, bg_ref, taps_ref, est_ref, psf_ref, out_ref, tail):
    depth, height = est_ref.shape[:2]
    upside = lax.axis_index("gz") if mirrored else 0
    for k in range(depth):
        out_ref[k * height : (k + 1) * height, :] = est_ref[
            k + upside * (depth - 1 - 2 * k)
        ].astype(BF)
    tail[...] = jnp.zeros(tail.shape, F32)
    for i in range(3):
        tail[0:1, 3 * i : 3 * i + 3] = taps_ref[i + upside * (2 - 2 * i)]
    lanes = lax.broadcasted_iota(jnp.int32, (1, 128), 1)
    exact = jnp.where(lanes == 9, bg_ref[0], tail[0:1, :128])
    for n in range(3):
        part = exact.astype(BF).astype(F32)
        tail[n + 1 : n + 2, :128] = part
        exact = exact - part
    tail[0:1, : psf_ref.shape[1]] = psf_ref[...]
    out_ref[depth * height :, :] = tail[...].astype(BF)


def numbers_of(heard, at):
    rows = heard[at : at + 8, :128].astype(F32)
    exact = rows[1:2] + rows[2:3] + rows[3:4]
    wide = jnp.broadcast_to(exact, (16, 128))
    spot = lax.broadcasted_iota(jnp.int32, (16, 128), 0) == lax.broadcasted_iota(
        jnp.int32, (16, 128), 1
    )
    column = jnp.sum(jnp.where(spot, wide, 0.0), axis=1, keepdims=True)
    return jnp.broadcast_to(column, (16, 128))


def sum_kernel(pairs, parts, *refs):
    even_ref, other_ref = refs[:2]
    heard = refs[2:6]
    sums, stacks, done_ref = refs[7 : 7 + pairs], refs[7 + pairs : -1], refs[-1]
    done_ref[...] = jnp.zeros(done_ref.shape, F32)
    for k in range(pairs):
        sums[k][...] = (even_ref[k].astype(F32) + other_ref[k].astype(F32)).astype(BF)
    for rows, ref in zip(parts, stacks):
        for v in range(4):
            ref[v] = heard[v][rows, :]


def stack_kernel(rows, *refs):
    ins, (out_ref, done_ref) = refs[:-3], refs[-2:]
    done_ref[...] = jnp.zeros(done_ref.shape, F32)
    for v, ref in enumerate(ins):
        out_ref[v] = ref[..., rows, :]


def edges_kernel(height, depth, sides, *refs):
    out1, out2, done_ref = refs[-3:]
    done_ref[...] = jnp.zeros(done_ref.shape, F32)
    count = out1.shape[0]
    views = refs[:count] if depth else [None] * count
    fars = refs[count if depth else 0 : -4]
    half = height // 2
    gy = lax.axis_index("gy")
    even = gy % 2 == 0
    inner = (gy == 1) | (gy == 2)
    lead = out1.shape[1:-3]

    def put(at, block):
        turned = pltpu.roll(block, half, block.ndim - 2)
        one = jnp.where(even, turned, block)
        two = jnp.where(inner, jnp.where(even, block, turned), 0.0)
        out1[at] = one[..., :half, :].astype(BF)
        out2[at] = two[..., :half, :].astype(BF)

    def far_of(v, side):
        for ref in fars[side::sides]:
            if v < ref.shape[0]:
                return ref.at[v]
            v -= ref.shape[0]

    for v, own in enumerate(views):
        n = 0
        sources = [(depth, own)] if depth else []
        if fars:
            sources += [
                (fars[side].shape[-2] // height, far_of(v, side)) for side in range(sides)
            ]
        for number, source in sources:
            for k in range(number):
                rows = slice(k * height, (k + 1) * height)
                if lead:

                    def one_tile(t, carry, v=v, n=n, source=source, rows=rows):
                        put((v, t, n), source[t, rows, :].astype(F32))
                        return carry

                    lax.fori_loop(0, lead[0], one_tile, 0, unroll=True)
                else:
                    put((v, n), source[rows, :].astype(F32))
                n += 1


def beside(even, one, two):
    one, two = one.astype(F32), two.astype(F32)
    return jnp.where(
        even, jnp.concatenate([one, two], axis=0), jnp.concatenate([two, one], axis=0)
    )


def reversal():
    rows = lax.broadcasted_iota(jnp.int32, (TILE, TILE), 0)
    cols = lax.broadcasted_iota(jnp.int32, (TILE, TILE), 1)
    return jnp.where(rows + cols == TILE - 1, F32(1.0), F32(0.0)).astype(BF)


def total_kernel(parts, far_rows, *refs):
    ins, (out_ref, rev_ref, *far_refs, done_ref) = refs[:parts], refs[parts + 1 :]
    done_ref[...] = jnp.zeros(done_ref.shape, F32)
    tiles, rows, _ = out_ref.shape
    for t in range(tiles):
        cut = slice(t * TILE, (t + 1) * TILE)
        acc = ins[0][:, :, cut].astype(F32)
        for ref in ins[1:]:
            acc = acc + ref[:, :, cut].astype(F32)
        block = acc.reshape(rows, TILE).astype(BF)
        out_ref[t] = block
        for ref, part in zip(far_refs, far_rows):
            ref[0, t] = block[part]
    back = jnp.dot(
        out_ref[...].reshape(tiles * rows, TILE), reversal(), preferred_element_type=F32
    ).astype(BF)
    for t in range(tiles):
        rev_ref[tiles - 1 - t] = back[t * rows : (t + 1) * rows]


def band_kernel(at, *refs):
    heard, (out_ref, num_ref, done_ref) = refs[:4], refs[5:]
    done_ref[...] = jnp.zeros(done_ref.shape, F32)
    for v in range(4):
        num_ref[v * 16 : (v + 1) * 16, :] = numbers_of(heard[v], at)
    flip = reversal()
    for v in range(4):
        row = heard[v][at : at + 8, : 3 * 128].astype(F32)[0:1]
        edge = TILE // 2
        base = jnp.concatenate(
            [jnp.zeros((1, edge), F32), row, jnp.zeros((1, 2 * edge), F32)], axis=1
        )
        wide = pltpu.roll(
            jnp.broadcast_to(base, (TILE, 3 * TILE)), 0, 1, stride=1, stride_axis=0
        ).astype(BF)
        turned = jnp.dot(flip, wide, preferred_element_type=F32).astype(BF)
        for k in range(3):
            cut = slice(k * TILE, (k + 1) * TILE)
            to = slice((2 - k) * TILE, (3 - k) * TILE)
            if v >= 2:
                out_ref[2 + v, cut, :] = turned[:, cut]
            else:
                out_ref[2 + v, to, :] = wide[:, cut]
                out_ref[v, cut, :] = jnp.dot(
                    turned[:, cut], flip, preferred_element_type=F32
                ).astype(BF)


def forward_block(v):
    return v if v < 2 else v + 2


def backward_block(v):
    return v + 2


def conv(src, first, tiles, rows, blocks, dst, step):
    s = 0
    while s < tiles:
        n = min(step, tiles - s)
        lhs = jnp.concatenate(
            [
                src[pl.ds(first + s + k, n)].reshape(n * rows, TILE)
                for k in range(3)
            ],
            axis=1,
        )
        out = jnp.dot(lhs, blocks, preferred_element_type=F32).astype(BF)
        dst[s : s + n] = out.reshape(n, rows, TILE)
        s += n


def taps_sum(slices, zs, taps):
    result = {}
    for z in zs:
        sums = [None, None, None]
        for j in range(3):
            for i in range(3):
                at = z + i - 1
                if at in slices:
                    term = taps(z, i, j) * slices[at]
                    sums[j] = term if sums[j] is None else sums[j] + term
        result[z] = sums
    return result


def along_y(sums):
    n = sums[0].shape[0]
    return pltpu.roll(sums[0], 1, 0) + sums[1] + pltpu.roll(sums[2], n - 1, 0)


def write_frame(frame, tiles, sides, *refs):
    own_refs, refs = refs[:4], refs[4:]
    side_refs = dict(zip(sides, refs[: len(sides)]))
    one_ref, two_ref, out_ref = refs[len(sides) :]
    view = lax.axis_index("view")
    even = lax.axis_index("gy") % 2 == 0
    for e in (0, tiles + 1):
        out_ref[e] = jnp.zeros(out_ref.shape[1:], BF)
    for v in range(4):
        for s in range(tiles // 4):
            t = (view ^ v) * (tiles // 4) + s + 1
            cut = slice(s * TILE, (s + 1) * TILE)
            for f in range(frame.size):
                where, k = frame.source(f)
                rows = slice(k * 8, (k + 1) * 8)
                if where == "own":
                    own = own_refs[v][rows, cut]
                else:
                    own = side_refs[where][v, rows, cut]
                n = frame.place(f, frame.depth)
                out_ref[t, f * 16 : (f + 1) * 16, :] = jnp.concatenate(
                    [
                        own.astype(F32),
                        beside(even, one_ref[v, n, :, cut], two_ref[v, n, :, cut]),
                    ],
                    axis=0,
                ).astype(BF)


def start_kernel(frame, tiles, sides, views, num_ref, blocks_ref, *refs):
    count = len(sides)
    out_ref, recip_ref, done_ref, c = refs[7 + count :]
    write_frame(frame, tiles, sides, *refs[: 6 + count], out_ref)
    forward_views(frame, tiles, views, num_ref, blocks_ref, out_ref, recip_ref, c)
    done_ref[...] = jnp.zeros(done_ref.shape, F32)


def forward_kernel(frame, tiles, views, num_ref, blocks_ref, frame_ref, _, recip_ref, done_ref, c):
    forward_views(frame, tiles, views, num_ref, blocks_ref, frame_ref, recip_ref, c)
    done_ref[...] = jnp.zeros(done_ref.shape, F32)


def forward_views(frame, tiles, views, num_ref, blocks_ref, frame_ref, recip_ref, c):
    size = frame.size
    zs = frame.need(3)
    for at, v in enumerate(views):
        conv(frame_ref, 0, tiles, size * 16, blocks_ref[forward_block(v)], c, 2)

        def divide(t, carry, v=v, at=at):
            from_t = t if v < 2 else tiles - 1 - t
            for h in range(TILE // 128):
                cut = slice(h * 128, (h + 1) * 128)
                slices = {
                    f: c[from_t, f * 16 : (f + 1) * 16, cut].astype(F32)
                    for f in range(size)
                }
                sums = taps_sum(slices, zs, lambda z, i, j: num_ref[v * 16 + i * 3 + j : v * 16 + i * 3 + j + 1, :])
                for n, z in enumerate(zs):
                    recip_ref[at, t, n * 16 : (n + 1) * 16, cut] = (
                        1.0 / (along_y(sums[z]) + num_ref[v * 16 + 9 : v * 16 + 10, :])
                    ).astype(BF)
            return carry

        lax.fori_loop(0, tiles, divide, 0)


def main_kernel(frame, tiles, sides, table_ref, *refs):
    count = len(sides)
    index_refs, refs = refs[: count + 1], refs[count + 1 :]
    num_ref, est_ref, refs = refs[0], refs[1], refs[2:]
    own_refs, refs = refs[:4], refs[4:]
    far_refs, refs = refs[: 2 * count], refs[2 * count :]
    near_refs, beyond_refs = refs[:2], refs[2:4]
    recip_refs = refs[4:6]
    blocks_ref, frame_ref, out_ref = refs[6:9]
    m1, u2, m2, c0, c1, c2, c3, kept, wt = refs[9:]
    even = lax.axis_index("gy") % 2 == 0
    c = [c0, c1, c2, c3]
    view = lax.axis_index("view")
    upside = lax.axis_index("gz") if frame.mirrored else 0
    depth = frame.depth
    z3, z2, z1, z0 = (frame.need(r) for r in (3, 2, 1, 0))
    sent = frame.sent(3)

    for f in z2:
        where, k = frame.source(f)
        index_ref = index_refs[0 if where == "own" else 1 + sides.index(where)]
        over = upside if where == "own" else 1 - upside
        raw = k + over * (depth - 1 - 2 * k) if frame.mirrored else k
        weights = [
            jnp.full((16, 128), table_ref[v, index_ref[v, raw]], F32) for v in range(4)
        ]
        total = (weights[0] + weights[1]) + (weights[2] + weights[3])
        for v in range(4):
            mine = jnp.full(
                (16, 128), table_ref[view ^ v, index_ref[view ^ v, raw]], F32
            )
            at = (v * frame.size + f) * 16
            wt[at : at + 16, :] = num_ref[v * 16 : (v + 1) * 16, :] * (mine / total)

    def weighted(v, z, n):
        at = (v * frame.size + z) * 16 + 8 - n
        return wt[at : at + 1, :]

    def measured(v, t, z, cut):
        where, k = frame.source(z)
        if where == "own":
            own = own_refs[v][t, k * 8 : (k + 1) * 8, cut]
        else:
            k = k - sent[where].start
            far = far_refs[(count if v else 0) + sides.index(where)]
            own = far[v - 1 if v else 0, t, k * 8 : (k + 1) * 8, cut]
        n = frame.place(z, 3)
        one_ref, two_ref = near_refs if n < depth else beyond_refs
        n = n if n < depth else n - depth
        return jnp.concatenate(
            [
                own.astype(F32),
                beside(
                    even,
                    one_ref[v, t, n, :, cut],
                    two_ref[v, t, n, :, cut],
                ),
            ],
            axis=0,
        )

    def mix(v, t, z, cut, recip_a, recip_b):
        a = (measured(v, t, z, cut) * recip_a).astype(BF).astype(F32)
        b = (measured(v + 2, t, z, cut) * recip_b).astype(BF).astype(F32)
        return (0.5 * (a + b)).astype(BF)

    def zero_ends(ref):
        for e in (0, ref.shape[0] - 1):
            ref[e] = jnp.zeros(ref.shape[1:], BF)

    for ref in (m1, u2, m2):
        zero_ends(ref)

    for v in range(2):

        def ratios(t, carry, v=v):
            for h in range(TILE // 128):
                cut = slice(h * 128, (h + 1) * 128)
                for n, z in enumerate(z3):
                    at = slice(n * 16, (n + 1) * 16)
                    m1[t + 1, at, cut] = mix(
                        v,
                        t,
                        z,
                        cut,
                        recip_refs[0][v, t, at, cut].astype(F32),
                        recip_refs[1][v, t, at, cut].astype(F32),
                    )
            return carry

        lax.fori_loop(0, tiles, ratios, 0)
        for w in (v, v + 2):
            conv(m1, 0, tiles, m1.shape[1], blocks_ref[backward_block(w)], c[w], 2)

    def numerator(slices_of, zs):
        totals = {z: [None, None, None] for z in zs}
        for v in range(4):
            slices = slices_of(v)
            sums = taps_sum(
                slices,
                zs,
                lambda z, i, j, v=v: weighted(v, z, i * 3 + j),
            )
            for z in zs:
                for j in range(3):
                    old = totals[z][j]
                    totals[z][j] = sums[z][j] if old is None else old + sums[z][j]
        return totals

    def update(t, carry):
        for h in range(TILE // 128):
            cut = slice(h * 128, (h + 1) * 128)

            def slices_of(v):
                from_t = t if v < 2 else tiles - 1 - t
                return {
                    z: c[v][from_t, n * 16 : (n + 1) * 16, cut].astype(F32)
                    for n, z in enumerate(z3)
                }

            totals = numerator(slices_of, z2)
            for n, z in enumerate(z2):
                change = along_y(totals[z])
                before = frame_ref[t + 1, z * 16 : (z + 1) * 16, cut].astype(F32)
                u2[t + 1, n * 16 : (n + 1) * 16, cut] = (before * change).astype(BF)
                if z in z0:
                    k = z - frame.own
                    kept[t, k * 8 : (k + 1) * 8, cut] = change[:8]
        return carry

    lax.fori_loop(0, tiles, update, 0)

    rows1 = m2.shape[1]
    n2 = u2.shape[1]
    for v in range(2):
        for w in (v, v + 2):
            conv(u2, 0, tiles, n2, blocks_ref[forward_block(w)], c[w].at[:, :n2, :], 2)

        def ratios2(t, carry, v=v):
            for h in range(TILE // 128):
                cut = slice(h * 128, (h + 1) * 128)
                recips = []
                for w in (v, v + 2):
                    from_t = t if w < 2 else tiles - 1 - t
                    slices = {
                        z: c[w][from_t, n * 16 : (n + 1) * 16, cut].astype(F32)
                        for n, z in enumerate(z2)
                    }
                    sums = taps_sum(
                        slices, z1, lambda z, i, j, w=w: num_ref[w * 16 + i * 3 + j : w * 16 + i * 3 + j + 1, :]
                    )
                    recips.append(
                        {z: 1.0 / (along_y(sums[z]) + num_ref[w * 16 + 9 : w * 16 + 10, :]) for z in z1}
                    )
                for n, z in enumerate(z1):
                    m2[t + 1, n * 16 : (n + 1) * 16, cut] = mix(
                        v, t, z, cut, recips[0][z], recips[1][z]
                    )
            return carry

        lax.fori_loop(0, tiles, ratios2, 0)
        mine = tiles // 4
        for w in (v, v + 2):
            first = view * mine if w < 2 else tiles - (view + 1) * mine
            conv(m2, first, mine, rows1, blocks_ref[backward_block(w)], c[w].at[:, :rows1, :], 2)

    mine = tiles // 4
    for s in range(mine):
        for h in range(TILE // 128):
            cut = slice(h * 128, (h + 1) * 128)

            def slices_of(v):
                from_s = s if v < 2 else mine - 1 - s
                return {
                    z: c[v][from_s, n * 16 : (n + 1) * 16, cut].astype(F32)
                    for n, z in enumerate(z1)
                }

            totals = numerator(slices_of, z0)
            for z in z0:
                k = z - frame.own
                to = k + upside * (depth - 1 - 2 * k)
                lanes = slice(s * TILE + h * 128, s * TILE + (h + 1) * 128)
                first_change = kept[view * mine + s, k * 8 : (k + 1) * 8, cut]
                out_ref[to, :, lanes] = (
                    est_ref[to, :, lanes] * first_change * along_y(totals[z])[:8]
                )


def shards(
    pieces, piece_owner, piece_row, estimate, psf_x, stencil, background, bleach_table, bleach_index
):
    depth, height, chunk = estimate.shape
    width = pieces.shape[3]
    tiles = width // TILE
    slabs = lax.axis_size("gz")
    bands = lax.axis_size("gy")
    blocks = slabs * bands
    frame = Frame(slabs, depth)
    size = frame.size
    sides = tuple(frame.sent(1))
    vmem, smem = pltpu.VMEM, pltpu.SMEM
    params = pltpu.CompilerParams(vmem_limit_bytes=LIMIT)

    def stay(array):
        return pltpu.with_memory_space_constraint(array, pltpu.VMEM)

    def call(kernel, shapes, ins, outs, *args, scratch=()):
        args = [
            stay(x) if space is vmem else x
            for space, x in zip(ins, args)
        ]
        out = pl.pallas_call(
            kernel,
            out_shape=shapes,
            in_specs=whole(*ins),
            out_specs=whole(*outs) if isinstance(shapes, tuple) else whole(*outs)[0],
            scratch_shapes=list(scratch),
            compiler_params=params,
        )(*args)
        return out

    def resident(*dims, dtype=BF):
        return pltpu.VMEM(dims, dtype)

    mark = jax.ShapeDtypeStruct((8, 128), F32)

    free = pl.ANY
    area = depth * height

    pairs = blocks // 2
    half_cells = resident(pairs, depth, height, width)
    even, odd, payload = call(
        functools.partial(first_kernel, pairs, bands, frame.mirrored),
        (half_cells, half_cells, resident(area + 8, chunk)),
        (smem, smem, smem, vmem, vmem, vmem, vmem),
        (vmem, vmem, vmem),
        piece_owner.transpose(0, 2, 1),
        piece_row,
        background,
        pieces[0],
        stencil.transpose(1, 0, 2),
        estimate,
        psf_x,
        scratch=[vmem((blocks * depth, height, width), F32), vmem((8, chunk), F32)],
    )
    other = swap(odd, "gy", bands, 1)
    heard = [payload] + [swap(payload, "view", 4, mask) for mask in (1, 2, 3)]
    index_far = exchange_z(frame, lambda s: bleach_index[:, s.start : s.stop], slabs, depth)
    est_slices = frame.sent(depth)
    out = call(
        functools.partial(
            sum_kernel,
            pairs,
            [slice(s.start * height, s.stop * height) for s in est_slices.values()],
        ),
        (resident(depth, height, width),) * pairs
        + tuple(resident(4, len(s) * height, chunk) for s in est_slices.values())
        + (mark,),
        [vmem] * 6 + [free],
        [vmem] * (pairs + len(sides) + 1),
        even,
        other,
        *heard,
        index_far[sides[0]],
    )
    kept, est_stacks, sums_done = out[:pairs], out[pairs:-1], out[-1]
    moved = [swap(kept[k], ("gz", "gy"), blocks, 2 * k) for k in range(1, pairs)]

    def stack(arrays, slices, token):
        rows = slice(slices.start * height, slices.stop * height)
        dims = (len(arrays),) + arrays[0].shape[:-2] + (len(slices) * height, arrays[0].shape[-1])
        return call(
            functools.partial(stack_kernel, rows),
            (resident(*dims), mark),
            [vmem] * len(arrays) + [free],
            (vmem, vmem),
            *arrays,
            token,
        )

    def edges(arrays, fars, token, slices, dims):
        out = resident(4, *dims[:-2], slices, height // 2, dims[-1])
        return call(
            functools.partial(
                edges_kernel, height, depth if arrays else 0, len(sides)
            ),
            (out, out, mark),
            [vmem] * (len(arrays) + len(fars)) + [free],
            (vmem, vmem, vmem),
            *arrays,
            *fars,
            token,
        )

    stacks = dict(zip([(s.start, s.stop) for s in est_slices.values()], est_stacks))
    far_est = exchange_z(frame, lambda s: stacks[s.start, s.stop], slabs, depth)
    far_est = [far_est[s] for s in sides]
    table, nums, token = call(
        functools.partial(band_kernel, area),
        (resident(6, 3 * TILE, TILE), resident(64, 128, dtype=F32), mark),
        [vmem] * 4 + [free],
        (vmem, vmem, vmem),
        *heard,
        sums_done,
    )
    kept_table, kept_nums = table, nums
    est_edges = edges(heard, far_est, token, size, payload.shape)
    one_est, two_est = core_side(est_edges, bands, True)

    far_slices = frame.sent(3)
    plain, turned, *own_far, total_done = call(
        functools.partial(
            total_kernel,
            pairs,
            [slice(s.start * height, s.stop * height) for s in far_slices.values()],
        ),
        (resident(tiles, area, TILE), resident(tiles, area, TILE))
        + tuple(resident(1, tiles, len(s) * height, TILE) for s in far_slices.values())
        + (mark,),
        [vmem] * pairs + [free],
        [vmem] * (3 + len(sides)),
        kept[0],
        *moved,
        est_edges[2],
    )
    near = swap(plain, "view", 4, 1)
    opposite = swap(turned, "view", 4, 2)
    last = swap(opposite, "view", 4, 1)
    ready = dict(zip([(s.start, s.stop) for s in far_slices.values()], own_far))
    far_own = exchange_z(frame, lambda s: ready[s.start, s.stop], slabs, 3)
    far_own = [far_own[s] for s in sides]
    n3, n2, n1 = (len(frame.need(r)) * 16 for r in (3, 2, 1))

    scratch = [vmem((tiles, size * 16, TILE), BF)]
    est_frame, recip_a, token = call(
        functools.partial(start_kernel, frame, tiles, sides, (0, 1)),
        (
            resident(tiles + 2, size * 16, TILE),
            resident(2, tiles, n3, TILE),
            mark,
        ),
        [vmem] * (8 + len(sides)) + [free],
        (vmem, vmem, vmem),
        kept_nums,
        kept_table,
        *heard,
        *far_est,
        one_est,
        two_est,
        total_done,
        scratch=scratch,
    )
    tokens = []

    def others(slices):
        rows, done = stack((near, opposite, last), slices, token)
        tokens.append(done)
        return rows

    far_others = exchange_z(frame, others, slabs, 3)
    far_others = [far_others[s] for s in sides]
    own_edges = edges((plain, near, opposite, last), (), tokens[-1], depth, plain.shape)
    near_halo = core_side(own_edges, bands, False)
    recip_b, token_b = call(
        functools.partial(forward_kernel, frame, tiles, (2, 3)),
        (resident(2, tiles, n3, TILE), mark),
        (vmem, vmem, vmem, free),
        (vmem, vmem),
        kept_nums,
        kept_table,
        est_frame,
        own_edges[2],
        scratch=scratch,
    )
    far_edges = edges(
        (), far_own + far_others, token_b, len(frame.need(3)) - depth, plain.shape
    )
    far_halo = core_side(far_edges, bands, False)
    return call(
        functools.partial(main_kernel, frame, tiles, sides),
        jax.ShapeDtypeStruct(estimate.shape, F32),
        [smem] * (2 + len(sides)) + [vmem] * (14 + 2 * len(sides)),
        (vmem,),
        bleach_table,
        bleach_index,
        *[index_far[s] for s in sides],
        kept_nums,
        estimate,
        plain,
        near,
        opposite,
        last,
        *far_own,
        *far_others,
        *near_halo,
        *far_halo,
        recip_a,
        recip_b,
        kept_table,
        est_frame,
        scratch=[
            vmem((tiles + 2, n3, TILE), BF),
            vmem((tiles + 2, n2, TILE), BF),
            vmem((tiles + 2, n1, TILE), BF),
        ]
        + [vmem((tiles, n3, TILE), BF)] * 4
        + [vmem((tiles, area, TILE), F32), vmem((4 * size * 16, 128), F32)],
    )


def solution(mesh):
    placed = (
        P("view", ("gz", "gy"), None, None),
        P("view", ("gz", "gy"), None),
        P("view", ("gz", "gy")),
        P("gz", "gy", "view"),
        P("view", None),
        P("view", None, None),
        P("view"),
        P(),
        P(None, "gz"),
    )
    return jax.shard_map(
        shards, mesh=mesh, in_specs=placed, out_specs=P("gz", "gy", "view"), check_vma=False
    )
```

```python
import functools

import jax
import jax.numpy as jnp
from jax import lax
from jax.experimental import pallas as pl
from jax.experimental.pallas import tpu as pltpu
from jax.sharding import PartitionSpec as P

BF = jnp.bfloat16
F32 = jnp.float32
TILE = 256
LIMIT = 24 << 20


def whole(*spaces):
    return [pl.BlockSpec(memory_space=space) for space in spaces]


def swap(array, axis, size, mask):
    return lax.ppermute(array, axis, [(i, i ^ mask) for i in range(size)])


def core_side(own, bands, all_take_part):
    first = swap(own[0], "gy", bands, 1)
    if all_take_part:
        return first, swap(own[1], "gy", bands, 3)
    return first, lax.ppermute(own[1], "gy", [(1, 2), (2, 1)])


def upward(array, axis, size):
    return lax.ppermute(array, axis, [(i, i + 1) for i in range(size - 1)])


def downward(array, axis, size):
    return lax.ppermute(array, axis, [(i + 1, i) for i in range(size - 1)])


class Frame:
    def __init__(self, slabs, depth):
        self.mirrored = slabs == 2
        self.depth = depth
        self.own = 0 if self.mirrored else depth
        self.size = 2 * depth if self.mirrored else 3 * depth

    def need(self, radius):
        return range(
            max(0, self.own - radius), min(self.size, self.own + self.depth + radius)
        )

    def source(self, f):
        k = f - self.own
        if 0 <= k < self.depth:
            return "own", k
        if self.mirrored:
            return "up", 2 * self.depth - 1 - k
        return ("dn", f) if k < 0 else ("up", k - self.depth)

    def place(self, f, radius):
        where, k = self.source(f)
        at = 0
        for name, slices in [("own", range(self.depth))] + list(self.sent(radius).items()):
            if name == where:
                return at + k - slices.start
            at += len(slices)

    def sent(self, radius):
        if self.mirrored:
            return {"up": range(self.depth - radius, self.depth)}
        return {
            "dn": range(self.depth - radius, self.depth),
            "up": range(0, radius),
        }


def exchange_z(frame, make, slabs, radius):
    got = {}
    for side, slices in frame.sent(radius).items():
        payload = make(slices)
        if frame.mirrored:
            got[side] = swap(payload, "gz", slabs, 1)
        elif side == "dn":
            got[side] = upward(payload, "gz", slabs)
        else:
            got[side] = downward(payload, "gz", slabs)
    return got


def place():
    return lax.axis_index("view"), lax.axis_index("gz")


def first_kernel(
    pairs,
    bands,
    mirrored,
    owner_ref,
    row_ref,
    bg_ref,
    pieces_ref,
    taps_ref,
    est_ref,
    psf_ref,
    even_ref,
    odd_ref,
    payload_ref,
    acc,
    tail,
):
    write_payload(mirrored, bg_ref, taps_ref, est_ref, psf_ref, payload_ref, tail)
    count = pieces_ref.shape[0]
    depth = even_ref.shape[1]
    me = lax.axis_index("gz") * bands + lax.axis_index("gy")

    def clear(i, carry):
        acc[i] = jnp.zeros(acc.shape[1:], F32)
        return carry

    lax.fori_loop(0, acc.shape[0], clear, 0)

    def add(i, carry):
        owner = owner_ref[0, 0, i]
        row = row_ref[0, i]
        if mirrored:
            row = jnp.where(owner >= bands, depth - 1 - row, row)
        c = (owner ^ me) * depth + row
        acc[c] = acc[c] + pieces_ref[i].astype(F32)
        return carry

    lax.fori_loop(0, count, add, 0)

    def put(pair, carry):
        for f in range(depth):
            even_ref[pair, f] = acc[pair * 2 * depth + f].astype(BF)
            odd_ref[pair, f] = acc[(pair * 2 + 1) * depth + f].astype(BF)
        return carry

    lax.fori_loop(0, pairs, put, 0)


def write_payload(mirrored, bg_ref, taps_ref, est_ref, psf_ref, out_ref, tail):
    depth, height = est_ref.shape[:2]
    upside = lax.axis_index("gz") if mirrored else 0
    for k in range(depth):
        out_ref[k * height : (k + 1) * height, :] = est_ref[
            k + upside * (depth - 1 - 2 * k)
        ].astype(BF)
    tail[...] = jnp.zeros(tail.shape, F32)
    for i in range(3):
        tail[0:1, 3 * i : 3 * i + 3] = taps_ref[i + upside * (2 - 2 * i)]
    lanes = lax.broadcasted_iota(jnp.int32, (1, 128), 1)
    exact = jnp.where(lanes == 9, bg_ref[0], tail[0:1, :128])
    for n in range(3):
        part = exact.astype(BF).astype(F32)
        tail[n + 1 : n + 2, :128] = part
        exact = exact - part
    tail[0:1, : psf_ref.shape[1]] = psf_ref[...]
    out_ref[depth * height :, :] = tail[...].astype(BF)


def numbers_of(heard, at):
    rows = heard[at : at + 8, :128].astype(F32)
    exact = rows[1:2] + rows[2:3] + rows[3:4]
    wide = jnp.broadcast_to(exact, (16, 128))
    spot = lax.broadcasted_iota(jnp.int32, (16, 128), 0) == lax.broadcasted_iota(
        jnp.int32, (16, 128), 1
    )
    column = jnp.sum(jnp.where(spot, wide, 0.0), axis=1, keepdims=True)
    return jnp.broadcast_to(column, (16, 128))


def sum_kernel(pairs, parts, *refs):
    even_ref, other_ref = refs[:2]
    heard = refs[2:6]
    sums, stacks, done_ref = refs[6 : 6 + pairs], refs[6 + pairs : -1], refs[-1]
    done_ref[...] = jnp.zeros(done_ref.shape, F32)
    for k in range(pairs):
        sums[k][...] = (even_ref[k].astype(F32) + other_ref[k].astype(F32)).astype(BF)
    for rows, ref in zip(parts, stacks):
        for v in range(4):
            ref[v] = heard[v][rows, :]


def stack_kernel(rows, count, *refs):
    ins, (out_ref, done_ref) = refs[:count], refs[-2:]
    done_ref[...] = jnp.zeros(done_ref.shape, F32)
    for v, ref in enumerate(ins):
        out_ref[v] = ref[..., rows, :]


def edges_kernel(height, depth, sides, *refs):
    out1, out2, done_ref = refs[-3:]
    done_ref[...] = jnp.zeros(done_ref.shape, F32)
    count = out1.shape[0]
    views = refs[:count] if depth else [None] * count
    fars = refs[count if depth else 0 : -4]
    half = height // 2
    gy = lax.axis_index("gy")
    even = gy % 2 == 0
    inner = (gy == 1) | (gy == 2)
    lead = out1.shape[1:-3]

    def put(at, block):
        turned = pltpu.roll(block, half, block.ndim - 2)
        one = jnp.where(even, turned, block)
        two = jnp.where(inner, jnp.where(even, block, turned), 0.0)
        out1[at] = one[..., :half, :].astype(BF)
        out2[at] = two[..., :half, :].astype(BF)

    def far_of(v, side):
        for ref in fars[side::sides]:
            if v < ref.shape[0]:
                return ref.at[v]
            v -= ref.shape[0]

    for v, own in enumerate(views):
        n = 0
        sources = [(depth, own)] if depth else []
        if fars:
            sources += [
                (fars[side].shape[-2] // height, far_of(v, side)) for side in range(sides)
            ]
        for number, source in sources:
            for k in range(number):
                rows = slice(k * height, (k + 1) * height)
                if lead:

                    def one_tile(t, carry, v=v, n=n, source=source, rows=rows):
                        put((v, t, n), source[t, rows, :].astype(F32))
                        return carry

                    lax.fori_loop(0, lead[0], one_tile, 0, unroll=True)
                else:
                    put((v, n), source[rows, :].astype(F32))
                n += 1


def beside(even, one, two):
    one, two = one.astype(F32), two.astype(F32)
    return jnp.where(
        even, jnp.concatenate([one, two], axis=0), jnp.concatenate([two, one], axis=0)
    )


def reversal():
    rows = lax.broadcasted_iota(jnp.int32, (TILE, TILE), 0)
    cols = lax.broadcasted_iota(jnp.int32, (TILE, TILE), 1)
    return jnp.where(rows + cols == TILE - 1, F32(1.0), F32(0.0)).astype(BF)


def total_kernel(parts, far_rows, *refs):
    ins, (out_ref, rev_ref, *far_refs, done_ref) = refs[:parts], refs[parts + 1 :]
    done_ref[...] = jnp.zeros(done_ref.shape, F32)
    tiles, rows, _ = out_ref.shape
    for t in range(tiles):
        cut = slice(t * TILE, (t + 1) * TILE)
        acc = ins[0][:, :, cut].astype(F32)
        for ref in ins[1:]:
            acc = acc + ref[:, :, cut].astype(F32)
        block = acc.reshape(rows, TILE).astype(BF)
        out_ref[t] = block
        for ref, part in zip(far_refs, far_rows):
            ref[0, t] = block[part]
    back = jnp.dot(
        out_ref[...].reshape(tiles * rows, TILE), reversal(), preferred_element_type=F32
    ).astype(BF)
    for t in range(tiles):
        rev_ref[tiles - 1 - t] = back[t * rows : (t + 1) * rows]


def band_kernel(at, *refs):
    heard, (out_ref, num_ref, done_ref) = refs[:4], refs[5:]
    done_ref[...] = jnp.zeros(done_ref.shape, F32)
    for v in range(4):
        num_ref[v * 16 : (v + 1) * 16, :] = numbers_of(heard[v], at)
    flip = reversal()
    for v in range(4):
        row = heard[v][at : at + 8, : 3 * 128].astype(F32)[0:1]
        edge = TILE // 2
        base = jnp.concatenate(
            [jnp.zeros((1, edge), F32), row, jnp.zeros((1, 2 * edge), F32)], axis=1
        )
        wide = pltpu.roll(
            jnp.broadcast_to(base, (TILE, 3 * TILE)), 0, 1, stride=1, stride_axis=0
        ).astype(BF)
        turned = jnp.dot(flip, wide, preferred_element_type=F32).astype(BF)
        half = TILE // 2
        for k, (rows, to) in enumerate(
            (
                (slice(half, TILE), slice(0, half)),
                (slice(0, TILE), slice(half, half + TILE)),
                (slice(0, half), slice(half + TILE, 2 * TILE)),
            )
        ):
            cut = slice(k * TILE, (k + 1) * TILE)
            across = slice((2 - k) * TILE, (3 - k) * TILE)
            if v >= 2:
                out_ref[2 + v, to, :] = turned[rows, cut]
            else:
                out_ref[2 + v, to, :] = wide[rows, across]
                out_ref[v, to, :] = jnp.dot(
                    turned[rows, cut], flip, preferred_element_type=F32
                ).astype(BF)


def forward_block(v):
    return v if v < 2 else v + 2


def backward_block(v):
    return v + 2


def conv(src, first, tiles, rows, blocks, dst, step):
    half = TILE // 2
    s = 0
    while s < tiles:
        n = min(step, tiles - s)
        lhs = jnp.concatenate(
            [
                src[pl.ds(first + s + k, n), :, cut].reshape(n * rows, cut.stop - cut.start)
                for k, cut in enumerate(
                    (slice(half, TILE), slice(0, TILE), slice(0, half))
                )
            ],
            axis=1,
        )
        out = jnp.dot(lhs, blocks, preferred_element_type=F32).astype(BF)
        dst[s : s + n] = out.reshape(n, rows, TILE)
        s += n


def taps_sum(slices, zs, taps):
    result = {}
    for z in zs:
        sums = [None, None, None]
        for j in range(3):
            for i in range(3):
                at = z + i - 1
                if at in slices:
                    term = taps(z, i, j) * slices[at]
                    sums[j] = term if sums[j] is None else sums[j] + term
        result[z] = sums
    return result


def along_y(sums):
    n = sums[0].shape[0]
    return pltpu.roll(sums[0], 1, 0) + sums[1] + pltpu.roll(sums[2], n - 1, 0)


def write_frame(frame, tiles, sides, *refs):
    own_refs, refs = refs[:4], refs[4:]
    side_refs = dict(zip(sides, refs[: len(sides)]))
    one_ref, two_ref, out_ref = refs[len(sides) :]
    view = lax.axis_index("view")
    even = lax.axis_index("gy") % 2 == 0
    for e in (0, tiles + 1):
        out_ref[e] = jnp.zeros(out_ref.shape[1:], BF)
    for v in range(4):
        for s in range(tiles // 4):
            t = (view ^ v) * (tiles // 4) + s + 1
            cut = slice(s * TILE, (s + 1) * TILE)
            for f in range(frame.size):
                where, k = frame.source(f)
                rows = slice(k * 8, (k + 1) * 8)
                if where == "own":
                    own = own_refs[v][rows, cut]
                else:
                    own = side_refs[where][v, rows, cut]
                n = frame.place(f, frame.depth)
                out_ref[t, f * 16 : (f + 1) * 16, :] = jnp.concatenate(
                    [
                        own.astype(F32),
                        beside(even, one_ref[v, n, :, cut], two_ref[v, n, :, cut]),
                    ],
                    axis=0,
                ).astype(BF)


def start_kernel(frame, tiles, sides, views, num_ref, blocks_ref, *refs):
    count = len(sides)
    out_ref, recip_ref, done_ref, c = refs[7 + count :]
    write_frame(frame, tiles, sides, *refs[: 6 + count], out_ref)
    forward_views(frame, tiles, views, num_ref, blocks_ref, out_ref, recip_ref, c)
    done_ref[...] = jnp.zeros(done_ref.shape, F32)


def forward_kernel(frame, tiles, views, num_ref, blocks_ref, frame_ref, _, recip_ref, done_ref, c):
    forward_views(frame, tiles, views, num_ref, blocks_ref, frame_ref, recip_ref, c)
    done_ref[...] = jnp.zeros(done_ref.shape, F32)


def forward_views(frame, tiles, views, num_ref, blocks_ref, frame_ref, recip_ref, c):
    size = frame.size
    zs = frame.need(3)
    for at, v in enumerate(views):
        conv(frame_ref, 0, tiles, size * 16, blocks_ref[forward_block(v)], c, 2)

        def divide(t, carry, v=v, at=at):
            from_t = t if v < 2 else tiles - 1 - t
            for h in range(TILE // 128):
                cut = slice(h * 128, (h + 1) * 128)
                slices = {
                    f: c[from_t, f * 16 : (f + 1) * 16, cut].astype(F32)
                    for f in range(size)
                }
                sums = taps_sum(slices, zs, lambda z, i, j: num_ref[v * 16 + i * 3 + j : v * 16 + i * 3 + j + 1, :])
                for n, z in enumerate(zs):
                    recip_ref[at, t, n * 16 : (n + 1) * 16, cut] = (
                        1.0 / (along_y(sums[z]) + num_ref[v * 16 + 9 : v * 16 + 10, :])
                    ).astype(BF)
            return carry

        lax.fori_loop(0, tiles, divide, 0)


def main_kernel(frame, tiles, sides, table_ref, *refs):
    count = len(sides)
    index_refs, refs = refs[: count + 1], refs[count + 1 :]
    num_ref, est_ref, refs = refs[0], refs[1], refs[2:]
    own_refs, refs = refs[:4], refs[4:]
    far_refs, refs = refs[: 2 * count], refs[2 * count :]
    near_refs, beyond_refs = refs[:2], refs[2:4]
    recip_refs = refs[4:6]
    blocks_ref, frame_ref, out_ref = refs[6:9]
    m1, u2, m2, c0, c1, c2, c3, kept, wt = refs[9:]
    even = lax.axis_index("gy") % 2 == 0
    c = [c0, c1, c2, c3]
    view = lax.axis_index("view")
    upside = lax.axis_index("gz") if frame.mirrored else 0
    depth = frame.depth
    z3, z2, z1, z0 = (frame.need(r) for r in (3, 2, 1, 0))
    sent = frame.sent(3)

    for f in z2:
        where, k = frame.source(f)
        index_ref = index_refs[0 if where == "own" else 1 + sides.index(where)]
        over = upside if where == "own" else 1 - upside
        raw = k + over * (depth - 1 - 2 * k) if frame.mirrored else k
        weights = [
            jnp.full((16, 128), table_ref[v, index_ref[v, raw]], F32) for v in range(4)
        ]
        total = (weights[0] + weights[1]) + (weights[2] + weights[3])
        for v in range(4):
            mine = jnp.full(
                (16, 128), table_ref[view ^ v, index_ref[view ^ v, raw]], F32
            )
            at = (v * frame.size + f) * 16
            wt[at : at + 16, :] = num_ref[v * 16 : (v + 1) * 16, :] * (mine / total)

    def weighted(v, z, n):
        at = (v * frame.size + z) * 16 + 8 - n
        return wt[at : at + 1, :]

    def measured(v, t, z, cut):
        where, k = frame.source(z)
        if where == "own":
            own = own_refs[v][t, k * 8 : (k + 1) * 8, cut]
        else:
            k = k - sent[where].start
            far = far_refs[(count if v else 0) + sides.index(where)]
            own = far[v - 1 if v else 0, t, k * 8 : (k + 1) * 8, cut]
        n = frame.place(z, 3)
        one_ref, two_ref = near_refs if n < depth else beyond_refs
        n = n if n < depth else n - depth
        return jnp.concatenate(
            [
                own.astype(F32),
                beside(
                    even,
                    one_ref[v, t, n, :, cut],
                    two_ref[v, t, n, :, cut],
                ),
            ],
            axis=0,
        )

    def mix(v, t, z, cut, recip_a, recip_b):
        a = (measured(v, t, z, cut) * recip_a).astype(BF).astype(F32)
        b = (measured(v + 2, t, z, cut) * recip_b).astype(BF).astype(F32)
        return (0.5 * (a + b)).astype(BF)

    def zero_ends(ref):
        for e in (0, ref.shape[0] - 1):
            ref[e] = jnp.zeros(ref.shape[1:], BF)

    for ref in (m1, u2, m2):
        zero_ends(ref)

    for v in range(2):

        def ratios(t, carry, v=v):
            for h in range(TILE // 128):
                cut = slice(h * 128, (h + 1) * 128)
                for n, z in enumerate(z3):
                    at = slice(n * 16, (n + 1) * 16)
                    m1[t + 1, at, cut] = mix(
                        v,
                        t,
                        z,
                        cut,
                        recip_refs[0][v, t, at, cut].astype(F32),
                        recip_refs[1][v, t, at, cut].astype(F32),
                    )
            return carry

        lax.fori_loop(0, tiles, ratios, 0)
        for w in (v, v + 2):
            conv(m1, 0, tiles, m1.shape[1], blocks_ref[backward_block(w)], c[w], 2)

    def numerator(slices_of, zs):
        totals = {z: [None, None, None] for z in zs}
        for v in range(4):
            slices = slices_of(v)
            sums = taps_sum(
                slices,
                zs,
                lambda z, i, j, v=v: weighted(v, z, i * 3 + j),
            )
            for z in zs:
                for j in range(3):
                    old = totals[z][j]
                    totals[z][j] = sums[z][j] if old is None else old + sums[z][j]
        return totals

    def update(t, carry):
        for h in range(TILE // 128):
            cut = slice(h * 128, (h + 1) * 128)

            def slices_of(v):
                from_t = t if v < 2 else tiles - 1 - t
                return {
                    z: c[v][from_t, n * 16 : (n + 1) * 16, cut].astype(F32)
                    for n, z in enumerate(z3)
                }

            totals = numerator(slices_of, z2)
            for n, z in enumerate(z2):
                change = along_y(totals[z])
                before = frame_ref[t + 1, z * 16 : (z + 1) * 16, cut].astype(F32)
                u2[t + 1, n * 16 : (n + 1) * 16, cut] = (before * change).astype(BF)
                if z in z0:
                    k = z - frame.own
                    kept[t, k * 8 : (k + 1) * 8, cut] = change[:8]
        return carry

    lax.fori_loop(0, tiles, update, 0)

    rows1 = m2.shape[1]
    n2 = u2.shape[1]
    for v in range(2):
        for w in (v, v + 2):
            conv(u2, 0, tiles, n2, blocks_ref[forward_block(w)], c[w].at[:, :n2, :], 2)

        def ratios2(t, carry, v=v):
            for h in range(TILE // 128):
                cut = slice(h * 128, (h + 1) * 128)
                recips = []
                for w in (v, v + 2):
                    from_t = t if w < 2 else tiles - 1 - t
                    slices = {
                        z: c[w][from_t, n * 16 : (n + 1) * 16, cut].astype(F32)
                        for n, z in enumerate(z2)
                    }
                    sums = taps_sum(
                        slices, z1, lambda z, i, j, w=w: num_ref[w * 16 + i * 3 + j : w * 16 + i * 3 + j + 1, :]
                    )
                    recips.append(
                        {z: 1.0 / (along_y(sums[z]) + num_ref[w * 16 + 9 : w * 16 + 10, :]) for z in z1}
                    )
                for n, z in enumerate(z1):
                    m2[t + 1, n * 16 : (n + 1) * 16, cut] = mix(
                        v, t, z, cut, recips[0][z], recips[1][z]
                    )
            return carry

        lax.fori_loop(0, tiles, ratios2, 0)
        mine = tiles // 4
        for w in (v, v + 2):
            first = view * mine if w < 2 else tiles - (view + 1) * mine
            conv(m2, first, mine, rows1, blocks_ref[backward_block(w)], c[w].at[:, :rows1, :], 2)

    mine = tiles // 4
    for s in range(mine):
        for h in range(TILE // 128):
            cut = slice(h * 128, (h + 1) * 128)

            def slices_of(v):
                from_s = s if v < 2 else mine - 1 - s
                return {
                    z: c[v][from_s, n * 16 : (n + 1) * 16, cut].astype(F32)
                    for n, z in enumerate(z1)
                }

            totals = numerator(slices_of, z0)
            for z in z0:
                k = z - frame.own
                to = k + upside * (depth - 1 - 2 * k)
                lanes = slice(s * TILE + h * 128, s * TILE + (h + 1) * 128)
                first_change = kept[view * mine + s, k * 8 : (k + 1) * 8, cut]
                out_ref[to, :, lanes] = (
                    est_ref[to, :, lanes] * first_change * along_y(totals[z])[:8]
                )


def shards(
    pieces, piece_owner, piece_row, estimate, psf_x, stencil, background, bleach_table, bleach_index
):
    depth, height, chunk = estimate.shape
    width = pieces.shape[3]
    tiles = width // TILE
    slabs = lax.axis_size("gz")
    bands = lax.axis_size("gy")
    blocks = slabs * bands
    frame = Frame(slabs, depth)
    size = frame.size
    sides = tuple(frame.sent(1))
    vmem, smem = pltpu.VMEM, pltpu.SMEM
    params = pltpu.CompilerParams(vmem_limit_bytes=LIMIT)

    def stay(array):
        return pltpu.with_memory_space_constraint(array, pltpu.VMEM)

    given = [piece_row, estimate, psf_x, bleach_table]
    given += [pieces[0], stencil.transpose(1, 0, 2), piece_owner.transpose(0, 2, 1)]
    first_pieces, first_taps, first_owner = given[-3:]

    def is_given(x):
        return any(x is y for y in given)

    def call(kernel, shapes, ins, outs, *args, scratch=()):
        args = [
            (
                pltpu.with_memory_space_constraint(x, pltpu.HBM)
                if is_given(x)
                else stay(x)
                if space is vmem
                else x
            )
            for space, x in zip(ins, args)
        ]
        out = pl.pallas_call(
            kernel,
            out_shape=shapes,
            in_specs=whole(*ins),
            out_specs=whole(*outs) if isinstance(shapes, tuple) else whole(*outs)[0],
            scratch_shapes=list(scratch),
            compiler_params=params,
        )(*args)
        return out

    def resident(*dims, dtype=BF):
        return pltpu.VMEM(dims, dtype)

    mark = jax.ShapeDtypeStruct((8, 128), F32)

    free = pl.ANY
    area = depth * height

    pairs = blocks // 2
    half_cells = resident(pairs, depth, height, width)
    even, odd, payload = call(
        functools.partial(first_kernel, pairs, bands, frame.mirrored),
        (half_cells, half_cells, resident(area + 8, chunk)),
        (smem, smem, smem, vmem, vmem, vmem, vmem),
        (vmem, vmem, vmem),
        first_owner,
        piece_row,
        background,
        first_pieces,
        first_taps,
        estimate,
        psf_x,
        scratch=[vmem((blocks * depth, height, width), F32), vmem((8, chunk), F32)],
    )
    other = swap(odd, "gy", bands, 1)
    heard = [payload] + [swap(payload, "view", 4, mask) for mask in (1, 2, 3)]
    index_far = exchange_z(frame, lambda s: bleach_index[:, s.start : s.stop], slabs, depth)
    est_slices = frame.sent(depth)
    out = call(
        functools.partial(
            sum_kernel,
            pairs,
            [slice(s.start * height, s.stop * height) for s in est_slices.values()],
        ),
        (resident(depth, height, width),) * pairs
        + tuple(resident(4, len(s) * height, chunk) for s in est_slices.values())
        + (mark,),
        [vmem] * 6,
        [vmem] * (pairs + len(sides) + 1),
        even,
        other,
        *heard,
    )
    kept, est_stacks, sums_done = out[:pairs], out[pairs:-1], out[-1]
    moved = [swap(kept[k], ("gz", "gy"), blocks, 2 * k) for k in range(1, pairs)]

    def stack(arrays, slices, *tokens):
        rows = slice(slices.start * height, slices.stop * height)
        dims = (len(arrays),) + arrays[0].shape[:-2] + (len(slices) * height, arrays[0].shape[-1])
        return call(
            functools.partial(stack_kernel, rows, len(arrays)),
            (resident(*dims), mark),
            [vmem] * len(arrays) + [free] + [vmem] * (len(tokens) - 1),
            (vmem, vmem),
            *arrays,
            *tokens,
        )

    def edges(arrays, fars, token, slices, dims):
        out = resident(4, *dims[:-2], slices, height // 2, dims[-1])
        return call(
            functools.partial(
                edges_kernel, height, depth if arrays else 0, len(sides)
            ),
            (out, out, mark),
            [vmem] * (len(arrays) + len(fars)) + [free],
            (vmem, vmem, vmem),
            *arrays,
            *fars,
            token,
        )

    stacks = dict(zip([(s.start, s.stop) for s in est_slices.values()], est_stacks))
    far_est = exchange_z(frame, lambda s: stacks[s.start, s.stop], slabs, depth)
    far_est = [far_est[s] for s in sides]
    table, nums, token = call(
        functools.partial(band_kernel, area),
        (resident(6, 2 * TILE, TILE), resident(64, 128, dtype=F32), mark),
        [vmem] * 4 + [free],
        (vmem, vmem, vmem),
        *heard,
        sums_done,
    )
    kept_table, kept_nums = table, nums
    est_edges = edges(heard, far_est, token, size, payload.shape)
    one_est, two_est = core_side(est_edges, bands, True)

    far_slices = frame.sent(3)
    plain, turned, *own_far, total_done = call(
        functools.partial(
            total_kernel,
            pairs,
            [slice(s.start * height, s.stop * height) for s in far_slices.values()],
        ),
        (resident(tiles, area, TILE), resident(tiles, area, TILE))
        + tuple(resident(1, tiles, len(s) * height, TILE) for s in far_slices.values())
        + (mark,),
        [vmem] * pairs + [free],
        [vmem] * (3 + len(sides)),
        kept[0],
        *moved,
        est_edges[2],
    )
    near = swap(plain, "view", 4, 1)
    opposite = swap(turned, "view", 4, 2)
    last = swap(opposite, "view", 4, 1)
    ready = dict(zip([(s.start, s.stop) for s in far_slices.values()], own_far))
    far_own = exchange_z(frame, lambda s: ready[s.start, s.stop], slabs, 3)
    far_own = [far_own[s] for s in sides]
    n3, n2, n1 = (len(frame.need(r)) * 16 for r in (3, 2, 1))

    scratch = [vmem((tiles, size * 16, TILE), BF)]
    tokens = []

    def others(slices):
        rows, done = stack(
            (near, opposite, last), slices, index_far[sides[0]], one_est, two_est
        )
        tokens.append(done)
        return rows

    far_others = exchange_z(frame, others, slabs, 3)
    far_others = [far_others[s] for s in sides]
    own_edges = edges((plain, near, opposite, last), (), tokens[-1], depth, plain.shape)
    near_halo = core_side(own_edges, bands, False)
    est_frame, recip_a, token = call(
        functools.partial(start_kernel, frame, tiles, sides, (0, 1)),
        (
            resident(tiles + 2, size * 16, TILE),
            resident(2, tiles, n3, TILE),
            mark,
        ),
        [vmem] * (8 + len(sides)) + [free],
        (vmem, vmem, vmem),
        kept_nums,
        kept_table,
        *heard,
        *far_est,
        one_est,
        two_est,
        own_edges[2],
        scratch=scratch,
    )
    far_edges = edges(
        (), far_own + far_others, token, len(frame.need(3)) - depth, plain.shape
    )
    far_halo = core_side(far_edges, bands, False)
    recip_b, token_b = call(
        functools.partial(forward_kernel, frame, tiles, (2, 3)),
        (resident(2, tiles, n3, TILE), mark),
        (vmem, vmem, vmem, free),
        (vmem, vmem),
        kept_nums,
        kept_table,
        est_frame,
        far_edges[2],
        scratch=scratch,
    )
    return call(
        functools.partial(main_kernel, frame, tiles, sides),
        jax.ShapeDtypeStruct(estimate.shape, F32),
        [smem] * (2 + len(sides)) + [vmem] * (14 + 2 * len(sides)),
        (vmem,),
        bleach_table,
        bleach_index,
        *[index_far[s] for s in sides],
        kept_nums,
        estimate,
        plain,
        near,
        opposite,
        last,
        *far_own,
        *far_others,
        *near_halo,
        *far_halo,
        recip_a,
        recip_b,
        kept_table,
        est_frame,
        scratch=[
            vmem((tiles + 2, n3, TILE), BF),
            vmem((tiles + 2, n2, TILE), BF),
            vmem((tiles + 2, n1, TILE), BF),
        ]
        + [vmem((tiles, n3, TILE), BF)] * 4
        + [vmem((tiles, area, TILE), F32), vmem((4 * size * 16, 128), F32)],
    )


def solution(mesh):
    placed = (
        P("view", ("gz", "gy"), None, None),
        P("view", ("gz", "gy"), None),
        P("view", ("gz", "gy")),
        P("gz", "gy", "view"),
        P("view", None),
        P("view", None, None),
        P("view"),
        P(),
        P(None, "gz"),
    )
    return jax.shard_map(
        shards, mesh=mesh, in_specs=placed, out_specs=P("gz", "gy", "view"), check_vma=False
    )
```

```python
import functools

import jax
import jax.numpy as jnp
from jax import lax
from jax.experimental import pallas as pl
from jax.experimental.pallas import tpu as pltpu
from jax.sharding import PartitionSpec as P

BF = jnp.bfloat16
F32 = jnp.float32
TILE = 256
LIMIT = 24 << 20


def whole(*spaces):
    return [pl.BlockSpec(memory_space=space) for space in spaces]


def swap(array, axis, size, mask):
    return lax.ppermute(array, axis, [(i, i ^ mask) for i in range(size)])


def core_side(own, bands, all_take_part):
    first = swap(own[0], "gy", bands, 1)
    if all_take_part:
        return first, swap(own[1], "gy", bands, 3)
    return first, lax.ppermute(own[1], "gy", [(1, 2), (2, 1)])


def upward(array, axis, size):
    return lax.ppermute(array, axis, [(i, i + 1) for i in range(size - 1)])


def downward(array, axis, size):
    return lax.ppermute(array, axis, [(i + 1, i) for i in range(size - 1)])


class Frame:
    def __init__(self, slabs, depth):
        self.mirrored = slabs == 2
        self.depth = depth
        self.own = 0 if self.mirrored else depth
        self.size = 2 * depth if self.mirrored else 3 * depth

    def need(self, radius):
        return range(
            max(0, self.own - radius), min(self.size, self.own + self.depth + radius)
        )

    def source(self, f):
        k = f - self.own
        if 0 <= k < self.depth:
            return "own", k
        if self.mirrored:
            return "up", 2 * self.depth - 1 - k
        return ("dn", f) if k < 0 else ("up", k - self.depth)

    def place(self, f, radius):
        where, k = self.source(f)
        at = 0
        for name, slices in [("own", range(self.depth))] + list(self.sent(radius).items()):
            if name == where:
                return at + k - slices.start
            at += len(slices)

    def sent(self, radius):
        if self.mirrored:
            return {"up": range(self.depth - radius, self.depth)}
        return {
            "dn": range(self.depth - radius, self.depth),
            "up": range(0, radius),
        }


def exchange_z(frame, make, slabs, radius):
    got = {}
    for side, slices in frame.sent(radius).items():
        payload = make(slices)
        if frame.mirrored:
            got[side] = swap(payload, "gz", slabs, 1)
        elif side == "dn":
            got[side] = upward(payload, "gz", slabs)
        else:
            got[side] = downward(payload, "gz", slabs)
    return got


def place():
    return lax.axis_index("view"), lax.axis_index("gz")


def first_kernel(
    pairs,
    bands,
    mirrored,
    owner_ref,
    row_ref,
    bg_ref,
    pieces_ref,
    taps_ref,
    est_ref,
    psf_ref,
    even_ref,
    odd_ref,
    payload_ref,
    acc,
    tail,
):
    write_payload(mirrored, bg_ref, taps_ref, est_ref, psf_ref, payload_ref, tail)
    count = pieces_ref.shape[0]
    depth = even_ref.shape[1]
    me = lax.axis_index("gz") * bands + lax.axis_index("gy")

    def clear(i, carry):
        acc[i] = jnp.zeros(acc.shape[1:], F32)
        return carry

    lax.fori_loop(0, acc.shape[0], clear, 0)

    def add(i, carry):
        owner = owner_ref[0, 0, i]
        row = row_ref[0, i]
        if mirrored:
            row = jnp.where(owner >= bands, depth - 1 - row, row)
        c = (owner ^ me) * depth + row
        acc[c] = acc[c] + pieces_ref[i].astype(F32)
        return carry

    lax.fori_loop(0, count, add, 0)

    def put(pair, carry):
        for f in range(depth):
            even_ref[pair, f] = acc[pair * 2 * depth + f].astype(BF)
            odd_ref[pair, f] = acc[(pair * 2 + 1) * depth + f].astype(BF)
        return carry

    lax.fori_loop(0, pairs, put, 0)


def write_payload(mirrored, bg_ref, taps_ref, est_ref, psf_ref, out_ref, tail):
    depth, height = est_ref.shape[:2]
    upside = lax.axis_index("gz") if mirrored else 0
    for k in range(depth):
        out_ref[k * height : (k + 1) * height, :] = est_ref[
            k + upside * (depth - 1 - 2 * k)
        ].astype(BF)
    tail[...] = jnp.zeros(tail.shape, F32)
    for i in range(3):
        tail[0:1, 3 * i : 3 * i + 3] = taps_ref[i + upside * (2 - 2 * i)]
    lanes = lax.broadcasted_iota(jnp.int32, (1, 128), 1)
    exact = jnp.where(lanes == 9, bg_ref[0], tail[0:1, :128])
    for n in range(3):
        part = exact.astype(BF).astype(F32)
        tail[n + 1 : n + 2, :128] = part
        exact = exact - part
    tail[0:1, : psf_ref.shape[1]] = psf_ref[...]
    out_ref[depth * height :, :] = tail[...].astype(BF)


def numbers_of(heard, at):
    rows = heard[at : at + 8, :128].astype(F32)
    exact = rows[1:2] + rows[2:3] + rows[3:4]
    wide = jnp.broadcast_to(exact, (16, 128))
    spot = lax.broadcasted_iota(jnp.int32, (16, 128), 0) == lax.broadcasted_iota(
        jnp.int32, (16, 128), 1
    )
    column = jnp.sum(jnp.where(spot, wide, 0.0), axis=1, keepdims=True)
    return jnp.broadcast_to(column, (16, 128))


def sum_kernel(pairs, *refs):
    even_ref, other_ref, own_ref, near_ref, _ = refs[:5]
    sums, (pair_ref, done_ref) = refs[5 : 5 + pairs], refs[5 + pairs :]
    done_ref[...] = jnp.zeros(done_ref.shape, F32)
    for k in range(pairs):
        sums[k][...] = (even_ref[k].astype(F32) + other_ref[k].astype(F32)).astype(BF)
    pair_ref[0] = own_ref[...]
    pair_ref[1] = near_ref[...]


def views_of(first, second):
    return [first.at[0], first.at[1], second.at[0], second.at[1]]


def est_rows_kernel(rows, first, second, _, out_ref):
    for v, ref in enumerate(views_of(first, second)):
        out_ref[v] = ref[rows, :]


def stack_kernel(rows, count, *refs):
    ins, (out_ref, done_ref) = refs[:count], refs[-2:]
    done_ref[...] = jnp.zeros(done_ref.shape, F32)
    for v, ref in enumerate(ins):
        out_ref[v] = ref[..., rows, :]


def edges_kernel(height, depth, sides, paired, *refs):
    out1, out2, done_ref = refs[-3:]
    done_ref[...] = jnp.zeros(done_ref.shape, F32)
    count = out1.shape[0]
    views = refs[:count] if depth else [None] * count
    fars = refs[count if depth else 0 : -4]
    if paired:
        views, fars = views_of(*refs[:2]), refs[2:-4]
    half = height // 2
    gy = lax.axis_index("gy")
    even = gy % 2 == 0
    inner = (gy == 1) | (gy == 2)
    lead = out1.shape[1:-3]

    def put(at, block):
        turned = pltpu.roll(block, half, block.ndim - 2)
        one = jnp.where(even, turned, block)
        two = jnp.where(inner, jnp.where(even, block, turned), 0.0)
        out1[at] = one[..., :half, :].astype(BF)
        out2[at] = two[..., :half, :].astype(BF)

    def far_of(v, side):
        for ref in fars[side::sides]:
            if v < ref.shape[0]:
                return ref.at[v]
            v -= ref.shape[0]

    for v, own in enumerate(views):
        n = 0
        sources = [(depth, own)] if depth else []
        if fars:
            sources += [
                (fars[side].shape[-2] // height, far_of(v, side)) for side in range(sides)
            ]
        for number, source in sources:
            for k in range(number):
                rows = slice(k * height, (k + 1) * height)
                if lead:

                    def one_tile(t, carry, v=v, n=n, source=source, rows=rows):
                        put((v, t, n), source[t, rows, :].astype(F32))
                        return carry

                    lax.fori_loop(0, lead[0], one_tile, 0, unroll=True)
                else:
                    put((v, n), source[rows, :].astype(F32))
                n += 1


def beside(even, one, two):
    one, two = one.astype(F32), two.astype(F32)
    return jnp.where(
        even, jnp.concatenate([one, two], axis=0), jnp.concatenate([two, one], axis=0)
    )


def reversal():
    rows = lax.broadcasted_iota(jnp.int32, (TILE, TILE), 0)
    cols = lax.broadcasted_iota(jnp.int32, (TILE, TILE), 1)
    return jnp.where(rows + cols == TILE - 1, F32(1.0), F32(0.0)).astype(BF)


def total_kernel(parts, far_rows, *refs):
    ins, (out_ref, rev_ref, *far_refs, done_ref) = refs[:parts], refs[parts + 1 :]
    done_ref[...] = jnp.zeros(done_ref.shape, F32)
    tiles, rows, _ = out_ref.shape
    for t in range(tiles):
        cut = slice(t * TILE, (t + 1) * TILE)
        acc = ins[0][:, :, cut].astype(F32)
        for ref in ins[1:]:
            acc = acc + ref[:, :, cut].astype(F32)
        block = acc.reshape(rows, TILE).astype(BF)
        out_ref[t] = block
        for ref, part in zip(far_refs, far_rows):
            ref[0, t] = block[part]
    back = jnp.dot(
        out_ref[...].reshape(tiles * rows, TILE), reversal(), preferred_element_type=F32
    ).astype(BF)
    for t in range(tiles):
        rev_ref[tiles - 1 - t] = back[t * rows : (t + 1) * rows]


def band_kernel(at, *refs):
    heard, (out_ref, num_ref, done_ref) = views_of(*refs[:2]), refs[3:]
    done_ref[...] = jnp.zeros(done_ref.shape, F32)
    for v in range(4):
        num_ref[v * 16 : (v + 1) * 16, :] = numbers_of(heard[v], at)
    flip = reversal()
    for v in range(4):
        row = heard[v][at : at + 8, : 3 * 128].astype(F32)[0:1]
        edge = TILE // 2
        base = jnp.concatenate(
            [jnp.zeros((1, edge), F32), row, jnp.zeros((1, 2 * edge), F32)], axis=1
        )
        wide = pltpu.roll(
            jnp.broadcast_to(base, (TILE, 3 * TILE)), 0, 1, stride=1, stride_axis=0
        ).astype(BF)
        turned = jnp.dot(flip, wide, preferred_element_type=F32).astype(BF)
        half = TILE // 2
        for k, (rows, to) in enumerate(
            (
                (slice(half, TILE), slice(0, half)),
                (slice(0, TILE), slice(half, half + TILE)),
                (slice(0, half), slice(half + TILE, 2 * TILE)),
            )
        ):
            cut = slice(k * TILE, (k + 1) * TILE)
            across = slice((2 - k) * TILE, (3 - k) * TILE)
            if v >= 2:
                out_ref[2 + v, to, :] = turned[rows, cut]
            else:
                out_ref[2 + v, to, :] = wide[rows, across]
                out_ref[v, to, :] = jnp.dot(
                    turned[rows, cut], flip, preferred_element_type=F32
                ).astype(BF)


def forward_block(v):
    return v if v < 2 else v + 2


def backward_block(v):
    return v + 2


def spots(t, h):
    return t + h, slice((1 - h) * (TILE // 2), (2 - h) * (TILE // 2))


def zero_ends(ref):
    half = TILE // 2
    ref[0, :, :half] = jnp.zeros((ref.shape[1], half), BF)
    ref[ref.shape[0] - 1, :, half:] = jnp.zeros((ref.shape[1], half), BF)


def conv(src, first, tiles, rows, blocks, dst, step):
    s = 0
    while s < tiles:
        n = min(step, tiles - s)
        out = sum(
            jnp.dot(
                src[pl.ds(first + s + k, n)].reshape(n * rows, TILE),
                blocks[k * TILE : (k + 1) * TILE, :],
                preferred_element_type=F32,
            )
            for k in range(2)
        ).astype(BF)
        dst[s : s + n] = out.reshape(n, rows, TILE)
        s += n


def taps_sum(slices, zs, taps):
    result = {}
    for z in zs:
        sums = [None, None, None]
        for j in range(3):
            for i in range(3):
                at = z + i - 1
                if at in slices:
                    term = taps(z, i, j) * slices[at]
                    sums[j] = term if sums[j] is None else sums[j] + term
        result[z] = sums
    return result


def along_y(sums):
    n = sums[0].shape[0]
    return pltpu.roll(sums[0], 1, 0) + sums[1] + pltpu.roll(sums[2], n - 1, 0)


def write_frame(frame, tiles, sides, *refs):
    own_refs, refs = views_of(*refs[:2]), refs[2:]
    side_refs = dict(zip(sides, refs[: len(sides)]))
    one_ref, two_ref, out_ref = refs[len(sides) :]
    view = lax.axis_index("view")
    even = lax.axis_index("gy") % 2 == 0
    zero_ends(out_ref)
    for v in range(4):
        for s in range(tiles // 4 * 2):
            t, lanes = spots((view ^ v) * (tiles // 4) + s // 2, s % 2)
            cut = slice(s * TILE // 2, (s + 1) * TILE // 2)
            for f in range(frame.size):
                where, k = frame.source(f)
                rows = slice(k * 8, (k + 1) * 8)
                if where == "own":
                    own = own_refs[v][rows, cut]
                else:
                    own = side_refs[where][v, rows, cut]
                n = frame.place(f, frame.depth)
                out_ref[t, f * 16 : (f + 1) * 16, lanes] = jnp.concatenate(
                    [
                        own.astype(F32),
                        beside(even, one_ref[v, n, :, cut], two_ref[v, n, :, cut]),
                    ],
                    axis=0,
                ).astype(BF)


def start_kernel(frame, tiles, sides, views, num_ref, blocks_ref, *refs):
    count = len(sides)
    out_ref, recip_ref, done_ref, c = refs[5 + count :]
    write_frame(frame, tiles, sides, *refs[: 4 + count], out_ref)
    forward_views(frame, tiles, views, num_ref, blocks_ref, out_ref, recip_ref, c)
    done_ref[...] = jnp.zeros(done_ref.shape, F32)


def forward_kernel(frame, tiles, views, num_ref, blocks_ref, frame_ref, _, recip_ref, done_ref, c):
    forward_views(frame, tiles, views, num_ref, blocks_ref, frame_ref, recip_ref, c)
    done_ref[...] = jnp.zeros(done_ref.shape, F32)


def forward_views(frame, tiles, views, num_ref, blocks_ref, frame_ref, recip_ref, c):
    size = frame.size
    zs = frame.need(3)
    for at, v in enumerate(views):
        conv(frame_ref, 0, tiles, size * 16, blocks_ref.at[forward_block(v)], c, 2)

        def divide(t, carry, v=v, at=at):
            from_t = t if v < 2 else tiles - 1 - t
            for h in range(TILE // 128):
                cut = slice(h * 128, (h + 1) * 128)
                slices = {
                    f: c[from_t, f * 16 : (f + 1) * 16, cut].astype(F32)
                    for f in range(size)
                }
                sums = taps_sum(slices, zs, lambda z, i, j: num_ref[v * 16 + i * 3 + j : v * 16 + i * 3 + j + 1, :])
                for n, z in enumerate(zs):
                    recip_ref[at, t, n * 16 : (n + 1) * 16, cut] = (
                        1.0 / (along_y(sums[z]) + num_ref[v * 16 + 9 : v * 16 + 10, :])
                    ).astype(BF)
            return carry

        lax.fori_loop(0, tiles, divide, 0, unroll=True)


def main_kernel(frame, tiles, sides, table_ref, *refs):
    count = len(sides)
    index_refs, refs = refs[: count + 1], refs[count + 1 :]
    num_ref, est_ref, refs = refs[0], refs[1], refs[2:]
    own_refs, refs = refs[:4], refs[4:]
    far_refs, refs = refs[: 2 * count], refs[2 * count :]
    near_refs, beyond_refs = refs[:2], refs[2:4]
    recip_refs = refs[4:6]
    blocks_ref, frame_ref, out_ref = refs[6:9]
    m1, u2, m2, c0, c1, c2, c3, kept, wt = refs[9:]
    even = lax.axis_index("gy") % 2 == 0
    c = [c0, c1, c2, c3]
    view = lax.axis_index("view")
    upside = lax.axis_index("gz") if frame.mirrored else 0
    depth = frame.depth
    z3, z2, z1, z0 = (frame.need(r) for r in (3, 2, 1, 0))
    sent = frame.sent(3)

    for f in z2:
        where, k = frame.source(f)
        index_ref = index_refs[0 if where == "own" else 1 + sides.index(where)]
        over = upside if where == "own" else 1 - upside
        raw = k + over * (depth - 1 - 2 * k) if frame.mirrored else k
        weights = [
            jnp.full((16, 128), table_ref[v, index_ref[v, raw]], F32) for v in range(4)
        ]
        total = (weights[0] + weights[1]) + (weights[2] + weights[3])
        for v in range(4):
            mine = jnp.full(
                (16, 128), table_ref[view ^ v, index_ref[view ^ v, raw]], F32
            )
            at = (v * frame.size + f) * 16
            wt[at : at + 16, :] = num_ref[v * 16 : (v + 1) * 16, :] * (mine / total)

    def weighted(v, z, n):
        at = (v * frame.size + z) * 16 + 8 - n
        return wt[at : at + 1, :]

    def measured(v, t, z, cut):
        where, k = frame.source(z)
        if where == "own":
            own = own_refs[v][t, k * 8 : (k + 1) * 8, cut]
        else:
            k = k - sent[where].start
            far = far_refs[(count if v else 0) + sides.index(where)]
            own = far[v - 1 if v else 0, t, k * 8 : (k + 1) * 8, cut]
        n = frame.place(z, 3)
        one_ref, two_ref = near_refs if n < depth else beyond_refs
        n = n if n < depth else n - depth
        return jnp.concatenate(
            [
                own.astype(F32),
                beside(
                    even,
                    one_ref[v, t, n, :, cut],
                    two_ref[v, t, n, :, cut],
                ),
            ],
            axis=0,
        )

    def mix(v, t, z, cut, recip_a, recip_b):
        a = (measured(v, t, z, cut) * recip_a).astype(BF).astype(F32)
        b = (measured(v + 2, t, z, cut) * recip_b).astype(BF).astype(F32)
        return (0.5 * (a + b)).astype(BF)

    for ref in (m1, u2, m2):
        zero_ends(ref)

    for v in range(2):

        def ratios(t, carry, v=v):
            for h in range(TILE // 128):
                cut = slice(h * 128, (h + 1) * 128)
                to, lanes = spots(t, h)
                for n, z in enumerate(z3):
                    at = slice(n * 16, (n + 1) * 16)
                    m1[to, at, lanes] = mix(
                        v,
                        t,
                        z,
                        cut,
                        recip_refs[0][v, t, at, cut].astype(F32),
                        recip_refs[1][v, t, at, cut].astype(F32),
                    )
            return carry

        lax.fori_loop(0, tiles, ratios, 0, unroll=True)
        for w in (v, v + 2):
            conv(m1, 0, tiles, m1.shape[1], blocks_ref.at[backward_block(w)], c[w], 2)

    def numerator(slices_of, zs):
        totals = {z: [None, None, None] for z in zs}
        for v in range(4):
            slices = slices_of(v)
            sums = taps_sum(
                slices,
                zs,
                lambda z, i, j, v=v: weighted(v, z, i * 3 + j),
            )
            for z in zs:
                for j in range(3):
                    old = totals[z][j]
                    totals[z][j] = sums[z][j] if old is None else old + sums[z][j]
        return totals

    def update(t, carry):
        for h in range(TILE // 128):
            cut = slice(h * 128, (h + 1) * 128)

            def slices_of(v):
                from_t = t if v < 2 else tiles - 1 - t
                return {
                    z: c[v][from_t, n * 16 : (n + 1) * 16, cut].astype(F32)
                    for n, z in enumerate(z3)
                }

            to, lanes = spots(t, h)
            totals = numerator(slices_of, z2)
            for n, z in enumerate(z2):
                change = along_y(totals[z])
                before = frame_ref[to, z * 16 : (z + 1) * 16, lanes].astype(F32)
                u2[to, n * 16 : (n + 1) * 16, lanes] = (before * change).astype(BF)
                if z in z0:
                    k = z - frame.own
                    kept[t, k * 8 : (k + 1) * 8, cut] = change[:8]
        return carry

    lax.fori_loop(0, tiles, update, 0, unroll=True)

    rows1 = m2.shape[1]
    n2 = u2.shape[1]
    for v in range(2):
        for w in (v, v + 2):
            conv(u2, 0, tiles, n2, blocks_ref.at[forward_block(w)], c[w].at[:, :n2, :], 2)

        def ratios2(t, carry, v=v):
            for h in range(TILE // 128):
                cut = slice(h * 128, (h + 1) * 128)
                recips = []
                for w in (v, v + 2):
                    from_t = t if w < 2 else tiles - 1 - t
                    slices = {
                        z: c[w][from_t, n * 16 : (n + 1) * 16, cut].astype(F32)
                        for n, z in enumerate(z2)
                    }
                    sums = taps_sum(
                        slices, z1, lambda z, i, j, w=w: num_ref[w * 16 + i * 3 + j : w * 16 + i * 3 + j + 1, :]
                    )
                    recips.append(
                        {z: 1.0 / (along_y(sums[z]) + num_ref[w * 16 + 9 : w * 16 + 10, :]) for z in z1}
                    )
                to, lanes = spots(t, h)
                for n, z in enumerate(z1):
                    m2[to, n * 16 : (n + 1) * 16, lanes] = mix(
                        v, t, z, cut, recips[0][z], recips[1][z]
                    )
            return carry

        lax.fori_loop(0, tiles, ratios2, 0, unroll=True)
        mine = tiles // 4
        for w in (v, v + 2):
            first = view * mine if w < 2 else tiles - (view + 1) * mine
            conv(m2, first, mine, rows1, blocks_ref.at[backward_block(w)], c[w].at[:, :rows1, :], 2)

    mine = tiles // 4
    for s in range(mine):
        for h in range(TILE // 128):
            cut = slice(h * 128, (h + 1) * 128)

            def slices_of(v):
                from_s = s if v < 2 else mine - 1 - s
                return {
                    z: c[v][from_s, n * 16 : (n + 1) * 16, cut].astype(F32)
                    for n, z in enumerate(z1)
                }

            totals = numerator(slices_of, z0)
            for z in z0:
                k = z - frame.own
                to = k + upside * (depth - 1 - 2 * k)
                lanes = slice(s * TILE + h * 128, s * TILE + (h + 1) * 128)
                first_change = kept[view * mine + s, k * 8 : (k + 1) * 8, cut]
                out_ref[to, :, lanes] = (
                    est_ref[to, :, lanes] * first_change * along_y(totals[z])[:8]
                )


def shards(
    pieces, piece_owner, piece_row, estimate, psf_x, stencil, background, bleach_table, bleach_index
):
    depth, height, chunk = estimate.shape
    width = pieces.shape[3]
    tiles = width // TILE
    slabs = lax.axis_size("gz")
    bands = lax.axis_size("gy")
    blocks = slabs * bands
    frame = Frame(slabs, depth)
    size = frame.size
    sides = tuple(frame.sent(1))
    vmem, smem = pltpu.VMEM, pltpu.SMEM
    params = pltpu.CompilerParams(vmem_limit_bytes=LIMIT)

    def stay(array):
        return pltpu.with_memory_space_constraint(array, pltpu.VMEM)

    given = [piece_row, estimate, psf_x, bleach_table]
    given += [pieces[0], stencil.transpose(1, 0, 2), piece_owner.transpose(0, 2, 1)]
    first_pieces, first_taps, first_owner = given[-3:]

    def is_given(x):
        return any(x is y for y in given)

    def call(kernel, shapes, ins, outs, *args, scratch=()):
        args = [
            (
                pltpu.with_memory_space_constraint(x, pltpu.HBM)
                if is_given(x)
                else stay(x)
                if space is vmem
                else x
            )
            for space, x in zip(ins, args)
        ]
        out = pl.pallas_call(
            kernel,
            out_shape=shapes,
            in_specs=whole(*ins),
            out_specs=whole(*outs) if isinstance(shapes, tuple) else whole(*outs)[0],
            scratch_shapes=list(scratch),
            compiler_params=params,
        )(*args)
        return out

    def resident(*dims, dtype=BF):
        return pltpu.VMEM(dims, dtype)

    mark = jax.ShapeDtypeStruct((8, 128), F32)

    free = pl.ANY
    area = depth * height

    pairs = blocks // 2
    half_cells = resident(pairs, depth, height, width)
    even, odd, payload = call(
        functools.partial(first_kernel, pairs, bands, frame.mirrored),
        (half_cells, half_cells, resident(area + 8, chunk)),
        (smem, smem, smem, vmem, vmem, vmem, vmem),
        (vmem, vmem, vmem),
        first_owner,
        piece_row,
        background,
        first_pieces,
        first_taps,
        estimate,
        psf_x,
        scratch=[vmem((blocks * depth, height, width), F32), vmem((8, chunk), F32)],
    )
    other = swap(odd, "gy", bands, 1)
    near_payload = swap(payload, "view", 4, 1)
    index_far = exchange_z(frame, lambda s: bleach_index[:, s.start : s.stop], slabs, depth)
    *kept, pair, sums_done = call(
        functools.partial(sum_kernel, pairs),
        (resident(depth, height, width),) * pairs
        + (resident(2, area + 8, chunk), mark),
        [vmem] * 4 + [free],
        [vmem] * (pairs + 2),
        even,
        other,
        payload,
        near_payload,
        index_far[sides[0]],
    )
    heard = (pair, swap(pair, "view", 4, 2))
    moved = [swap(kept[k], ("gz", "gy"), blocks, 2 * k) for k in range(1, pairs)]

    def stack(arrays, slices, *tokens):
        rows = slice(slices.start * height, slices.stop * height)
        dims = (len(arrays),) + arrays[0].shape[:-2] + (len(slices) * height, arrays[0].shape[-1])
        return call(
            functools.partial(stack_kernel, rows, len(arrays)),
            (resident(*dims), mark),
            [vmem] * len(arrays) + [free] + [vmem] * (len(tokens) - 1),
            (vmem, vmem),
            *arrays,
            *tokens,
        )

    def edges(arrays, fars, token, slices, dims):
        out = resident(4, *dims[:-2], slices, height // 2, dims[-1])
        return call(
            functools.partial(
                edges_kernel,
                height,
                depth if arrays else 0,
                len(sides),
                len(arrays) == 2,
            ),
            (out, out, mark),
            [vmem] * (len(arrays) + len(fars)) + [free],
            (vmem, vmem, vmem),
            *arrays,
            *fars,
            token,
        )

    table, nums, token = call(
        functools.partial(band_kernel, area),
        (resident(6, 2 * TILE, TILE), resident(64, 128, dtype=F32), mark),
        [vmem] * 2 + [free],
        (vmem, vmem, vmem),
        *heard,
        sums_done,
    )
    kept_table, kept_nums = table, nums

    far_slices = frame.sent(3)
    plain, turned, *own_far, total_done = call(
        functools.partial(
            total_kernel,
            pairs,
            [slice(s.start * height, s.stop * height) for s in far_slices.values()],
        ),
        (resident(tiles, area, TILE), resident(tiles, area, TILE))
        + tuple(resident(1, tiles, len(s) * height, TILE) for s in far_slices.values())
        + (mark,),
        [vmem] * pairs + [free],
        [vmem] * (3 + len(sides)),
        kept[0],
        *moved,
        token,
    )
    near = swap(plain, "view", 4, 1)
    opposite = swap(turned, "view", 4, 2)
    last = swap(opposite, "view", 4, 1)
    ready = dict(zip([(s.start, s.stop) for s in far_slices.values()], own_far))
    def est_rows(slices):
        return call(
            functools.partial(
                est_rows_kernel, slice(slices.start * height, slices.stop * height)
            ),
            resident(4, len(slices) * height, chunk),
            [vmem] * 2 + [free],
            (vmem,),
            *heard,
            total_done,
        )

    far_est = exchange_z(frame, est_rows, slabs, depth)
    far_est = [far_est[s] for s in sides]
    est_edges = edges(heard, far_est, total_done, size, payload.shape)
    one_est, two_est = core_side(est_edges, bands, True)
    far_own = exchange_z(frame, lambda s: ready[s.start, s.stop], slabs, 3)
    far_own = [far_own[s] for s in sides]
    n3, n2, n1 = (len(frame.need(r)) * 16 for r in (3, 2, 1))

    scratch = [vmem((tiles, size * 16, TILE), BF)]
    tokens = []

    def others(slices):
        rows, done = stack(
            (near, opposite, last), slices, total_done, one_est, two_est
        )
        tokens.append(done)
        return rows

    far_others = exchange_z(frame, others, slabs, 3)
    far_others = [far_others[s] for s in sides]
    own_edges = edges((plain, near, opposite, last), (), tokens[-1], depth, plain.shape)
    near_halo = core_side(own_edges, bands, False)
    est_frame, recip_a, token = call(
        functools.partial(start_kernel, frame, tiles, sides, (0, 1)),
        (
            resident(tiles + 1, size * 16, TILE),
            resident(2, tiles, n3, TILE),
            mark,
        ),
        [vmem] * (6 + len(sides)) + [free],
        (vmem, vmem, vmem),
        kept_nums,
        kept_table,
        *heard,
        *far_est,
        one_est,
        two_est,
        own_edges[2],
        scratch=scratch,
    )
    far_edges = edges(
        (), far_own + far_others, token, len(frame.need(3)) - depth, plain.shape
    )
    far_halo = core_side(far_edges, bands, False)
    recip_b, token_b = call(
        functools.partial(forward_kernel, frame, tiles, (2, 3)),
        (resident(2, tiles, n3, TILE), mark),
        (vmem, vmem, vmem, free),
        (vmem, vmem),
        kept_nums,
        kept_table,
        est_frame,
        far_edges[2],
        scratch=scratch,
    )
    return call(
        functools.partial(main_kernel, frame, tiles, sides),
        jax.ShapeDtypeStruct(estimate.shape, F32),
        [smem] * (2 + len(sides)) + [vmem] * (14 + 2 * len(sides)),
        (vmem,),
        bleach_table,
        bleach_index,
        *[index_far[s] for s in sides],
        kept_nums,
        estimate,
        plain,
        near,
        opposite,
        last,
        *far_own,
        *far_others,
        *near_halo,
        *far_halo,
        recip_a,
        recip_b,
        kept_table,
        est_frame,
        scratch=[
            vmem((tiles + 1, n3, TILE), BF),
            vmem((tiles + 1, n2, TILE), BF),
            vmem((tiles + 1, n1, TILE), BF),
        ]
        + [vmem((tiles, n3, TILE), BF)] * 4
        + [vmem((tiles, area, TILE), F32), vmem((4 * size * 16, 128), F32)],
    )


def solution(mesh):
    placed = (
        P("view", ("gz", "gy"), None, None),
        P("view", ("gz", "gy"), None),
        P("view", ("gz", "gy")),
        P("gz", "gy", "view"),
        P("view", None),
        P("view", None, None),
        P("view"),
        P(),
        P(None, "gz"),
    )
    return jax.shard_map(
        shards, mesh=mesh, in_specs=placed, out_specs=P("gz", "gy", "view"), check_vma=False
    )
```

```python
import functools

import jax
import jax.numpy as jnp
from jax import lax
from jax.experimental import pallas as pl
from jax.experimental.pallas import tpu as pltpu
from jax.sharding import PartitionSpec as P

BF = jnp.bfloat16
F32 = jnp.float32
TILE = 256
LIMIT = 24 << 20


def whole(*spaces):
    return [pl.BlockSpec(memory_space=space) for space in spaces]


def swap(array, axis, size, mask):
    return lax.ppermute(array, axis, [(i, i ^ mask) for i in range(size)])


def core_side(own, bands, all_take_part):
    first = swap(own[0], "gy", bands, 1)
    if all_take_part:
        return first, swap(own[1], "gy", bands, 3)
    return first, lax.ppermute(own[1], "gy", [(1, 2), (2, 1)])


def upward(array, axis, size):
    return lax.ppermute(array, axis, [(i, i + 1) for i in range(size - 1)])


def downward(array, axis, size):
    return lax.ppermute(array, axis, [(i + 1, i) for i in range(size - 1)])


class Frame:
    def __init__(self, slabs, depth):
        self.mirrored = slabs == 2
        self.depth = depth
        self.own = 0 if self.mirrored else depth
        self.size = 2 * depth if self.mirrored else 3 * depth

    def need(self, radius):
        return range(
            max(0, self.own - radius), min(self.size, self.own + self.depth + radius)
        )

    def source(self, f):
        k = f - self.own
        if 0 <= k < self.depth:
            return "own", k
        if self.mirrored:
            return "up", 2 * self.depth - 1 - k
        return ("dn", f) if k < 0 else ("up", k - self.depth)

    def place(self, f, radius):
        where, k = self.source(f)
        at = 0
        for name, slices in [("own", range(self.depth))] + list(self.sent(radius).items()):
            if name == where:
                return at + k - slices.start
            at += len(slices)

    def sent(self, radius):
        if self.mirrored:
            return {"up": range(self.depth - radius, self.depth)}
        return {
            "dn": range(self.depth - radius, self.depth),
            "up": range(0, radius),
        }


def exchange_z(frame, make, slabs, radius):
    got = {}
    for side, slices in frame.sent(radius).items():
        payload = make(slices)
        if frame.mirrored:
            got[side] = swap(payload, "gz", slabs, 1)
        elif side == "dn":
            got[side] = upward(payload, "gz", slabs)
        else:
            got[side] = downward(payload, "gz", slabs)
    return got


def place():
    return lax.axis_index("view"), lax.axis_index("gz")


def first_kernel(
    pairs,
    bands,
    mirrored,
    owner_ref,
    row_ref,
    bg_ref,
    index_ref,
    pieces_ref,
    taps_ref,
    est_ref,
    psf_ref,
    even_ref,
    odd_ref,
    payload_ref,
    acc,
    tail,
):
    write_payload(mirrored, bg_ref, index_ref, taps_ref, est_ref, psf_ref, payload_ref, tail)
    count = pieces_ref.shape[0]
    depth = even_ref.shape[1]
    me = lax.axis_index("gz") * bands + lax.axis_index("gy")

    def clear(i, carry):
        acc[i] = jnp.zeros(acc.shape[1:], F32)
        return carry

    lax.fori_loop(0, acc.shape[0], clear, 0)

    def add(i, carry):
        owner = owner_ref[0, 0, i]
        row = row_ref[0, i]
        if mirrored:
            row = jnp.where(owner >= bands, depth - 1 - row, row)
        c = (owner ^ me) * depth + row
        acc[c] = acc[c] + pieces_ref[i].astype(F32)
        return carry

    lax.fori_loop(0, count, add, 0)

    def put(pair, carry):
        for f in range(depth):
            even_ref[pair, f] = acc[pair * 2 * depth + f].astype(BF)
            odd_ref[pair, f] = acc[(pair * 2 + 1) * depth + f].astype(BF)
        return carry

    lax.fori_loop(0, pairs, put, 0)


def write_payload(mirrored, bg_ref, index_ref, taps_ref, est_ref, psf_ref, out_ref, tail):
    depth, height = est_ref.shape[:2]
    upside = lax.axis_index("gz") if mirrored else 0
    for k in range(depth):
        out_ref[k * height : (k + 1) * height, :] = est_ref[
            k + upside * (depth - 1 - 2 * k)
        ].astype(BF)
    tail[...] = jnp.zeros(tail.shape, F32)
    for i in range(3):
        tail[0:1, 3 * i : 3 * i + 3] = taps_ref[i + upside * (2 - 2 * i)]
    lanes = lax.broadcasted_iota(jnp.int32, (1, 128), 1)
    exact = jnp.where(lanes == 9, bg_ref[0], tail[0:1, :128])
    for n in range(3):
        part = exact.astype(BF).astype(F32)
        tail[n + 1 : n + 2, :128] = part
        exact = exact - part
    levels = jnp.zeros((1, 128), F32)
    for v in range(4):
        for k in range(depth):
            level = jnp.full((1, 128), index_ref[v, k], jnp.int32).astype(F32)
            levels = jnp.where(lanes == v * depth + k, level, levels)
    tail[4:5, :128] = levels
    tail[0:1, : psf_ref.shape[1]] = psf_ref[...]
    out_ref[depth * height :, :] = tail[...].astype(BF)


def bleach_weights(rows, table):
    wide = jnp.broadcast_to(rows[4:5], (16, 128))
    down = lax.broadcasted_iota(jnp.int32, (16, 128), 0)
    across = lax.broadcasted_iota(jnp.int32, (16, 128), 1)
    level = jnp.sum(jnp.where(down == across, wide, 0.0), axis=1, keepdims=True)
    listed = jnp.broadcast_to(table[0:1], (16, 128))
    for v in range(1, 4):
        listed = jnp.where(down // 4 == v, jnp.broadcast_to(table[v : v + 1], (16, 128)), listed)
    hit = across.astype(F32) == level
    weight = jnp.sum(jnp.where(hit, listed, 0.0), axis=1, keepdims=True)
    return jnp.broadcast_to(weight, (16, 128))


def numbers_of(heard, at):
    rows = heard[at : at + 8, :128].astype(F32)
    exact = rows[1:2] + rows[2:3] + rows[3:4]
    wide = jnp.broadcast_to(exact, (16, 128))
    spot = lax.broadcasted_iota(jnp.int32, (16, 128), 0) == lax.broadcasted_iota(
        jnp.int32, (16, 128), 1
    )
    column = jnp.sum(jnp.where(spot, wide, 0.0), axis=1, keepdims=True)
    return jnp.broadcast_to(column, (16, 128))


def sum_kernel(pairs, *refs):
    even_ref, other_ref, own_ref, near_ref = refs[:4]
    sums, (pair_ref, done_ref) = refs[4 : 4 + pairs], refs[4 + pairs :]
    done_ref[...] = jnp.zeros(done_ref.shape, F32)
    for k in range(pairs):
        sums[k][...] = (even_ref[k].astype(F32) + other_ref[k].astype(F32)).astype(BF)
    pair_ref[0] = own_ref[...]
    pair_ref[1] = near_ref[...]


def views_of(first, second):
    return [first.at[0], first.at[1], second.at[0], second.at[1]]


def est_rows_kernel(first, second, _, out_ref):
    for v, ref in enumerate(views_of(first, second)):
        out_ref[v] = ref[...]


def stack_kernel(rows, count, *refs):
    ins, (out_ref, done_ref) = refs[:count], refs[-2:]
    done_ref[...] = jnp.zeros(done_ref.shape, F32)
    for v, ref in enumerate(ins):
        out_ref[v] = ref[..., rows, :]


def edges_kernel(height, depth, sides, paired, *refs):
    out1, out2, done_ref = refs[-3:]
    done_ref[...] = jnp.zeros(done_ref.shape, F32)
    count = out1.shape[0]
    views = refs[:count] if depth else [None] * count
    fars = refs[count if depth else 0 : -4]
    if paired:
        views, fars = views_of(*refs[:2]), refs[2:-4]
    half = height // 2
    gy = lax.axis_index("gy")
    even = gy % 2 == 0
    inner = (gy == 1) | (gy == 2)
    lead = out1.shape[1:-3]

    def put(at, block):
        turned = pltpu.roll(block, half, block.ndim - 2)
        one = jnp.where(even, turned, block)
        two = jnp.where(inner, jnp.where(even, block, turned), 0.0)
        out1[at] = one[..., :half, :].astype(BF)
        out2[at] = two[..., :half, :].astype(BF)

    def far_of(v, side):
        for ref in fars[side::sides]:
            if v < ref.shape[0]:
                return ref.at[v]
            v -= ref.shape[0]

    for v, own in enumerate(views):
        n = 0
        sources = [(depth, own)] if depth else []
        if fars:
            sources += [
                (min(4, fars[side].shape[-2] // height), far_of(v, side)) for side in range(sides)
            ]
        for number, source in sources:
            for k in range(number):
                rows = slice(k * height, (k + 1) * height)
                if lead:

                    def one_tile(t, carry, v=v, n=n, source=source, rows=rows):
                        put((v, t, n), source[t, rows, :].astype(F32))
                        return carry

                    lax.fori_loop(0, lead[0], one_tile, 0, unroll=True)
                else:
                    put((v, n), source[rows, :].astype(F32))
                n += 1


def beside(even, one, two):
    one, two = one.astype(F32), two.astype(F32)
    return jnp.where(
        even, jnp.concatenate([one, two], axis=0), jnp.concatenate([two, one], axis=0)
    )


def reversal():
    rows = lax.broadcasted_iota(jnp.int32, (TILE, TILE), 0)
    cols = lax.broadcasted_iota(jnp.int32, (TILE, TILE), 1)
    return jnp.where(rows + cols == TILE - 1, F32(1.0), F32(0.0)).astype(BF)


def total_kernel(parts, far_rows, *refs):
    ins, (out_ref, rev_ref, *far_refs, done_ref) = refs[:parts], refs[parts + 1 :]
    done_ref[...] = jnp.zeros(done_ref.shape, F32)
    tiles, rows, _ = out_ref.shape
    for t in range(tiles):
        cut = slice(t * TILE, (t + 1) * TILE)
        acc = ins[0][:, :, cut].astype(F32)
        for ref in ins[1:]:
            acc = acc + ref[:, :, cut].astype(F32)
        block = acc.reshape(rows, TILE).astype(BF)
        out_ref[t] = block
        for ref, part in zip(far_refs, far_rows):
            ref[0, t] = block[part]
    back = jnp.dot(
        out_ref[...].reshape(tiles * rows, TILE), reversal(), preferred_element_type=F32
    ).astype(BF)
    for t in range(tiles):
        rev_ref[tiles - 1 - t] = back[t * rows : (t + 1) * rows]


def band_kernel(at, *refs):
    heard, (out_ref, num_ref, done_ref) = views_of(*refs[:2]), refs[3:]
    done_ref[...] = jnp.zeros(done_ref.shape, F32)
    for v in range(4):
        num_ref[v * 16 : (v + 1) * 16, :] = numbers_of(heard[v], at)
    flip = reversal()
    for v in range(4):
        row = heard[v][at : at + 8, : 3 * 128].astype(F32)[0:1]
        edge = TILE // 2
        base = jnp.concatenate(
            [jnp.zeros((1, edge), F32), row, jnp.zeros((1, 2 * edge), F32)], axis=1
        )
        wide = pltpu.roll(
            jnp.broadcast_to(base, (TILE, 3 * TILE)), 0, 1, stride=1, stride_axis=0
        ).astype(BF)
        turned = jnp.dot(flip, wide, preferred_element_type=F32).astype(BF)
        half = TILE // 2
        for k, (rows, to) in enumerate(
            (
                (slice(half, TILE), slice(0, half)),
                (slice(0, TILE), slice(half, half + TILE)),
                (slice(0, half), slice(half + TILE, 2 * TILE)),
            )
        ):
            cut = slice(k * TILE, (k + 1) * TILE)
            across = slice((2 - k) * TILE, (3 - k) * TILE)
            if v >= 2:
                out_ref[2 + v, to, :] = turned[rows, cut]
            else:
                out_ref[2 + v, to, :] = wide[rows, across]
                out_ref[v, to, :] = jnp.dot(
                    turned[rows, cut], flip, preferred_element_type=F32
                ).astype(BF)


def forward_block(v):
    return v if v < 2 else v + 2


def backward_block(v):
    return v + 2


def spots(t, h):
    return t + h, slice((1 - h) * (TILE // 2), (2 - h) * (TILE // 2))


def zero_ends(ref):
    half = TILE // 2
    ref[0, :, :half] = jnp.zeros((ref.shape[1], half), BF)
    ref[ref.shape[0] - 1, :, half:] = jnp.zeros((ref.shape[1], half), BF)


def conv(src, first, tiles, rows, blocks, dst, step):
    s = 0
    while s < tiles:
        n = min(step, tiles - s)
        out = sum(
            jnp.dot(
                src[pl.ds(first + s + k, n)].reshape(n * rows, TILE),
                blocks[k * TILE : (k + 1) * TILE, :],
                preferred_element_type=F32,
            )
            for k in range(2)
        ).astype(BF)
        dst[s : s + n] = out.reshape(n, rows, TILE)
        s += n


def taps_sum(slices, zs, taps):
    result = {}
    for z in zs:
        sums = [None, None, None]
        for j in range(3):
            for i in range(3):
                at = z + i - 1
                if at in slices:
                    term = taps(z, i, j) * slices[at]
                    sums[j] = term if sums[j] is None else sums[j] + term
        result[z] = sums
    return result


def along_y(sums):
    n = sums[0].shape[0]
    return pltpu.roll(sums[0], 1, 0) + sums[1] + pltpu.roll(sums[2], n - 1, 0)


def write_frame(frame, tiles, sides, *refs):
    own_refs, refs = views_of(*refs[:2]), refs[2:]
    side_refs = dict(zip(sides, refs[: len(sides)]))
    one_ref, two_ref, out_ref = refs[len(sides) :]
    view = lax.axis_index("view")
    even = lax.axis_index("gy") % 2 == 0
    zero_ends(out_ref)
    for v in range(4):
        for s in range(tiles // 4 * 2):
            t, lanes = spots((view ^ v) * (tiles // 4) + s // 2, s % 2)
            cut = slice(s * TILE // 2, (s + 1) * TILE // 2)
            for f in range(frame.size):
                where, k = frame.source(f)
                rows = slice(k * 8, (k + 1) * 8)
                if where == "own":
                    own = own_refs[v][rows, cut]
                else:
                    own = side_refs[where][v, rows, cut]
                n = frame.place(f, frame.depth)
                out_ref[t, f * 16 : (f + 1) * 16, lanes] = jnp.concatenate(
                    [
                        own.astype(F32),
                        beside(even, one_ref[v, n, :, cut], two_ref[v, n, :, cut]),
                    ],
                    axis=0,
                ).astype(BF)


def start_kernel(frame, tiles, sides, views, num_ref, blocks_ref, *refs):
    count = len(sides)
    out_ref, recip_ref, done_ref, c = refs[5 + count :]
    write_frame(frame, tiles, sides, *refs[: 4 + count], out_ref)
    forward_views(frame, tiles, views, num_ref, blocks_ref, out_ref, recip_ref, c)
    done_ref[...] = jnp.zeros(done_ref.shape, F32)


def forward_kernel(frame, tiles, views, num_ref, blocks_ref, frame_ref, _, recip_ref, done_ref, c):
    forward_views(frame, tiles, views, num_ref, blocks_ref, frame_ref, recip_ref, c)
    done_ref[...] = jnp.zeros(done_ref.shape, F32)


def forward_views(frame, tiles, views, num_ref, blocks_ref, frame_ref, recip_ref, c):
    size = frame.size
    zs = frame.need(3)
    for at, v in enumerate(views):
        conv(frame_ref, 0, tiles, size * 16, blocks_ref.at[forward_block(v)], c, 2)

        def divide(t, carry, v=v, at=at):
            from_t = t if v < 2 else tiles - 1 - t
            for h in range(TILE // 128):
                cut = slice(h * 128, (h + 1) * 128)
                slices = {
                    f: c[from_t, f * 16 : (f + 1) * 16, cut].astype(F32)
                    for f in range(size)
                }
                sums = taps_sum(slices, zs, lambda z, i, j: num_ref[v * 16 + i * 3 + j : v * 16 + i * 3 + j + 1, :])
                for n, z in enumerate(zs):
                    recip_ref[at, t, n * 16 : (n + 1) * 16, cut] = (
                        1.0 / (along_y(sums[z]) + num_ref[v * 16 + 9 : v * 16 + 10, :])
                    ).astype(BF)
            return carry

        lax.fori_loop(0, tiles, divide, 0, unroll=True)


def main_kernel(frame, tiles, sides, at, table_ref, *refs):
    count = len(sides)
    index_refs, refs = refs[: count + 1], refs[count + 1 :]
    num_ref, est_ref, refs = refs[0], refs[1], refs[2:]
    own_refs, refs = refs[:4], refs[4:]
    far_refs, refs = refs[: 2 * count], refs[2 * count :]
    near_refs, beyond_refs = refs[:2], refs[2:4]
    recip_refs = refs[4:6]
    blocks_ref, frame_ref, out_ref = refs[6:9]
    m1, u2, m2, c0, c1, c2, c3, kept, wt, listed, bleach = refs[9:]
    even = lax.axis_index("gy") % 2 == 0
    c = [c0, c1, c2, c3]
    view = lax.axis_index("view")
    upside = lax.axis_index("gz") if frame.mirrored else 0
    depth = frame.depth
    z3, z2, z1, z0 = (frame.need(r) for r in (3, 2, 1, 0))
    sent = frame.sent(3)

    listed[...] = jnp.zeros(listed.shape, F32)
    listed[0:4, : table_ref.shape[1]] = table_ref[...]
    for n, ref in enumerate(index_refs):
        bleach[n * 16 : (n + 1) * 16, :] = bleach_weights(
            ref[0, at : at + 8, :128].astype(F32), listed[...]
        )
    for f in z2:
        where, k = frame.source(f)
        n = 0 if where == "own" else 1 + sides.index(where)
        over = upside if where == "own" else 1 - upside
        raw = n * 16 + (k + over * (depth - 1 - 2 * k) if frame.mirrored else k)
        weights = [bleach[pl.ds(raw + v * depth, 1), :] for v in range(4)]
        total = (weights[0] + weights[1]) + (weights[2] + weights[3])
        for v in range(4):
            mine = bleach[pl.ds(raw + (view ^ v) * depth, 1), :]
            to = (v * frame.size + f) * 16
            wt[to : to + 16, :] = num_ref[v * 16 : (v + 1) * 16, :] * (mine / total)

    def weighted(v, z, n):
        at = (v * frame.size + z) * 16 + 8 - n
        return wt[at : at + 1, :]

    def measured(v, t, z, cut):
        where, k = frame.source(z)
        if where == "own":
            own = own_refs[v][t, k * 8 : (k + 1) * 8, cut]
        else:
            k = k - sent[where].start
            far = far_refs[(count if v else 0) + sides.index(where)]
            own = far[v - 1 if v else 0, t, k * 8 : (k + 1) * 8, cut]
        n = frame.place(z, 3)
        one_ref, two_ref = near_refs if n < depth else beyond_refs
        n = n if n < depth else n - depth
        return jnp.concatenate(
            [
                own.astype(F32),
                beside(
                    even,
                    one_ref[v, t, n, :, cut],
                    two_ref[v, t, n, :, cut],
                ),
            ],
            axis=0,
        )

    def mix(v, t, z, cut, recip_a, recip_b):
        a = (measured(v, t, z, cut) * recip_a).astype(BF).astype(F32)
        b = (measured(v + 2, t, z, cut) * recip_b).astype(BF).astype(F32)
        return (0.5 * (a + b)).astype(BF)

    for ref in (m1, u2, m2):
        zero_ends(ref)

    for v in range(2):

        def ratios(t, carry, v=v):
            for h in range(TILE // 128):
                cut = slice(h * 128, (h + 1) * 128)
                to, lanes = spots(t, h)
                for n, z in enumerate(z3):
                    at = slice(n * 16, (n + 1) * 16)
                    m1[to, at, lanes] = mix(
                        v,
                        t,
                        z,
                        cut,
                        recip_refs[0][v, t, at, cut].astype(F32),
                        recip_refs[1][v, t, at, cut].astype(F32),
                    )
            return carry

        lax.fori_loop(0, tiles, ratios, 0, unroll=True)
        for w in (v, v + 2):
            conv(m1, 0, tiles, m1.shape[1], blocks_ref.at[backward_block(w)], c[w], 2)

    def numerator(slices_of, zs):
        totals = {z: [None, None, None] for z in zs}
        for v in range(4):
            slices = slices_of(v)
            sums = taps_sum(
                slices,
                zs,
                lambda z, i, j, v=v: weighted(v, z, i * 3 + j),
            )
            for z in zs:
                for j in range(3):
                    old = totals[z][j]
                    totals[z][j] = sums[z][j] if old is None else old + sums[z][j]
        return totals

    def update(t, carry):
        for h in range(TILE // 128):
            cut = slice(h * 128, (h + 1) * 128)

            def slices_of(v):
                from_t = t if v < 2 else tiles - 1 - t
                return {
                    z: c[v][from_t, n * 16 : (n + 1) * 16, cut].astype(F32)
                    for n, z in enumerate(z3)
                }

            to, lanes = spots(t, h)
            totals = numerator(slices_of, z2)
            for n, z in enumerate(z2):
                change = along_y(totals[z])
                before = frame_ref[to, z * 16 : (z + 1) * 16, lanes].astype(F32)
                u2[to, n * 16 : (n + 1) * 16, lanes] = (before * change).astype(BF)
                if z in z0:
                    k = z - frame.own
                    kept[t, k * 8 : (k + 1) * 8, cut] = change[:8]
        return carry

    lax.fori_loop(0, tiles, update, 0, unroll=True)

    rows1 = m2.shape[1]
    n2 = u2.shape[1]
    for v in range(2):
        for w in (v, v + 2):
            conv(u2, 0, tiles, n2, blocks_ref.at[forward_block(w)], c[w].at[:, :n2, :], 2)

        def ratios2(t, carry, v=v):
            for h in range(TILE // 128):
                cut = slice(h * 128, (h + 1) * 128)
                recips = []
                for w in (v, v + 2):
                    from_t = t if w < 2 else tiles - 1 - t
                    slices = {
                        z: c[w][from_t, n * 16 : (n + 1) * 16, cut].astype(F32)
                        for n, z in enumerate(z2)
                    }
                    sums = taps_sum(
                        slices, z1, lambda z, i, j, w=w: num_ref[w * 16 + i * 3 + j : w * 16 + i * 3 + j + 1, :]
                    )
                    recips.append(
                        {z: 1.0 / (along_y(sums[z]) + num_ref[w * 16 + 9 : w * 16 + 10, :]) for z in z1}
                    )
                to, lanes = spots(t, h)
                for n, z in enumerate(z1):
                    m2[to, n * 16 : (n + 1) * 16, lanes] = mix(
                        v, t, z, cut, recips[0][z], recips[1][z]
                    )
            return carry

        lax.fori_loop(0, tiles, ratios2, 0, unroll=True)
        mine = tiles // 4
        for w in (v, v + 2):
            first = view * mine if w < 2 else tiles - (view + 1) * mine
            conv(m2, first, mine, rows1, blocks_ref.at[backward_block(w)], c[w].at[:, :rows1, :], 2)

    mine = tiles // 4
    for s in range(mine):
        for h in range(TILE // 128):
            cut = slice(h * 128, (h + 1) * 128)

            def slices_of(v):
                from_s = s if v < 2 else mine - 1 - s
                return {
                    z: c[v][from_s, n * 16 : (n + 1) * 16, cut].astype(F32)
                    for n, z in enumerate(z1)
                }

            totals = numerator(slices_of, z0)
            for z in z0:
                k = z - frame.own
                to = k + upside * (depth - 1 - 2 * k)
                lanes = slice(s * TILE + h * 128, s * TILE + (h + 1) * 128)
                first_change = kept[view * mine + s, k * 8 : (k + 1) * 8, cut]
                out_ref[to, :, lanes] = (
                    est_ref[to, :, lanes] * first_change * along_y(totals[z])[:8]
                )


def shards(
    pieces, piece_owner, piece_row, estimate, psf_x, stencil, background, bleach_table, bleach_index
):
    depth, height, chunk = estimate.shape
    width = pieces.shape[3]
    tiles = width // TILE
    slabs = lax.axis_size("gz")
    bands = lax.axis_size("gy")
    blocks = slabs * bands
    frame = Frame(slabs, depth)
    size = frame.size
    sides = tuple(frame.sent(1))
    vmem, smem = pltpu.VMEM, pltpu.SMEM
    params = pltpu.CompilerParams(vmem_limit_bytes=LIMIT)

    def stay(array):
        return pltpu.with_memory_space_constraint(array, pltpu.VMEM)

    given = [piece_row, estimate, psf_x, bleach_table]
    given += [pieces[0], stencil.transpose(1, 0, 2), piece_owner.transpose(0, 2, 1)]
    first_pieces, first_taps, first_owner = given[-3:]

    def is_given(x):
        return any(x is y for y in given)

    def call(kernel, shapes, ins, outs, *args, scratch=()):
        args = [
            (
                pltpu.with_memory_space_constraint(x, pltpu.HBM)
                if is_given(x)
                else stay(x)
                if space is vmem
                else x
            )
            for space, x in zip(ins, args)
        ]
        out = pl.pallas_call(
            kernel,
            out_shape=shapes,
            in_specs=whole(*ins),
            out_specs=whole(*outs) if isinstance(shapes, tuple) else whole(*outs)[0],
            scratch_shapes=list(scratch),
            compiler_params=params,
        )(*args)
        return out

    def resident(*dims, dtype=BF):
        return pltpu.VMEM(dims, dtype)

    mark = jax.ShapeDtypeStruct((8, 128), F32)

    free = pl.ANY
    area = depth * height

    pairs = blocks // 2
    half_cells = resident(pairs, depth, height, width)
    even, odd, payload = call(
        functools.partial(first_kernel, pairs, bands, frame.mirrored),
        (half_cells, half_cells, resident(area + 8, chunk)),
        (smem, smem, smem, smem, vmem, vmem, vmem, vmem),
        (vmem, vmem, vmem),
        first_owner,
        piece_row,
        background,
        bleach_index,
        first_pieces,
        first_taps,
        estimate,
        psf_x,
        scratch=[vmem((blocks * depth, height, width), F32), vmem((8, chunk), F32)],
    )
    other = swap(odd, "gy", bands, 1)
    near_payload = swap(payload, "view", 4, 1)
    *kept, pair, sums_done = call(
        functools.partial(sum_kernel, pairs),
        (resident(depth, height, width),) * pairs
        + (resident(2, area + 8, chunk), mark),
        [vmem] * 4,
        [vmem] * (pairs + 2),
        even,
        other,
        payload,
        near_payload,
    )
    heard = (pair, swap(pair, "view", 4, 2))
    moved = [swap(kept[k], ("gz", "gy"), blocks, 2 * k) for k in range(1, pairs)]

    def stack(arrays, slices, *tokens):
        rows = slice(slices.start * height, slices.stop * height)
        dims = (len(arrays),) + arrays[0].shape[:-2] + (len(slices) * height, arrays[0].shape[-1])
        return call(
            functools.partial(stack_kernel, rows, len(arrays)),
            (resident(*dims), mark),
            [vmem] * len(arrays) + [free] + [vmem] * (len(tokens) - 1),
            (vmem, vmem),
            *arrays,
            *tokens,
        )

    def edges(arrays, fars, token, slices, dims):
        out = resident(4, *dims[:-2], slices, height // 2, dims[-1])
        return call(
            functools.partial(
                edges_kernel,
                height,
                depth if arrays else 0,
                len(sides),
                len(arrays) == 2,
            ),
            (out, out, mark),
            [vmem] * (len(arrays) + len(fars)) + [free],
            (vmem, vmem, vmem),
            *arrays,
            *fars,
            token,
        )

    far_slices = frame.sent(3)
    plain, turned, *own_far, total_done = call(
        functools.partial(
            total_kernel,
            pairs,
            [slice(s.start * height, s.stop * height) for s in far_slices.values()],
        ),
        (resident(tiles, area, TILE), resident(tiles, area, TILE))
        + tuple(resident(1, tiles, len(s) * height, TILE) for s in far_slices.values())
        + (mark,),
        [vmem] * pairs + [free],
        [vmem] * (3 + len(sides)),
        kept[0],
        *moved,
        sums_done,
    )
    near = swap(plain, "view", 4, 1)
    opposite = swap(turned, "view", 4, 2)
    last = swap(opposite, "view", 4, 1)
    ready = dict(zip([(s.start, s.stop) for s in far_slices.values()], own_far))
    table, nums, token = call(
        functools.partial(band_kernel, area),
        (resident(6, 2 * TILE, TILE), resident(64, 128, dtype=F32), mark),
        [vmem] * 3,
        (vmem, vmem, vmem),
        *heard,
        near,
    )
    kept_table, kept_nums = table, nums

    def est_rows(slices):
        return call(
            est_rows_kernel,
            resident(4, area + 8, chunk),
            [vmem] * 2 + [free],
            (vmem,),
            *heard,
            total_done,
        )

    far_est = exchange_z(frame, est_rows, slabs, depth)
    far_est = [far_est[s] for s in sides]
    est_edges = edges(heard, far_est, total_done, size, payload.shape)
    one_est, two_est = core_side(est_edges, bands, True)
    far_own = exchange_z(frame, lambda s: ready[s.start, s.stop], slabs, 3)
    far_own = [far_own[s] for s in sides]
    n3, n2, n1 = (len(frame.need(r)) * 16 for r in (3, 2, 1))

    scratch = [vmem((tiles, size * 16, TILE), BF)]
    tokens = []

    def others(slices):
        rows, done = stack(
            (near, opposite, last), slices, total_done, one_est, two_est
        )
        tokens.append(done)
        return rows

    far_others = exchange_z(frame, others, slabs, 3)
    far_others = [far_others[s] for s in sides]
    own_edges = edges((plain, near, opposite, last), (), tokens[-1], depth, plain.shape)
    near_halo = core_side(own_edges, bands, False)
    est_frame, recip_a, token = call(
        functools.partial(start_kernel, frame, tiles, sides, (0, 1)),
        (
            resident(tiles + 1, size * 16, TILE),
            resident(2, tiles, n3, TILE),
            mark,
        ),
        [vmem] * (6 + len(sides)) + [free],
        (vmem, vmem, vmem),
        kept_nums,
        kept_table,
        *heard,
        *far_est,
        one_est,
        two_est,
        own_edges[2],
        scratch=scratch,
    )
    far_edges = edges(
        (), far_own + far_others, token, len(frame.need(3)) - depth, plain.shape
    )
    far_halo = core_side(far_edges, bands, False)
    recip_b, token_b = call(
        functools.partial(forward_kernel, frame, tiles, (2, 3)),
        (resident(2, tiles, n3, TILE), mark),
        (vmem, vmem, vmem, free),
        (vmem, vmem),
        kept_nums,
        kept_table,
        est_frame,
        far_edges[2],
        scratch=scratch,
    )
    return call(
        functools.partial(main_kernel, frame, tiles, sides, area),
        jax.ShapeDtypeStruct(estimate.shape, F32),
        [vmem] * (16 + 3 * len(sides)),
        (vmem,),
        bleach_table,
        pair,
        *far_est,
        kept_nums,
        estimate,
        plain,
        near,
        opposite,
        last,
        *far_own,
        *far_others,
        *near_halo,
        *far_halo,
        recip_a,
        recip_b,
        kept_table,
        est_frame,
        scratch=[
            vmem((tiles + 1, n3, TILE), BF),
            vmem((tiles + 1, n2, TILE), BF),
            vmem((tiles + 1, n1, TILE), BF),
        ]
        + [vmem((tiles, n3, TILE), BF)] * 4
        + [vmem((tiles, area, TILE), F32), vmem((4 * size * 16, 128), F32)]
        + [vmem((8, 128), F32), vmem(((1 + len(sides)) * 16, 128), F32)],
    )


def solution(mesh):
    placed = (
        P("view", ("gz", "gy"), None, None),
        P("view", ("gz", "gy"), None),
        P("view", ("gz", "gy")),
        P("gz", "gy", "view"),
        P("view", None),
        P("view", None, None),
        P("view"),
        P(),
        P(None, "gz"),
    )
    return jax.shard_map(
        shards, mesh=mesh, in_specs=placed, out_specs=P("gz", "gy", "view"), check_vma=False
    )
```

```python
import functools

import jax
import jax.numpy as jnp
from jax import lax
from jax.experimental import pallas as pl
from jax.experimental.pallas import tpu as pltpu
from jax.sharding import PartitionSpec as P

BF = jnp.bfloat16
F32 = jnp.float32
TILE = 256
LIMIT = 24 << 20


def whole(*spaces):
    return [pl.BlockSpec(memory_space=space) for space in spaces]


def swap(array, axis, size, mask):
    return lax.ppermute(array, axis, [(i, i ^ mask) for i in range(size)])


def core_side(own, bands, all_take_part):
    first = swap(own[0], "gy", bands, 1)
    if all_take_part:
        return first, swap(own[1], "gy", bands, 3)
    return first, lax.ppermute(own[1], "gy", [(1, 2), (2, 1)])


def upward(array, axis, size):
    return lax.ppermute(array, axis, [(i, i + 1) for i in range(size - 1)])


def downward(array, axis, size):
    return lax.ppermute(array, axis, [(i + 1, i) for i in range(size - 1)])


class Frame:
    def __init__(self, slabs, depth):
        self.mirrored = slabs == 2
        self.depth = depth
        self.own = 0 if self.mirrored else depth
        self.size = 2 * depth if self.mirrored else 3 * depth

    def need(self, radius):
        return range(
            max(0, self.own - radius), min(self.size, self.own + self.depth + radius)
        )

    def source(self, f):
        k = f - self.own
        if 0 <= k < self.depth:
            return "own", k
        if self.mirrored:
            return "up", 2 * self.depth - 1 - k
        return ("dn", f) if k < 0 else ("up", k - self.depth)

    def place(self, f, radius):
        where, k = self.source(f)
        at = 0
        for name, slices in [("own", range(self.depth))] + list(self.sent(radius).items()):
            if name == where:
                return at + k - slices.start
            at += len(slices)

    def sent(self, radius):
        if self.mirrored:
            return {"up": range(self.depth - radius, self.depth)}
        return {
            "dn": range(self.depth - radius, self.depth),
            "up": range(0, radius),
        }


def exchange_z(frame, make, slabs, radius):
    got = {}
    for side, slices in frame.sent(radius).items():
        payload = make(slices)
        if frame.mirrored:
            got[side] = swap(payload, "gz", slabs, 1)
        elif side == "dn":
            got[side] = upward(payload, "gz", slabs)
        else:
            got[side] = downward(payload, "gz", slabs)
    return got


def place():
    return lax.axis_index("view"), lax.axis_index("gz")


def first_kernel(
    pairs,
    bands,
    mirrored,
    owner_ref,
    row_ref,
    bg_ref,
    index_ref,
    pieces_ref,
    taps_ref,
    est_ref,
    psf_ref,
    even_ref,
    odd_ref,
    payload_ref,
    acc,
    tail,
):
    write_payload(mirrored, bg_ref, index_ref, taps_ref, est_ref, psf_ref, payload_ref, tail)
    count = pieces_ref.shape[0]
    depth = even_ref.shape[1]
    me = lax.axis_index("gz") * bands + lax.axis_index("gy")

    def clear(i, carry):
        acc[i] = jnp.zeros(acc.shape[1:], F32)
        return carry

    lax.fori_loop(0, acc.shape[0], clear, 0)

    def add(i, carry):
        owner = owner_ref[0, 0, i]
        row = row_ref[0, i]
        if mirrored:
            row = jnp.where(owner >= bands, depth - 1 - row, row)
        c = (owner ^ me) * depth + row
        acc[c] = acc[c] + pieces_ref[i].astype(F32)
        return carry

    lax.fori_loop(0, count, add, 0)

    def put(pair, carry):
        for f in range(depth):
            even_ref[pair, f] = acc[pair * 2 * depth + f].astype(BF)
            odd_ref[pair, f] = acc[(pair * 2 + 1) * depth + f].astype(BF)
        return carry

    lax.fori_loop(0, pairs, put, 0)


def write_payload(mirrored, bg_ref, index_ref, taps_ref, est_ref, psf_ref, out_ref, tail):
    depth, height = est_ref.shape[:2]
    upside = lax.axis_index("gz") if mirrored else 0
    for k in range(depth):
        out_ref[k * height : (k + 1) * height, :] = est_ref[
            k + upside * (depth - 1 - 2 * k)
        ].astype(BF)
    tail[...] = jnp.zeros(tail.shape, F32)
    for i in range(3):
        tail[0:1, 3 * i : 3 * i + 3] = taps_ref[i + upside * (2 - 2 * i)]
    lanes = lax.broadcasted_iota(jnp.int32, (1, 128), 1)
    exact = jnp.where(lanes == 9, bg_ref[0], tail[0:1, :128])
    for n in range(3):
        part = exact.astype(BF).astype(F32)
        tail[n + 1 : n + 2, :128] = part
        exact = exact - part
    levels = jnp.zeros((1, 128), F32)
    for v in range(4):
        for k in range(depth):
            level = jnp.full((1, 128), index_ref[v, k], jnp.int32).astype(F32)
            levels = jnp.where(lanes == v * depth + k, level, levels)
    tail[4:5, :128] = levels
    tail[0:1, : psf_ref.shape[1]] = psf_ref[...]
    out_ref[depth * height :, :] = tail[...].astype(BF)


def bleach_weights(rows, table):
    wide = jnp.broadcast_to(rows[4:5], (16, 128))
    down = lax.broadcasted_iota(jnp.int32, (16, 128), 0)
    across = lax.broadcasted_iota(jnp.int32, (16, 128), 1)
    level = jnp.sum(jnp.where(down == across, wide, 0.0), axis=1, keepdims=True)
    listed = jnp.broadcast_to(table[0:1], (16, 128))
    for v in range(1, 4):
        listed = jnp.where(down // 4 == v, jnp.broadcast_to(table[v : v + 1], (16, 128)), listed)
    hit = across.astype(F32) == level
    weight = jnp.sum(jnp.where(hit, listed, 0.0), axis=1, keepdims=True)
    return jnp.broadcast_to(weight, (16, 128))


def numbers_of(heard, at):
    rows = heard[at : at + 8, :128].astype(F32)
    exact = rows[1:2] + rows[2:3] + rows[3:4]
    wide = jnp.broadcast_to(exact, (16, 128))
    spot = lax.broadcasted_iota(jnp.int32, (16, 128), 0) == lax.broadcasted_iota(
        jnp.int32, (16, 128), 1
    )
    column = jnp.sum(jnp.where(spot, wide, 0.0), axis=1, keepdims=True)
    return jnp.broadcast_to(column, (16, 128))


def sum_kernel(pairs, *refs):
    even_ref, other_ref, own_ref, near_ref = refs[:4]
    sums, (pair_ref, done_ref) = refs[4 : 4 + pairs], refs[4 + pairs :]
    done_ref[...] = jnp.zeros(done_ref.shape, F32)
    for k in range(pairs):
        sums[k][...] = (even_ref[k].astype(F32) + other_ref[k].astype(F32)).astype(BF)
    pair_ref[0] = own_ref[...]
    pair_ref[1] = near_ref[...]


def views_of(first, second):
    return [first.at[0], first.at[1], second.at[0], second.at[1]]


def est_rows_kernel(first, second, _, out_ref):
    for v, ref in enumerate(views_of(first, second)):
        out_ref[v] = ref[...]


def stack_kernel(rows, count, *refs):
    ins, (out_ref, done_ref) = refs[:count], refs[-2:]
    done_ref[...] = jnp.zeros(done_ref.shape, F32)
    for v, ref in enumerate(ins):
        out_ref[v] = ref[..., rows, :]


def edges_kernel(height, depth, sides, paired, *refs):
    out1, out2, done_ref = refs[-3:]
    done_ref[...] = jnp.zeros(done_ref.shape, F32)
    count = out1.shape[0]
    views = refs[:count] if depth else [None] * count
    fars = refs[count if depth else 0 : -4]
    if paired:
        views, fars = views_of(*refs[:2]), refs[2:-4]
    half = height // 2
    gy = lax.axis_index("gy")
    even = gy % 2 == 0
    inner = (gy == 1) | (gy == 2)
    lead = out1.shape[1:-3]

    def put(at, block):
        turned = pltpu.roll(block, half, block.ndim - 2)
        one = jnp.where(even, turned, block)
        two = jnp.where(inner, jnp.where(even, block, turned), 0.0)
        out1[at] = one[..., :half, :].astype(BF)
        out2[at] = two[..., :half, :].astype(BF)

    def far_of(v, side):
        for ref in fars[side::sides]:
            if v < ref.shape[0]:
                return ref.at[v]
            v -= ref.shape[0]

    for v, own in enumerate(views):
        n = 0
        sources = [(depth, own)] if depth else []
        if fars:
            sources += [
                (min(4, fars[side].shape[-2] // height), far_of(v, side)) for side in range(sides)
            ]
        for number, source in sources:
            for k in range(number):
                rows = slice(k * height, (k + 1) * height)
                if lead:

                    def one_tile(t, carry, v=v, n=n, source=source, rows=rows):
                        put((v, t, n), source[t, rows, :].astype(F32))
                        return carry

                    lax.fori_loop(0, lead[0], one_tile, 0, unroll=True)
                else:
                    put((v, n), source[rows, :].astype(F32))
                n += 1


def beside(even, one, two):
    one, two = one.astype(F32), two.astype(F32)
    return jnp.where(
        even, jnp.concatenate([one, two], axis=0), jnp.concatenate([two, one], axis=0)
    )


def reversal():
    rows = lax.broadcasted_iota(jnp.int32, (TILE, TILE), 0)
    cols = lax.broadcasted_iota(jnp.int32, (TILE, TILE), 1)
    return jnp.where(rows + cols == TILE - 1, F32(1.0), F32(0.0)).astype(BF)


def total_kernel(parts, far_rows, *refs):
    ins, (out_ref, rev_ref, *far_refs, done_ref) = refs[:parts], refs[parts + 1 :]
    done_ref[...] = jnp.zeros(done_ref.shape, F32)
    tiles, rows, _ = out_ref.shape
    for t in range(tiles):
        cut = slice(t * TILE, (t + 1) * TILE)
        acc = ins[0][:, :, cut].astype(F32)
        for ref in ins[1:]:
            acc = acc + ref[:, :, cut].astype(F32)
        block = acc.reshape(rows, TILE).astype(BF)
        out_ref[t] = block
        for ref, part in zip(far_refs, far_rows):
            ref[0, t] = block[part]
    back = jnp.dot(
        out_ref[...].reshape(tiles * rows, TILE), reversal(), preferred_element_type=F32
    ).astype(BF)
    for t in range(tiles):
        rev_ref[tiles - 1 - t] = back[t * rows : (t + 1) * rows]


def band_kernel(at, *refs):
    heard, (out_ref, num_ref, done_ref) = views_of(*refs[:2]), refs[3:]
    done_ref[...] = jnp.zeros(done_ref.shape, F32)
    for v in range(4):
        num_ref[v * 16 : (v + 1) * 16, :] = numbers_of(heard[v], at)
    flip = reversal()
    for v in range(4):
        row = heard[v][at : at + 8, : 3 * 128].astype(F32)[0:1]
        edge = TILE // 2
        base = jnp.concatenate(
            [jnp.zeros((1, edge), F32), row, jnp.zeros((1, 2 * edge), F32)], axis=1
        )
        wide = pltpu.roll(
            jnp.broadcast_to(base, (TILE, 3 * TILE)), 0, 1, stride=1, stride_axis=0
        ).astype(BF)
        turned = jnp.dot(flip, wide, preferred_element_type=F32).astype(BF)
        half = TILE // 2
        for k, (rows, to) in enumerate(
            (
                (slice(half, TILE), slice(0, half)),
                (slice(0, TILE), slice(half, half + TILE)),
                (slice(0, half), slice(half + TILE, 2 * TILE)),
            )
        ):
            cut = slice(k * TILE, (k + 1) * TILE)
            across = slice((2 - k) * TILE, (3 - k) * TILE)
            if v >= 2:
                out_ref[2 + v, to, :] = turned[rows, cut]
            else:
                out_ref[2 + v, to, :] = wide[rows, across]
                out_ref[v, to, :] = jnp.dot(
                    turned[rows, cut], flip, preferred_element_type=F32
                ).astype(BF)


def forward_block(v):
    return v if v < 2 else v + 2


def backward_block(v):
    return v + 2


def spots(t, h):
    return t + h, slice((1 - h) * (TILE // 2), (2 - h) * (TILE // 2))


def zero_ends(ref):
    half = TILE // 2
    ref[0, :, :half] = jnp.zeros((ref.shape[1], half), BF)
    ref[ref.shape[0] - 1, :, half:] = jnp.zeros((ref.shape[1], half), BF)


def conv(src, first, tiles, rows, blocks, dst, step):
    s = 0
    while s < tiles:
        n = min(step, tiles - s)
        out = sum(
            jnp.dot(
                src[pl.ds(first + s + k, n)].reshape(n * rows, TILE),
                blocks[k * TILE : (k + 1) * TILE, :],
                preferred_element_type=F32,
            )
            for k in range(2)
        ).astype(BF)
        dst[s : s + n] = out.reshape(n, rows, TILE)
        s += n


def taps_sum(slices, zs, taps):
    result = {}
    for z in zs:
        sums = [None, None, None]
        for j in range(3):
            for i in range(3):
                at = z + i - 1
                if at in slices:
                    term = taps(z, i, j) * slices[at]
                    sums[j] = term if sums[j] is None else sums[j] + term
        result[z] = sums
    return result


def along_y(sums):
    n = sums[0].shape[0]
    return pltpu.roll(sums[0], 1, 0) + sums[1] + pltpu.roll(sums[2], n - 1, 0)


def write_frame(frame, tiles, sides, *refs):
    own_refs, refs = views_of(*refs[:2]), refs[2:]
    side_refs = dict(zip(sides, refs[: len(sides)]))
    one_ref, two_ref, out_ref = refs[len(sides) :]
    view = lax.axis_index("view")
    even = lax.axis_index("gy") % 2 == 0
    zero_ends(out_ref)
    for v in range(4):
        for s in range(tiles // 4 * 2):
            t, lanes = spots((view ^ v) * (tiles // 4) + s // 2, s % 2)
            cut = slice(s * TILE // 2, (s + 1) * TILE // 2)
            for f in range(frame.size):
                where, k = frame.source(f)
                rows = slice(k * 8, (k + 1) * 8)
                if where == "own":
                    own = own_refs[v][rows, cut]
                else:
                    own = side_refs[where][v, rows, cut]
                n = frame.place(f, frame.depth)
                out_ref[t, f * 16 : (f + 1) * 16, lanes] = jnp.concatenate(
                    [
                        own.astype(F32),
                        beside(even, one_ref[v, n, :, cut], two_ref[v, n, :, cut]),
                    ],
                    axis=0,
                ).astype(BF)


def start_kernel(frame, tiles, sides, views, num_ref, blocks_ref, *refs):
    count = len(sides)
    out_ref, recip_ref, done_ref, c = refs[5 + count :]
    write_frame(frame, tiles, sides, *refs[: 4 + count], out_ref)
    forward_views(frame, tiles, views, num_ref, blocks_ref, out_ref, recip_ref, c)
    done_ref[...] = jnp.zeros(done_ref.shape, F32)


def forward_kernel(frame, tiles, views, num_ref, blocks_ref, frame_ref, _, recip_ref, done_ref, c):
    forward_views(frame, tiles, views, num_ref, blocks_ref, frame_ref, recip_ref, c)
    done_ref[...] = jnp.zeros(done_ref.shape, F32)


def forward_views(frame, tiles, views, num_ref, blocks_ref, frame_ref, recip_ref, c):
    size = frame.size
    zs = frame.need(3)
    for at, v in enumerate(views):
        conv(frame_ref, 0, tiles, size * 16, blocks_ref.at[forward_block(v)], c, 2)

        def divide(t, carry, v=v, at=at):
            from_t = t if v < 2 else tiles - 1 - t
            for h in range(TILE // 128):
                cut = slice(h * 128, (h + 1) * 128)
                slices = {
                    f: c[from_t, f * 16 : (f + 1) * 16, cut].astype(F32)
                    for f in range(size)
                }
                sums = taps_sum(slices, zs, lambda z, i, j: num_ref[v * 16 + i * 3 + j : v * 16 + i * 3 + j + 1, :])
                for n, z in enumerate(zs):
                    recip_ref[at, t, n * 16 : (n + 1) * 16, cut] = (
                        1.0 / (along_y(sums[z]) + num_ref[v * 16 + 9 : v * 16 + 10, :])
                    ).astype(BF)
            return carry

        lax.fori_loop(0, tiles, divide, 0, unroll=True)


def main_kernel(frame, tiles, sides, at, table_ref, *refs):
    count = len(sides)
    index_refs, refs = refs[: count + 1], refs[count + 1 :]
    num_ref, est_ref, refs = refs[0], refs[1], refs[2:]
    own_refs, refs = refs[:4], refs[4:]
    far_refs, refs = refs[: 2 * count], refs[2 * count :]
    near_refs, beyond_refs = refs[:2], refs[2:4]
    recip_refs = refs[4:6]
    blocks_ref, frame_ref, out_ref = refs[6:9]
    m1a, m1b, u2, m2a, m2b, c0, c1, c2, c3, kept, wt, listed, bleach = refs[9:]
    m1s, m2s = (m1a, m1b), (m2a, m2b)
    even = lax.axis_index("gy") % 2 == 0
    c = [c0, c1, c2, c3]
    view = lax.axis_index("view")
    upside = lax.axis_index("gz") if frame.mirrored else 0
    depth = frame.depth
    z3, z2, z1, z0 = (frame.need(r) for r in (3, 2, 1, 0))
    sent = frame.sent(3)

    listed[...] = jnp.zeros(listed.shape, F32)
    listed[0:4, : table_ref.shape[1]] = table_ref[...]
    for n, ref in enumerate(index_refs):
        bleach[n * 16 : (n + 1) * 16, :] = bleach_weights(
            ref[0, at : at + 8, :128].astype(F32), listed[...]
        )
    for f in z2:
        where, k = frame.source(f)
        n = 0 if where == "own" else 1 + sides.index(where)
        over = upside if where == "own" else 1 - upside
        raw = n * 16 + (k + over * (depth - 1 - 2 * k) if frame.mirrored else k)
        weights = [bleach[pl.ds(raw + v * depth, 1), :] for v in range(4)]
        total = (weights[0] + weights[1]) + (weights[2] + weights[3])
        for v in range(4):
            mine = bleach[pl.ds(raw + (view ^ v) * depth, 1), :]
            to = (v * frame.size + f) * 16
            wt[to : to + 16, :] = num_ref[v * 16 : (v + 1) * 16, :] * (mine / total)

    def weighted(v, z, n):
        at = (v * frame.size + z) * 16 + 8 - n
        return wt[at : at + 1, :]

    def measured(v, t, z, cut):
        where, k = frame.source(z)
        if where == "own":
            own = own_refs[v][t, k * 8 : (k + 1) * 8, cut]
        else:
            k = k - sent[where].start
            far = far_refs[(count if v else 0) + sides.index(where)]
            own = far[v - 1 if v else 0, t, k * 8 : (k + 1) * 8, cut]
        n = frame.place(z, 3)
        one_ref, two_ref = near_refs if n < depth else beyond_refs
        n = n if n < depth else n - depth
        return jnp.concatenate(
            [
                own.astype(F32),
                beside(
                    even,
                    one_ref[v, t, n, :, cut],
                    two_ref[v, t, n, :, cut],
                ),
            ],
            axis=0,
        )

    def mix(v, t, z, cut, recip_a, recip_b):
        a = (measured(v, t, z, cut) * recip_a).astype(BF).astype(F32)
        b = (measured(v + 2, t, z, cut) * recip_b).astype(BF).astype(F32)
        return (0.5 * (a + b)).astype(BF)

    for ref in (m1a, m1b, u2, m2a, m2b):
        zero_ends(ref)

    for v in range(2):

        def ratios(t, carry, v=v):
            for h in range(TILE // 128):
                cut = slice(h * 128, (h + 1) * 128)
                to, lanes = spots(t, h)
                for n, z in enumerate(z3):
                    at = slice(n * 16, (n + 1) * 16)
                    m1s[v][to, at, lanes] = mix(
                        v,
                        t,
                        z,
                        cut,
                        recip_refs[0][v, t, at, cut].astype(F32),
                        recip_refs[1][v, t, at, cut].astype(F32),
                    )
            return carry

        lax.fori_loop(0, tiles, ratios, 0, unroll=True)
        for w in (v, v + 2):
            conv(m1s[v], 0, tiles, m1a.shape[1], blocks_ref.at[backward_block(w)], c[w], 2)

    def numerator(slices_of, zs):
        totals = {z: [None, None, None] for z in zs}
        for v in range(4):
            slices = slices_of(v)
            sums = taps_sum(
                slices,
                zs,
                lambda z, i, j, v=v: weighted(v, z, i * 3 + j),
            )
            for z in zs:
                for j in range(3):
                    old = totals[z][j]
                    totals[z][j] = sums[z][j] if old is None else old + sums[z][j]
        return totals

    def update(t, carry):
        for h in range(TILE // 128):
            cut = slice(h * 128, (h + 1) * 128)

            def slices_of(v):
                from_t = t if v < 2 else tiles - 1 - t
                return {
                    z: c[v][from_t, n * 16 : (n + 1) * 16, cut].astype(F32)
                    for n, z in enumerate(z3)
                }

            to, lanes = spots(t, h)
            totals = numerator(slices_of, z2)
            for n, z in enumerate(z2):
                change = along_y(totals[z])
                before = frame_ref[to, z * 16 : (z + 1) * 16, lanes].astype(F32)
                u2[to, n * 16 : (n + 1) * 16, lanes] = (before * change).astype(BF)
                if z in z0:
                    k = z - frame.own
                    kept[t, k * 8 : (k + 1) * 8, cut] = change[:8]
        return carry

    lax.fori_loop(0, tiles, update, 0, unroll=True)

    rows1 = m2a.shape[1]
    n2 = u2.shape[1]
    for w in (0, 2, 1, 3):
        conv(u2, 0, tiles, n2, blocks_ref.at[forward_block(w)], c[w].at[:, :n2, :], 2)
    for v in range(2):

        def ratios2(t, carry, v=v):
            for h in range(TILE // 128):
                cut = slice(h * 128, (h + 1) * 128)
                recips = []
                for w in (v, v + 2):
                    from_t = t if w < 2 else tiles - 1 - t
                    slices = {
                        z: c[w][from_t, n * 16 : (n + 1) * 16, cut].astype(F32)
                        for n, z in enumerate(z2)
                    }
                    sums = taps_sum(
                        slices, z1, lambda z, i, j, w=w: num_ref[w * 16 + i * 3 + j : w * 16 + i * 3 + j + 1, :]
                    )
                    recips.append(
                        {z: 1.0 / (along_y(sums[z]) + num_ref[w * 16 + 9 : w * 16 + 10, :]) for z in z1}
                    )
                to, lanes = spots(t, h)
                for n, z in enumerate(z1):
                    m2s[v][to, n * 16 : (n + 1) * 16, lanes] = mix(
                        v, t, z, cut, recips[0][z], recips[1][z]
                    )
            return carry

        lax.fori_loop(0, tiles, ratios2, 0, unroll=True)
        mine = tiles // 4
        for w in (v, v + 2):
            first = view * mine if w < 2 else tiles - (view + 1) * mine
            conv(m2s[v], first, mine, rows1, blocks_ref.at[backward_block(w)], c[w].at[:, :rows1, :], 2)

    mine = tiles // 4
    for s in range(mine):
        for h in range(TILE // 128):
            cut = slice(h * 128, (h + 1) * 128)

            def slices_of(v):
                from_s = s if v < 2 else mine - 1 - s
                return {
                    z: c[v][from_s, n * 16 : (n + 1) * 16, cut].astype(F32)
                    for n, z in enumerate(z1)
                }

            totals = numerator(slices_of, z0)
            for z in z0:
                k = z - frame.own
                to = k + upside * (depth - 1 - 2 * k)
                lanes = slice(s * TILE + h * 128, s * TILE + (h + 1) * 128)
                first_change = kept[view * mine + s, k * 8 : (k + 1) * 8, cut]
                out_ref[to, :, lanes] = (
                    est_ref[to, :, lanes] * first_change * along_y(totals[z])[:8]
                )


def shards(
    pieces, piece_owner, piece_row, estimate, psf_x, stencil, background, bleach_table, bleach_index
):
    depth, height, chunk = estimate.shape
    width = pieces.shape[3]
    tiles = width // TILE
    slabs = lax.axis_size("gz")
    bands = lax.axis_size("gy")
    blocks = slabs * bands
    frame = Frame(slabs, depth)
    size = frame.size
    sides = tuple(frame.sent(1))
    vmem, smem = pltpu.VMEM, pltpu.SMEM
    params = pltpu.CompilerParams(vmem_limit_bytes=LIMIT)

    def stay(array):
        return pltpu.with_memory_space_constraint(array, pltpu.VMEM)

    given = [piece_row, estimate, psf_x, bleach_table, bleach_index]
    given += [pieces[0], stencil.transpose(1, 0, 2), piece_owner.transpose(0, 2, 1)]
    first_pieces, first_taps, first_owner = given[-3:]

    def is_given(x):
        return any(x is y for y in given)

    def call(kernel, shapes, ins, outs, *args, scratch=()):
        args = [
            (
                pltpu.with_memory_space_constraint(x, pltpu.HBM)
                if is_given(x)
                else stay(x)
                if space is vmem
                else x
            )
            for space, x in zip(ins, args)
        ]
        out = pl.pallas_call(
            kernel,
            out_shape=shapes,
            in_specs=whole(*ins),
            out_specs=whole(*outs) if isinstance(shapes, tuple) else whole(*outs)[0],
            scratch_shapes=list(scratch),
            compiler_params=params,
        )(*args)
        return out

    def resident(*dims, dtype=BF):
        return pltpu.VMEM(dims, dtype)

    mark = jax.ShapeDtypeStruct((8, 128), F32)

    free = pl.ANY
    area = depth * height

    pairs = blocks // 2
    half_cells = resident(pairs, depth, height, width)
    even, odd, payload = call(
        functools.partial(first_kernel, pairs, bands, frame.mirrored),
        (half_cells, half_cells, resident(area + 8, chunk)),
        (smem, smem, smem, smem, vmem, vmem, vmem, vmem),
        (vmem, vmem, vmem),
        first_owner,
        piece_row,
        background,
        bleach_index,
        first_pieces,
        first_taps,
        estimate,
        psf_x,
        scratch=[vmem((blocks * depth, height, width), F32), vmem((8, chunk), F32)],
    )
    other = swap(odd, "gy", bands, 1)
    near_payload = swap(payload, "view", 4, 1)
    *kept, pair, sums_done = call(
        functools.partial(sum_kernel, pairs),
        (resident(depth, height, width),) * pairs
        + (resident(2, area + 8, chunk), mark),
        [vmem] * 4,
        [vmem] * (pairs + 2),
        even,
        other,
        payload,
        near_payload,
    )
    heard = (pair, swap(pair, "view", 4, 2))
    moved = [swap(kept[k], ("gz", "gy"), blocks, 2 * k) for k in range(1, pairs)]

    def stack(arrays, slices, *tokens):
        rows = slice(slices.start * height, slices.stop * height)
        dims = (len(arrays),) + arrays[0].shape[:-2] + (len(slices) * height, arrays[0].shape[-1])
        return call(
            functools.partial(stack_kernel, rows, len(arrays)),
            (resident(*dims), mark),
            [vmem] * len(arrays) + [free] + [vmem] * (len(tokens) - 1),
            (vmem, vmem),
            *arrays,
            *tokens,
        )

    def edges(arrays, fars, token, slices, dims):
        out = resident(4, *dims[:-2], slices, height // 2, dims[-1])
        return call(
            functools.partial(
                edges_kernel,
                height,
                depth if arrays else 0,
                len(sides),
                len(arrays) == 2,
            ),
            (out, out, mark),
            [vmem] * (len(arrays) + len(fars)) + [free],
            (vmem, vmem, vmem),
            *arrays,
            *fars,
            token,
        )

    far_slices = frame.sent(3)
    plain, turned, *own_far, total_done = call(
        functools.partial(
            total_kernel,
            pairs,
            [slice(s.start * height, s.stop * height) for s in far_slices.values()],
        ),
        (resident(tiles, area, TILE), resident(tiles, area, TILE))
        + tuple(resident(1, tiles, len(s) * height, TILE) for s in far_slices.values())
        + (mark,),
        [vmem] * pairs + [free],
        [vmem] * (3 + len(sides)),
        kept[0],
        *moved,
        sums_done,
    )
    near = swap(plain, "view", 4, 1)
    opposite = swap(turned, "view", 4, 2)
    last = swap(opposite, "view", 4, 1)
    ready = dict(zip([(s.start, s.stop) for s in far_slices.values()], own_far))
    table, nums, token = call(
        functools.partial(band_kernel, area),
        (resident(6, 2 * TILE, TILE), resident(64, 128, dtype=F32), mark),
        [vmem] * 3,
        (vmem, vmem, vmem),
        *heard,
        near,
    )
    kept_table, kept_nums = table, nums

    def est_rows(slices):
        return call(
            est_rows_kernel,
            resident(4, area + 8, chunk),
            [vmem] * 2 + [free],
            (vmem,),
            *heard,
            total_done,
        )

    far_est = exchange_z(frame, est_rows, slabs, depth)
    far_est = [far_est[s] for s in sides]
    est_edges = edges(heard, far_est, total_done, size, payload.shape)
    one_est, two_est = core_side(est_edges, bands, True)
    far_own = exchange_z(frame, lambda s: ready[s.start, s.stop], slabs, 3)
    far_own = [far_own[s] for s in sides]
    n3, n2, n1 = (len(frame.need(r)) * 16 for r in (3, 2, 1))

    scratch = [vmem((tiles, size * 16, TILE), BF)]
    tokens = []

    def others(slices):
        rows, done = stack(
            (near, opposite, last), slices, total_done, one_est, two_est
        )
        tokens.append(done)
        return rows

    far_others = exchange_z(frame, others, slabs, 3)
    far_others = [far_others[s] for s in sides]
    own_edges = edges((plain, near, opposite, last), (), tokens[-1], depth, plain.shape)
    near_halo = core_side(own_edges, bands, False)
    est_frame, recip_a, token = call(
        functools.partial(start_kernel, frame, tiles, sides, (0, 1)),
        (
            resident(tiles + 1, size * 16, TILE),
            resident(2, tiles, n3, TILE),
            mark,
        ),
        [vmem] * (6 + len(sides)) + [free],
        (vmem, vmem, vmem),
        kept_nums,
        kept_table,
        *heard,
        *far_est,
        one_est,
        two_est,
        own_edges[2],
        scratch=scratch,
    )
    far_edges = edges(
        (), far_own + far_others, token, len(frame.need(3)) - depth, plain.shape
    )
    far_halo = core_side(far_edges, bands, False)
    recip_b, token_b = call(
        functools.partial(forward_kernel, frame, tiles, (2, 3)),
        (resident(2, tiles, n3, TILE), mark),
        (vmem, vmem, vmem, free),
        (vmem, vmem),
        kept_nums,
        kept_table,
        est_frame,
        far_edges[2],
        scratch=scratch,
    )
    return call(
        functools.partial(main_kernel, frame, tiles, sides, area),
        jax.ShapeDtypeStruct(estimate.shape, F32),
        [vmem] * (16 + 3 * len(sides)),
        (vmem,),
        stay(bleach_table),
        pair,
        *far_est,
        kept_nums,
        stay(estimate),
        plain,
        near,
        opposite,
        last,
        *far_own,
        *far_others,
        *near_halo,
        *far_halo,
        recip_a,
        recip_b,
        kept_table,
        est_frame,
        scratch=[
            vmem((tiles + 1, n3, TILE), BF),
            vmem((tiles + 1, n3, TILE), BF),
            vmem((tiles + 1, n2, TILE), BF),
            vmem((tiles + 1, n1, TILE), BF),
            vmem((tiles + 1, n1, TILE), BF),
        ]
        + [vmem((tiles, n3, TILE), BF)] * 4
        + [vmem((tiles, area, TILE), F32), vmem((4 * size * 16, 128), F32)]
        + [vmem((8, 128), F32), vmem(((1 + len(sides)) * 16, 128), F32)],
    )


def solution(mesh):
    placed = (
        P("view", ("gz", "gy"), None, None),
        P("view", ("gz", "gy"), None),
        P("view", ("gz", "gy")),
        P("gz", "gy", "view"),
        P("view", None),
        P("view", None, None),
        P("view"),
        P(),
        P(None, "gz"),
    )
    return jax.shard_map(
        shards, mesh=mesh, in_specs=placed, out_specs=P("gz", "gy", "view"), check_vma=False
    )
```

```python
import functools

import jax
import jax.numpy as jnp
from jax import lax
from jax.experimental import pallas as pl
from jax.experimental.pallas import tpu as pltpu
from jax.sharding import PartitionSpec as P

BF = jnp.bfloat16
F32 = jnp.float32
TILE = 256
LIMIT = 24 << 20


def whole(*spaces):
    return [pl.BlockSpec(memory_space=space) for space in spaces]


def swap(array, axis, size, mask):
    return lax.ppermute(array, axis, [(i, i ^ mask) for i in range(size)])


def core_side(own, bands, all_take_part):
    first = swap(own[0], "gy", bands, 1)
    if all_take_part:
        return first, swap(own[1], "gy", bands, 3)
    return first, lax.ppermute(own[1], "gy", [(1, 2), (2, 1)])


def upward(array, axis, size):
    return lax.ppermute(array, axis, [(i, i + 1) for i in range(size - 1)])


def downward(array, axis, size):
    return lax.ppermute(array, axis, [(i + 1, i) for i in range(size - 1)])


class Frame:
    def __init__(self, slabs, depth):
        self.mirrored = slabs == 2
        self.depth = depth
        self.own = 0 if self.mirrored else depth
        self.size = 2 * depth if self.mirrored else 3 * depth

    def need(self, radius):
        return range(
            max(0, self.own - radius), min(self.size, self.own + self.depth + radius)
        )

    def source(self, f):
        k = f - self.own
        if 0 <= k < self.depth:
            return "own", k
        if self.mirrored:
            return "up", 2 * self.depth - 1 - k
        return ("dn", f) if k < 0 else ("up", k - self.depth)

    def place(self, f, radius):
        where, k = self.source(f)
        at = 0
        for name, slices in [("own", range(self.depth))] + list(self.sent(radius).items()):
            if name == where:
                return at + k - slices.start
            at += len(slices)

    def sent(self, radius):
        if self.mirrored:
            return {"up": range(self.depth - radius, self.depth)}
        return {
            "dn": range(self.depth - radius, self.depth),
            "up": range(0, radius),
        }


def exchange_z(frame, make, slabs, radius):
    got = {}
    for side, slices in frame.sent(radius).items():
        payload = make(slices)
        if frame.mirrored:
            got[side] = swap(payload, "gz", slabs, 1)
        elif side == "dn":
            got[side] = upward(payload, "gz", slabs)
        else:
            got[side] = downward(payload, "gz", slabs)
    return got


def place():
    return lax.axis_index("view"), lax.axis_index("gz")


def first_kernel(
    pairs,
    bands,
    mirrored,
    owner_ref,
    row_ref,
    bg_ref,
    index_ref,
    pieces_ref,
    taps_ref,
    est_ref,
    psf_ref,
    even_ref,
    odd_ref,
    payload_ref,
    acc,
    tail,
):
    write_payload(mirrored, bg_ref, index_ref, taps_ref, est_ref, psf_ref, payload_ref, tail)
    count = pieces_ref.shape[0]
    depth = even_ref.shape[1]
    me = lax.axis_index("gz") * bands + lax.axis_index("gy")

    def clear(i, carry):
        acc[i] = jnp.zeros(acc.shape[1:], F32)
        return carry

    lax.fori_loop(0, acc.shape[0], clear, 0)

    def add(i, carry):
        owner = owner_ref[0, 0, i]
        row = row_ref[0, i]
        if mirrored:
            row = jnp.where(owner >= bands, depth - 1 - row, row)
        c = (owner ^ me) * depth + row
        acc[c] = acc[c] + pieces_ref[i].astype(F32)
        return carry

    lax.fori_loop(0, count, add, 0)

    def put(pair, carry):
        for f in range(depth):
            even_ref[pair, f] = acc[pair * 2 * depth + f].astype(BF)
            odd_ref[pair, f] = acc[(pair * 2 + 1) * depth + f].astype(BF)
        return carry

    lax.fori_loop(0, pairs, put, 0)


def write_payload(mirrored, bg_ref, index_ref, taps_ref, est_ref, psf_ref, out_ref, tail):
    depth, height = est_ref.shape[:2]
    upside = lax.axis_index("gz") if mirrored else 0
    for k in range(depth):
        out_ref[k * height : (k + 1) * height, :] = est_ref[
            k + upside * (depth - 1 - 2 * k)
        ].astype(BF)
    tail[...] = jnp.zeros(tail.shape, F32)
    for i in range(3):
        tail[0:1, 3 * i : 3 * i + 3] = taps_ref[i + upside * (2 - 2 * i)]
    lanes = lax.broadcasted_iota(jnp.int32, (1, 128), 1)
    exact = jnp.where(lanes == 9, bg_ref[0], tail[0:1, :128])
    for n in range(3):
        part = exact.astype(BF).astype(F32)
        tail[n + 1 : n + 2, :128] = part
        exact = exact - part
    levels = jnp.zeros((1, 128), F32)
    for v in range(4):
        for k in range(depth):
            level = jnp.full((1, 128), index_ref[v, k], jnp.int32).astype(F32)
            levels = jnp.where(lanes == v * depth + k, level, levels)
    tail[4:5, :128] = levels
    tail[0:1, : psf_ref.shape[1]] = psf_ref[...]
    out_ref[depth * height :, :] = tail[...].astype(BF)


def bleach_weights(rows, table):
    wide = jnp.broadcast_to(rows[4:5], (16, 128))
    down = lax.broadcasted_iota(jnp.int32, (16, 128), 0)
    across = lax.broadcasted_iota(jnp.int32, (16, 128), 1)
    level = jnp.sum(jnp.where(down == across, wide, 0.0), axis=1, keepdims=True)
    listed = jnp.broadcast_to(table[0:1], (16, 128))
    for v in range(1, 4):
        listed = jnp.where(down // 4 == v, jnp.broadcast_to(table[v : v + 1], (16, 128)), listed)
    hit = across.astype(F32) == level
    weight = jnp.sum(jnp.where(hit, listed, 0.0), axis=1, keepdims=True)
    return jnp.broadcast_to(weight, (16, 128))


def numbers_of(heard, at):
    rows = heard[at : at + 8, :128].astype(F32)
    exact = rows[1:2] + rows[2:3] + rows[3:4]
    wide = jnp.broadcast_to(exact, (16, 128))
    spot = lax.broadcasted_iota(jnp.int32, (16, 128), 0) == lax.broadcasted_iota(
        jnp.int32, (16, 128), 1
    )
    column = jnp.sum(jnp.where(spot, wide, 0.0), axis=1, keepdims=True)
    return jnp.broadcast_to(column, (16, 128))


def sum_kernel(pairs, *refs):
    even_ref, other_ref, own_ref, near_ref = refs[:4]
    sums, (pair_ref, done_ref) = refs[4 : 4 + pairs], refs[4 + pairs :]
    done_ref[...] = jnp.zeros(done_ref.shape, F32)
    for k in range(pairs):
        sums[k][...] = (even_ref[k].astype(F32) + other_ref[k].astype(F32)).astype(BF)
    pair_ref[0] = own_ref[...]
    pair_ref[1] = near_ref[...]


def views_of(first, second):
    return [first.at[0], first.at[1], second.at[0], second.at[1]]


def est_rows_kernel(first, second, _, out_ref):
    for v, ref in enumerate(views_of(first, second)):
        out_ref[v] = ref[...]


def stack_kernel(rows, count, *refs):
    ins, (out_ref, done_ref) = refs[:count], refs[-2:]
    done_ref[...] = jnp.zeros(done_ref.shape, F32)
    for v, ref in enumerate(ins):
        out_ref[v] = ref[..., rows, :]


def edges_kernel(height, depth, sides, paired, unread, *refs):
    out1, out2, done_ref = refs[-3:]
    done_ref[...] = jnp.zeros(done_ref.shape, F32)
    count = out1.shape[0]
    views = refs[:count] if depth else [None] * count
    fars = refs[count if depth else 0 : -4 - unread]
    if paired:
        views, fars = views_of(*refs[:2]), refs[2 : -4 - unread]
    half = height // 2
    gy = lax.axis_index("gy")
    even = gy % 2 == 0
    inner = (gy == 1) | (gy == 2)
    lead = out1.shape[1:-3]

    def put(at, block):
        turned = pltpu.roll(block, half, block.ndim - 2)
        one = jnp.where(even, turned, block)
        two = jnp.where(inner, jnp.where(even, block, turned), 0.0)
        out1[at] = one[..., :half, :].astype(BF)
        out2[at] = two[..., :half, :].astype(BF)

    def far_of(v, side):
        for ref in fars[side::sides]:
            if v < ref.shape[0]:
                return ref.at[v]
            v -= ref.shape[0]

    for v, own in enumerate(views):
        n = 0
        sources = [(depth, own)] if depth else []
        if fars:
            sources += [
                (min(4, fars[side].shape[-2] // height), far_of(v, side)) for side in range(sides)
            ]
        for number, source in sources:
            for k in range(number):
                rows = slice(k * height, (k + 1) * height)
                if lead:

                    def one_tile(t, carry, v=v, n=n, source=source, rows=rows):
                        put((v, t, n), source[t, rows, :].astype(F32))
                        return carry

                    lax.fori_loop(0, lead[0], one_tile, 0, unroll=True)
                else:
                    put((v, n), source[rows, :].astype(F32))
                n += 1


def beside(even, one, two):
    one, two = one.astype(F32), two.astype(F32)
    return jnp.where(
        even, jnp.concatenate([one, two], axis=0), jnp.concatenate([two, one], axis=0)
    )


def reversal():
    rows = lax.broadcasted_iota(jnp.int32, (TILE, TILE), 0)
    cols = lax.broadcasted_iota(jnp.int32, (TILE, TILE), 1)
    return jnp.where(rows + cols == TILE - 1, F32(1.0), F32(0.0)).astype(BF)


def total_kernel(parts, far_rows, *refs):
    ins, (out_ref, rev_ref, *far_refs, done_ref) = refs[:parts], refs[parts + 1 :]
    done_ref[...] = jnp.zeros(done_ref.shape, F32)
    tiles, rows, _ = out_ref.shape
    for t in range(tiles):
        cut = slice(t * TILE, (t + 1) * TILE)
        acc = ins[0][:, :, cut].astype(F32)
        for ref in ins[1:]:
            acc = acc + ref[:, :, cut].astype(F32)
        block = acc.reshape(rows, TILE).astype(BF)
        out_ref[t] = block
        for ref, part in zip(far_refs, far_rows):
            ref[0, t] = block[part]
    back = jnp.dot(
        out_ref[...].reshape(tiles * rows, TILE), reversal(), preferred_element_type=F32
    ).astype(BF)
    for t in range(tiles):
        rev_ref[tiles - 1 - t] = back[t * rows : (t + 1) * rows]


def band_kernel(at, *refs):
    heard, (out_ref, num_ref, done_ref) = views_of(*refs[:2]), refs[3:]
    done_ref[...] = jnp.zeros(done_ref.shape, F32)
    for v in range(4):
        num_ref[v * 16 : (v + 1) * 16, :] = numbers_of(heard[v], at)
    flip = reversal()
    for v in range(4):
        row = heard[v][at : at + 8, : 3 * 128].astype(F32)[0:1]
        edge = TILE // 2
        base = jnp.concatenate(
            [jnp.zeros((1, edge), F32), row, jnp.zeros((1, 2 * edge), F32)], axis=1
        )
        wide = pltpu.roll(
            jnp.broadcast_to(base, (TILE, 3 * TILE)), 0, 1, stride=1, stride_axis=0
        ).astype(BF)
        turned = jnp.dot(flip, wide, preferred_element_type=F32).astype(BF)
        half = TILE // 2
        for k, (rows, to) in enumerate(
            (
                (slice(half, TILE), slice(0, half)),
                (slice(0, TILE), slice(half, half + TILE)),
                (slice(0, half), slice(half + TILE, 2 * TILE)),
            )
        ):
            cut = slice(k * TILE, (k + 1) * TILE)
            across = slice((2 - k) * TILE, (3 - k) * TILE)
            if v >= 2:
                out_ref[2 + v, to, :] = turned[rows, cut]
            else:
                out_ref[2 + v, to, :] = wide[rows, across]
                out_ref[v, to, :] = jnp.dot(
                    turned[rows, cut], flip, preferred_element_type=F32
                ).astype(BF)


def forward_block(v):
    return v if v < 2 else v + 2


def backward_block(v):
    return v + 2


def spots(t, h):
    return t + h, slice((1 - h) * (TILE // 2), (2 - h) * (TILE // 2))


def zero_ends(ref):
    half = TILE // 2
    ref[0, :, :half] = jnp.zeros((ref.shape[1], half), BF)
    ref[ref.shape[0] - 1, :, half:] = jnp.zeros((ref.shape[1], half), BF)


def conv(src, first, tiles, rows, blocks, dst, step):
    s = 0
    while s < tiles:
        n = min(step, tiles - s)
        out = sum(
            jnp.dot(
                src[pl.ds(first + s + k, n)].reshape(n * rows, TILE),
                blocks[k * TILE : (k + 1) * TILE, :],
                preferred_element_type=F32,
            )
            for k in range(2)
        ).astype(BF)
        dst[s : s + n] = out.reshape(n, rows, TILE)
        s += n


def taps_sum(slices, zs, taps):
    result = {}
    for z in zs:
        sums = [None, None, None]
        for j in range(3):
            for i in range(3):
                at = z + i - 1
                if at in slices:
                    term = taps(z, i, j) * slices[at]
                    sums[j] = term if sums[j] is None else sums[j] + term
        result[z] = sums
    return result


def along_y(sums):
    n = sums[0].shape[0]
    return pltpu.roll(sums[0], 1, 0) + sums[1] + pltpu.roll(sums[2], n - 1, 0)


def write_frame(frame, tiles, sides, *refs):
    own_refs, refs = views_of(*refs[:2]), refs[2:]
    side_refs = dict(zip(sides, refs[: len(sides)]))
    one_ref, two_ref, out_ref = refs[len(sides) :]
    view = lax.axis_index("view")
    even = lax.axis_index("gy") % 2 == 0
    zero_ends(out_ref)
    for v in range(4):
        for s in range(tiles // 4 * 2):
            t, lanes = spots((view ^ v) * (tiles // 4) + s // 2, s % 2)
            cut = slice(s * TILE // 2, (s + 1) * TILE // 2)
            for f in range(frame.size):
                where, k = frame.source(f)
                rows = slice(k * 8, (k + 1) * 8)
                if where == "own":
                    own = own_refs[v][rows, cut]
                else:
                    own = side_refs[where][v, rows, cut]
                n = frame.place(f, frame.depth)
                out_ref[t, f * 16 : (f + 1) * 16, lanes] = jnp.concatenate(
                    [
                        own.astype(F32),
                        beside(even, one_ref[v, n, :, cut], two_ref[v, n, :, cut]),
                    ],
                    axis=0,
                ).astype(BF)


def start_kernel(frame, tiles, sides, views, num_ref, blocks_ref, *refs):
    count = len(sides)
    out_ref, recip_ref, done_ref, c = refs[5 + count :]
    write_frame(frame, tiles, sides, *refs[: 4 + count], out_ref)
    forward_views(frame, tiles, views, num_ref, blocks_ref, out_ref, recip_ref, c)
    done_ref[...] = jnp.zeros(done_ref.shape, F32)


def forward_kernel(frame, tiles, views, num_ref, blocks_ref, frame_ref, _, recip_ref, done_ref, c):
    forward_views(frame, tiles, views, num_ref, blocks_ref, frame_ref, recip_ref, c)
    done_ref[...] = jnp.zeros(done_ref.shape, F32)


def forward_views(frame, tiles, views, num_ref, blocks_ref, frame_ref, recip_ref, c):
    size = frame.size
    zs = frame.need(3)
    for at, v in enumerate(views):
        conv(frame_ref, 0, tiles, size * 16, blocks_ref.at[forward_block(v)], c, 2)

        def divide(t, carry, v=v, at=at):
            from_t = t if v < 2 else tiles - 1 - t
            for h in range(TILE // 128):
                cut = slice(h * 128, (h + 1) * 128)
                slices = {
                    f: c[from_t, f * 16 : (f + 1) * 16, cut].astype(F32)
                    for f in range(size)
                }
                sums = taps_sum(slices, zs, lambda z, i, j: num_ref[v * 16 + i * 3 + j : v * 16 + i * 3 + j + 1, :])
                for n, z in enumerate(zs):
                    recip_ref[at, t, n * 16 : (n + 1) * 16, cut] = (
                        1.0 / (along_y(sums[z]) + num_ref[v * 16 + 9 : v * 16 + 10, :])
                    ).astype(BF)
            return carry

        lax.fori_loop(0, tiles, divide, 0, unroll=True)


def main_kernel(frame, tiles, sides, at, table_ref, *refs):
    count = len(sides)
    index_refs, refs = refs[: count + 1], refs[count + 1 :]
    num_ref, est_ref, refs = refs[0], refs[1], refs[2:]
    own_refs, refs = refs[:4], refs[4:]
    far_refs, refs = refs[: 2 * count], refs[2 * count :]
    near_refs, beyond_refs = refs[:2], refs[2:4]
    recip_refs = refs[4:6]
    blocks_ref, frame_ref, out_ref = refs[6:9]
    m1a, m1b, u2, m2a, m2b, c0, c1, c2, c3, kept, wt, listed, bleach = refs[9:]
    m1s, m2s = (m1a, m1b), (m2a, m2b)
    even = lax.axis_index("gy") % 2 == 0
    c = [c0, c1, c2, c3]
    view = lax.axis_index("view")
    upside = lax.axis_index("gz") if frame.mirrored else 0
    depth = frame.depth
    z3, z2, z1, z0 = (frame.need(r) for r in (3, 2, 1, 0))
    sent = frame.sent(3)

    listed[...] = jnp.zeros(listed.shape, F32)
    listed[0:4, : table_ref.shape[1]] = table_ref[...]
    for n, ref in enumerate(index_refs):
        bleach[n * 16 : (n + 1) * 16, :] = bleach_weights(
            ref[0, at : at + 8, :128].astype(F32), listed[...]
        )
    for f in z2:
        where, k = frame.source(f)
        n = 0 if where == "own" else 1 + sides.index(where)
        over = upside if where == "own" else 1 - upside
        raw = n * 16 + (k + over * (depth - 1 - 2 * k) if frame.mirrored else k)
        weights = [bleach[pl.ds(raw + v * depth, 1), :] for v in range(4)]
        total = (weights[0] + weights[1]) + (weights[2] + weights[3])
        for v in range(4):
            mine = bleach[pl.ds(raw + (view ^ v) * depth, 1), :]
            to = (v * frame.size + f) * 16
            wt[to : to + 16, :] = num_ref[v * 16 : (v + 1) * 16, :] * (mine / total)

    def weighted(v, z, n):
        at = (v * frame.size + z) * 16 + 8 - n
        return wt[at : at + 1, :]

    def measured(v, t, z, cut):
        where, k = frame.source(z)
        if where == "own":
            own = own_refs[v][t, k * 8 : (k + 1) * 8, cut]
        else:
            k = k - sent[where].start
            far = far_refs[(count if v else 0) + sides.index(where)]
            own = far[v - 1 if v else 0, t, k * 8 : (k + 1) * 8, cut]
        n = frame.place(z, 3)
        one_ref, two_ref = near_refs if n < depth else beyond_refs
        n = n if n < depth else n - depth
        return jnp.concatenate(
            [
                own.astype(F32),
                beside(
                    even,
                    one_ref[v, t, n, :, cut],
                    two_ref[v, t, n, :, cut],
                ),
            ],
            axis=0,
        )

    def mix(v, t, z, cut, recip_a, recip_b):
        a = (measured(v, t, z, cut) * recip_a).astype(BF).astype(F32)
        b = (measured(v + 2, t, z, cut) * recip_b).astype(BF).astype(F32)
        return (0.5 * (a + b)).astype(BF)

    for ref in (m1a, m1b, u2, m2a, m2b):
        zero_ends(ref)

    for v in range(2):

        def ratios(t, carry, v=v):
            for h in range(TILE // 128):
                cut = slice(h * 128, (h + 1) * 128)
                to, lanes = spots(t, h)
                for n, z in enumerate(z3):
                    at = slice(n * 16, (n + 1) * 16)
                    m1s[v][to, at, lanes] = mix(
                        v,
                        t,
                        z,
                        cut,
                        recip_refs[0][v, t, at, cut].astype(F32),
                        recip_refs[1][v, t, at, cut].astype(F32),
                    )
            return carry

        lax.fori_loop(0, tiles, ratios, 0, unroll=True)
        for w in (v, v + 2):
            conv(m1s[v], 0, tiles, m1a.shape[1], blocks_ref.at[backward_block(w)], c[w], 2)

    def numerator(slices_of, zs):
        totals = {z: [None, None, None] for z in zs}
        for v in range(4):
            slices = slices_of(v)
            sums = taps_sum(
                slices,
                zs,
                lambda z, i, j, v=v: weighted(v, z, i * 3 + j),
            )
            for z in zs:
                for j in range(3):
                    old = totals[z][j]
                    totals[z][j] = sums[z][j] if old is None else old + sums[z][j]
        return totals

    def update(t, carry):
        for h in range(TILE // 128):
            cut = slice(h * 128, (h + 1) * 128)

            def slices_of(v):
                from_t = t if v < 2 else tiles - 1 - t
                return {
                    z: c[v][from_t, n * 16 : (n + 1) * 16, cut].astype(F32)
                    for n, z in enumerate(z3)
                }

            to, lanes = spots(t, h)
            totals = numerator(slices_of, z2)
            for n, z in enumerate(z2):
                change = along_y(totals[z])
                before = frame_ref[to, z * 16 : (z + 1) * 16, lanes].astype(F32)
                u2[to, n * 16 : (n + 1) * 16, lanes] = (before * change).astype(BF)
                if z in z0:
                    k = z - frame.own
                    kept[t, k * 8 : (k + 1) * 8, cut] = change[:8]
        return carry

    lax.fori_loop(0, tiles, update, 0, unroll=True)

    rows1 = m2a.shape[1]
    n2 = u2.shape[1]
    for w in (0, 2, 1, 3):
        conv(u2, 0, tiles, n2, blocks_ref.at[forward_block(w)], c[w].at[:, :n2, :], 2)
    for v in range(2):

        def ratios2(t, carry, v=v):
            for h in range(TILE // 128):
                cut = slice(h * 128, (h + 1) * 128)
                recips = []
                for w in (v, v + 2):
                    from_t = t if w < 2 else tiles - 1 - t
                    slices = {
                        z: c[w][from_t, n * 16 : (n + 1) * 16, cut].astype(F32)
                        for n, z in enumerate(z2)
                    }
                    sums = taps_sum(
                        slices, z1, lambda z, i, j, w=w: num_ref[w * 16 + i * 3 + j : w * 16 + i * 3 + j + 1, :]
                    )
                    recips.append(
                        {z: 1.0 / (along_y(sums[z]) + num_ref[w * 16 + 9 : w * 16 + 10, :]) for z in z1}
                    )
                to, lanes = spots(t, h)
                for n, z in enumerate(z1):
                    m2s[v][to, n * 16 : (n + 1) * 16, lanes] = mix(
                        v, t, z, cut, recips[0][z], recips[1][z]
                    )
            return carry

        lax.fori_loop(0, tiles, ratios2, 0, unroll=True)
        mine = tiles // 4
        for w in (v, v + 2):
            first = view * mine if w < 2 else tiles - (view + 1) * mine
            conv(m2s[v], first, mine, rows1, blocks_ref.at[backward_block(w)], c[w].at[:, :rows1, :], 2)

    mine = tiles // 4
    for s in range(mine):
        for h in range(TILE // 128):
            cut = slice(h * 128, (h + 1) * 128)

            def slices_of(v):
                from_s = s if v < 2 else mine - 1 - s
                return {
                    z: c[v][from_s, n * 16 : (n + 1) * 16, cut].astype(F32)
                    for n, z in enumerate(z1)
                }

            totals = numerator(slices_of, z0)
            for z in z0:
                k = z - frame.own
                to = k + upside * (depth - 1 - 2 * k)
                lanes = slice(s * TILE + h * 128, s * TILE + (h + 1) * 128)
                first_change = kept[view * mine + s, k * 8 : (k + 1) * 8, cut]
                out_ref[to, :, lanes] = (
                    est_ref[to, :, lanes] * first_change * along_y(totals[z])[:8]
                )


def shards(
    pieces, piece_owner, piece_row, estimate, psf_x, stencil, background, bleach_table, bleach_index
):
    depth, height, chunk = estimate.shape
    width = pieces.shape[3]
    tiles = width // TILE
    slabs = lax.axis_size("gz")
    bands = lax.axis_size("gy")
    blocks = slabs * bands
    frame = Frame(slabs, depth)
    size = frame.size
    sides = tuple(frame.sent(1))
    vmem, smem = pltpu.VMEM, pltpu.SMEM
    params = pltpu.CompilerParams(vmem_limit_bytes=LIMIT)

    def stay(array):
        return pltpu.with_memory_space_constraint(array, pltpu.VMEM)

    given = [piece_row, estimate, psf_x, bleach_table, bleach_index]
    given += [pieces[0], stencil.transpose(1, 0, 2), piece_owner.transpose(0, 2, 1)]
    first_pieces, first_taps, first_owner = given[-3:]

    def is_given(x):
        return any(x is y for y in given)

    def call(kernel, shapes, ins, outs, *args, scratch=()):
        args = [
            (
                pltpu.with_memory_space_constraint(x, pltpu.HBM)
                if is_given(x)
                else stay(x)
                if space is vmem
                else x
            )
            for space, x in zip(ins, args)
        ]
        out = pl.pallas_call(
            kernel,
            out_shape=shapes,
            in_specs=whole(*ins),
            out_specs=whole(*outs) if isinstance(shapes, tuple) else whole(*outs)[0],
            scratch_shapes=list(scratch),
            compiler_params=params,
        )(*args)
        return out

    def resident(*dims, dtype=BF):
        return pltpu.VMEM(dims, dtype)

    mark = jax.ShapeDtypeStruct((8, 128), F32)

    free = pl.ANY
    area = depth * height

    pairs = blocks // 2
    half_cells = resident(pairs, depth, height, width)
    even, odd, payload = call(
        functools.partial(first_kernel, pairs, bands, frame.mirrored),
        (half_cells, half_cells, resident(area + 8, chunk)),
        (smem, smem, smem, smem, vmem, vmem, vmem, vmem),
        (vmem, vmem, vmem),
        first_owner,
        piece_row,
        background,
        bleach_index,
        first_pieces,
        first_taps,
        estimate,
        psf_x,
        scratch=[vmem((blocks * depth, height, width), F32), vmem((8, chunk), F32)],
    )
    other = swap(odd, "gy", bands, 1)
    near_payload = swap(payload, "view", 4, 1)
    *kept, pair, sums_done = call(
        functools.partial(sum_kernel, pairs),
        (resident(depth, height, width),) * pairs
        + (resident(2, area + 8, chunk), mark),
        [vmem] * 4,
        [vmem] * (pairs + 2),
        even,
        other,
        payload,
        near_payload,
    )
    heard = (pair, swap(pair, "view", 4, 2))
    moved = [swap(kept[k], ("gz", "gy"), blocks, 2 * k) for k in range(1, pairs)]

    def stack(arrays, slices, *tokens):
        rows = slice(slices.start * height, slices.stop * height)
        dims = (len(arrays),) + arrays[0].shape[:-2] + (len(slices) * height, arrays[0].shape[-1])
        return call(
            functools.partial(stack_kernel, rows, len(arrays)),
            (resident(*dims), mark),
            [vmem] * len(arrays) + [free] + [vmem] * (len(tokens) - 1),
            (vmem, vmem),
            *arrays,
            *tokens,
        )

    def edges(arrays, fars, token, slices, dims, unread=()):
        out = resident(4, *dims[:-2], slices, height // 2, dims[-1])
        return call(
            functools.partial(
                edges_kernel,
                height,
                depth if arrays else 0,
                len(sides),
                len(arrays) == 2,
                len(unread),
            ),
            (out, out, mark),
            [vmem] * (len(arrays) + len(fars) + len(unread)) + [free],
            (vmem, vmem, vmem),
            *arrays,
            *fars,
            *unread,
            token,
        )

    far_slices = frame.sent(3)
    plain, turned, *own_far, total_done = call(
        functools.partial(
            total_kernel,
            pairs,
            [slice(s.start * height, s.stop * height) for s in far_slices.values()],
        ),
        (resident(tiles, area, TILE), resident(tiles, area, TILE))
        + tuple(resident(1, tiles, len(s) * height, TILE) for s in far_slices.values())
        + (mark,),
        [vmem] * pairs + [free],
        [vmem] * (3 + len(sides)),
        kept[0],
        *moved,
        sums_done,
    )
    near = swap(plain, "view", 4, 1)
    opposite = swap(turned, "view", 4, 2)
    last = swap(opposite, "view", 4, 1)
    ready = dict(zip([(s.start, s.stop) for s in far_slices.values()], own_far))
    table, nums, token = call(
        functools.partial(band_kernel, area),
        (resident(6, 2 * TILE, TILE), resident(64, 128, dtype=F32), mark),
        [vmem] * 3,
        (vmem, vmem, vmem),
        *heard,
        near,
    )
    kept_table, kept_nums = table, nums

    def est_rows(slices):
        return call(
            est_rows_kernel,
            resident(4, area + 8, chunk),
            [vmem] * 2 + [free],
            (vmem,),
            *heard,
            total_done,
        )

    far_est = exchange_z(frame, est_rows, slabs, depth)
    far_est = [far_est[s] for s in sides]
    est_edges = edges(heard, far_est, total_done, size, payload.shape)
    one_est, two_est = core_side(est_edges, bands, True)
    far_own = exchange_z(frame, lambda s: ready[s.start, s.stop], slabs, 3)
    far_own = [far_own[s] for s in sides]
    n3, n2, n1 = (len(frame.need(r)) * 16 for r in (3, 2, 1))

    scratch = [vmem((tiles, size * 16, TILE), BF)]
    tokens = []

    def others(slices):
        rows, done = stack(
            (near, opposite, last), slices, total_done
        )
        tokens.append(done)
        return rows

    far_others = exchange_z(frame, others, slabs, 3)
    far_others = [far_others[s] for s in sides]
    own_edges = edges(
        (plain, near, opposite, last),
        (),
        tokens[-1],
        depth,
        plain.shape,
        (one_est, two_est),
    )
    near_halo = core_side(own_edges, bands, False)
    est_frame, recip_a, token = call(
        functools.partial(start_kernel, frame, tiles, sides, (0, 1)),
        (
            resident(tiles + 1, size * 16, TILE),
            resident(2, tiles, n3, TILE),
            mark,
        ),
        [vmem] * (6 + len(sides)) + [free],
        (vmem, vmem, vmem),
        kept_nums,
        kept_table,
        *heard,
        *far_est,
        one_est,
        two_est,
        own_edges[2],
        scratch=scratch,
    )
    far_edges = edges(
        (), far_own + far_others, token, len(frame.need(3)) - depth, plain.shape
    )
    far_halo = core_side(far_edges, bands, False)
    recip_b, token_b = call(
        functools.partial(forward_kernel, frame, tiles, (2, 3)),
        (resident(2, tiles, n3, TILE), mark),
        (vmem, vmem, vmem, free),
        (vmem, vmem),
        kept_nums,
        kept_table,
        est_frame,
        far_edges[2],
        scratch=scratch,
    )
    return call(
        functools.partial(main_kernel, frame, tiles, sides, area),
        jax.ShapeDtypeStruct(estimate.shape, F32),
        [vmem] * (16 + 3 * len(sides)),
        (vmem,),
        stay(bleach_table),
        pair,
        *far_est,
        kept_nums,
        stay(estimate),
        plain,
        near,
        opposite,
        last,
        *far_own,
        *far_others,
        *near_halo,
        *far_halo,
        recip_a,
        recip_b,
        kept_table,
        est_frame,
        scratch=[
            vmem((tiles + 1, n3, TILE), BF),
            vmem((tiles + 1, n3, TILE), BF),
            vmem((tiles + 1, n2, TILE), BF),
            vmem((tiles + 1, n1, TILE), BF),
            vmem((tiles + 1, n1, TILE), BF),
        ]
        + [vmem((tiles, n3, TILE), BF)] * 4
        + [vmem((tiles, area, TILE), F32), vmem((4 * size * 16, 128), F32)]
        + [vmem((8, 128), F32), vmem(((1 + len(sides)) * 16, 128), F32)],
    )


def solution(mesh):
    placed = (
        P("view", ("gz", "gy"), None, None),
        P("view", ("gz", "gy"), None),
        P("view", ("gz", "gy")),
        P("gz", "gy", "view"),
        P("view", None),
        P("view", None, None),
        P("view"),
        P(),
        P(None, "gz"),
    )
    return jax.shard_map(
        shards, mesh=mesh, in_specs=placed, out_specs=P("gz", "gy", "view"), check_vma=False
    )
```
